256 devices in a mesh: seq: 2 (over core), ctx: 64 (over x_lo, y, z), head: 2 (over x_hi).
Axes of the slice: x: 4 (x_hi: 2, x_lo: 2; x = x_hi * 2 + x_lo), y: 4, z: 8, core: 2. Of those that a mesh axis runs over, the one named last changes fastest.
Arguments:
- queries: bfloat16 [16384, 8, 128], P(('seq', 'ctx'), 'head'), parts along dimension 0, may hold values from -8 to 8
- key_rows: bfloat16 [16384, 128], P(('seq', 'ctx')), parts along dimension 0, may hold values from -8 to 8
- value_rows: bfloat16 [16384, 128], P(('seq', 'ctx')), parts along dimension 0, may hold values from -6 to 6
- out_grad: bfloat16 [16384, 8, 128], P(('seq', 'ctx'), 'head'), parts along dimension 0, may hold values from -6 to 6
- doc_lengths: int32 [16], P('seq'), parts along dimension 0, may hold values from 1 to 2048, 8192 in all
- balance: int32 [16384], P('seq'), parts along dimension 0, may hold values from 0 to 8191, as said below
Outputs:
- attended: bfloat16 [16384, 8, 128], P(('seq', 'ctx'), 'head'), parts along dimension 0
- query_grad: bfloat16 [16384, 8, 128], P(('seq', 'ctx'), 'head'), parts along dimension 0
- key_grad: bfloat16 [16384, 128], P(('seq', 'ctx')), parts along dimension 0
- value_grad: bfloat16 [16384, 128], P(('seq', 'ctx')), parts along dimension 0
The draws below stay inside these ranges and needn't reach their ends.
There are 2 independent parts, one for each index of `seq`. The reference program is written for one: setup_inputs(seed, part) draws one part's arguments, and reference() takes and returns one part's arrays. A program takes and returns all parts, laid end to end along the dimension named above; each array names one. Nothing has to cross between parts.
Inputs may be any that keep to these rules, and one draw needn't show every extreme that they name: `doc_lengths`: the lengths sum to 8192 and the longest is exactly 2048. `balance`: A permutation of the positions that moves aligned runs of 64 positions whole and in order.
All inputs are finite; a program needn't handle non-finite values.
Results may differ from the reference program's by a relative error of at most 0.034.
Values may be sent and summed in bfloat16 or wider, within the bound.
A program may use at most 64 MiB of HBM per device.

```python
import math
import jax
import jax.numpy as jnp
import numpy as np
from jax import lax

HEADS = 8
DH = 128
SEQ = 8192
HALF = 64
SPANS = 128
DOCS = 8
MOST_DOC = 2048


def draw_queries(key, part):
    values_now = jnp.clip(jax.random.normal(jax.random.fold_in(key, 11), (SEQ, HEADS, DH), jnp.float32), -6.0, 6.0)
    return values_now.astype(jnp.bfloat16)


def draw_key_rows(key, part):
    values_now = jnp.clip(jax.random.normal(jax.random.fold_in(key, 13), (SEQ, DH), jnp.float32), -6.0, 6.0)
    return values_now.astype(jnp.bfloat16)


def draw_balance(key, part):
    span_order = jax.random.permutation(jax.random.fold_in(key, 17), SPANS).astype(jnp.int32)
    offsets = jnp.arange(HALF, dtype=jnp.int32)
    return (span_order[:, None] * HALF + offsets[None, :]).reshape(-1).astype(jnp.int32)


def level_of(own_key, shape, shards, smallest, top_value):
    def one(axis_at, blocks):
        draws = jax.random.uniform(jax.random.fold_in(jax.random.fold_in(own_key, 6), axis_at), (blocks,), jnp.float32, smallest / len(shards), top_value / len(shards))
        return jnp.repeat(jnp.exp(draws), shape[axis_at] // blocks).reshape((-1,) + (1,) * (len(shape) - axis_at - 1))

    loudness = one(*shards[0])
    for cut in shards[1:]:
        loudness = loudness * one(*cut)
    return loudness


def length_profile(count, total, reach, lean):
    portions = [(1 << 20) // math.isqrt(rank ** lean) + 1 for rank in range(2, count + 1)]
    spare, holding = total - reach - (count - 1), [1] * (count - 1)
    while spare > 0:
        candidates = [i for i in range(count - 1) if holding[i] < reach]
        mass, left = sum([portions[i] for i in candidates]), spare
        for i in candidates:
            more = min(reach - holding[i], max(1, left * portions[i] // mass), spare)
            holding[i] = holding[i] + more
            spare = spare - more
    return np.array([reach] + holding)


def uneven(own_key, number_of, total, reach, lean):
    if number_of == 2:
        one = jax.random.randint(own_key, (), max(1, total - reach), min(reach, total - 1) + 1)
        return jnp.stack([one, total - one])
    sizes = jnp.asarray(length_profile(number_of, total, reach, lean), jnp.int32)
    couples = (number_of - 1) // 2
    donor, taker = sizes[1:1 + 2 * couples:2], sizes[2:2 + 2 * couples:2]
    slack = jnp.minimum(donor - 1, reach - taker)
    moved = jax.random.randint(jax.random.fold_in(own_key, 1), (couples,), 0, 1 << 20) % (slack + 1)
    sizes = sizes.at[1:1 + 2 * couples:2].set(donor - moved).at[2:2 + 2 * couples:2].set(taker + moved)
    return sizes[jax.random.permutation(jax.random.fold_in(own_key, 2), number_of)]


def gaussian(rng, shape, deviation, bound, split=(), kind=jnp.bfloat16):
    array = deviation * jax.random.normal(rng, shape, jnp.float32)
    if split:
        array = array * level_of(rng, shape, split, -0.22, 0.18)
    return jnp.clip(array, -bound, bound).astype(kind)


def setup_inputs(seed: int = 0, part: int = 0) -> dict:
    splits = jax.random.split(jax.random.key(seed), 7)
    part_splits = jax.random.split(jax.random.fold_in(splits[6], part), 7)
    queries = draw_queries(jax.random.fold_in(jax.random.fold_in(splits[6], part), 71), part)
    key_rows = draw_key_rows(jax.random.fold_in(jax.random.fold_in(splits[6], part), 71), part)
    value_rows = gaussian(part_splits[2], (SEQ, DH), 1.0, 6.0, ((0, 64),))
    out_grad = gaussian(part_splits[3], (SEQ, HEADS, DH), 1.0, 6.0, ((0, 64), (1, 2)))
    doc_lengths = uneven(part_splits[4], DOCS, SEQ, MOST_DOC, 2).astype(jnp.int32)
    balance = draw_balance(jax.random.fold_in(jax.random.fold_in(splits[6], part), 71), part)
    return {"queries": queries, "key_rows": key_rows, "value_rows": value_rows, "out_grad": out_grad, "doc_lengths": doc_lengths, "balance": balance}


NEGATIVE = -1e+30

def rounded(values):
    return lax.optimization_barrier(values.astype(jnp.bfloat16)).astype(jnp.float32)

def document_of(positions, doc_lengths):
    doc_ends = jnp.cumsum(doc_lengths).astype(jnp.int32)
    return lax.optimization_barrier(jnp.sum((positions[:, None] >= doc_ends[None, :]).astype(jnp.int32), axis=1)).astype(jnp.int32)

def reference(queries, key_rows, value_rows, out_grad, doc_lengths, balance):
    scaling = 1.0 / math.sqrt(DH)
    docs_all = document_of(balance, doc_lengths)
    block_len = min(512, SEQ)
    block_count = SEQ // block_len
    keys_f = key_rows.astype(jnp.float32)
    values_f = value_rows.astype(jnp.float32)
    query_blocks = queries.reshape(block_count, block_len, HEADS, DH)
    grad_blocks = out_grad.reshape(block_count, block_len, HEADS, DH)
    pos_blocks = balance.reshape(block_count, block_len)
    doc_blocks = docs_all.reshape(block_count, block_len)

    def step_block(state_now, inputs_now):
        key_acc, value_acc = state_now
        query_blk, grad_blk, query_pos, query_doc = inputs_now
        visible_pairs = (docs_all[None, :] == query_doc[:, None]) & (balance[None, :] <= query_pos[:, None])
        allowed = visible_pairs[:, None, :]
        query_f = query_blk.astype(jnp.float32)
        grad_f = grad_blk.astype(jnp.float32)
        scores = jnp.einsum('qhd,kd->qhk', query_f, keys_f) * scaling
        scores = jnp.where(allowed, scores, NEGATIVE)
        row_max = lax.optimization_barrier(jnp.max(scores, axis=2))
        raw_weights = jnp.where(allowed, jnp.exp(scores - row_max[:, :, None]), 0.0)
        weight_sum = lax.optimization_barrier(jnp.sum(raw_weights, axis=2))
        attended_blk = (jnp.einsum('qhk,kd->qhd', rounded(raw_weights), values_f) / weight_sum[:, :, None]).astype(jnp.bfloat16)
        log_total = row_max + jnp.log(weight_sum)
        weights = jnp.where(allowed, jnp.exp(scores - log_total[:, :, None]), 0.0)
        row_inner = lax.optimization_barrier(jnp.sum(grad_f * attended_blk.astype(jnp.float32), axis=2))
        grad_weights = jnp.einsum('qhd,kd->qhk', grad_f, values_f)
        grad_scores = rounded(weights * (grad_weights - row_inner[:, :, None]))
        query_grad_blk = (jnp.einsum('qhk,kd->qhd', grad_scores, keys_f) * scaling).astype(jnp.bfloat16)
        key_acc = key_acc + jnp.einsum('qhk,qhd->kd', grad_scores, query_f) * scaling
        value_acc = value_acc + jnp.einsum('qhk,qhd->kd', rounded(weights), grad_f)
        return ((key_acc, value_acc), (attended_blk, query_grad_blk))
    start_state = (jnp.zeros((SEQ, DH), jnp.float32), jnp.zeros((SEQ, DH), jnp.float32))
    final_state, outputs = lax.scan(step_block, start_state, (query_blocks, grad_blocks, pos_blocks, doc_blocks))
    attended = outputs[0].reshape(SEQ, HEADS, DH)
    query_grad = outputs[1].reshape(SEQ, HEADS, DH)
    return (attended, query_grad, final_state[0].astype(jnp.bfloat16), final_state[1].astype(jnp.bfloat16))
```

```python
import math

import jax
import jax.numpy as jnp
from jax import lax
from jax.experimental import pallas as pl
from jax.experimental.pallas import tpu as pltpu
from jax.sharding import PartitionSpec as P

NX, NY, NZ = 4, 4, 8
XLO = 2
RUN = 64
DH = 128
HEADS_HERE = 4
ROWS = RUN * HEADS_HERE
BLK = 2 * RUN
KRUNS = XLO * NZ * 2
QRUNS = NY * 2
TILE = 4
SPANS = 128
DOCS = 8
NEGATIVE = -1e30
FLOOR = -1e29
FAR = 1 << 20
SCALING = 1.0 / math.sqrt(DH)
LOG2E = 1.0 / math.log(2.0)
MESH = pl.DeviceIdType.MESH
F32 = jnp.float32
BF16 = jnp.bfloat16


def here():
    c = lax.axis_index("ctx")
    h = lax.axis_index("head")
    return h, c // (NY * NZ), (c // NZ) % NY, c % NZ


def device(x, y, z):
    return {"ctx": ((x % XLO) * NY + y) * NZ + z, "head": x // XLO}


def meet(targets):
    barrier = pltpu.get_barrier_semaphore()
    for target in targets:
        pl.semaphore_signal(barrier, inc=1, device_id=target, device_id_type=MESH)
    pl.semaphore_wait(barrier, len(targets))


def remote(src, dst, send, recv, target):
    return pltpu.make_async_remote_copy(
        src_ref=src, dst_ref=dst, send_sem=send, recv_sem=recv, device_id=target, device_id_type=MESH
    )


def gather_kernel(q_ref, g_ref, k_ref, v_ref, qg, kg, lsem, ysend, yrecv, zsend, zrecv, xsend, xrecv):
    h, xl, y, z = here()
    x = h * XLO + xl
    first = xl * NZ
    y_up, y_dn = device(x, (y + 1) % NY, z), device(x, (y + NY - 1) % NY, z)
    z_up, z_dn = device(x, y, (z + 1) % NZ), device(x, y, (z + NZ - 1) % NZ)
    x_up, x_dn = device((x + 1) % NX, y, z), device((x + NX - 1) % NX, y, z)
    meet([y_up, y_dn, z_up, z_dn, x_up, x_dn])
    kv = (k_ref, v_ref)
    started = []

    def go(copy):
        copy.start()
        started.append(copy)
        return copy

    def z_send(way, step, part):
        block = (z - (step - 1) + NZ) % NZ if way == 0 else (z + step - 1) % NZ
        dst = kg.at[first + block, part]
        src = kv[part] if step == 1 else dst
        return go(remote(src, dst, zsend.at[way, step - 1, part], zrecv.at[way, step - 1, part], z_up if way == 0 else z_dn))

    def x_send(slot, block, src):
        dst = kg.at[first + block, h]
        for side, target in ((0, x_up), (1, x_dn)):
            sent_x.append(go(remote(src, dst, xsend.at[side, slot], xrecv.at[side, slot], target)))

    sent_x = []
    sent_z = {}
    for part in (0, 1):
        for way in (0, 1):
            sent_z[way, 1, part] = z_send(way, 1, part)
    locals_kv = []
    for part in (0, 1):
        copy = pltpu.make_async_copy(kv[part], kg.at[first + z, part], lsem.at[part])
        copy.start()
        locals_kv.append(copy)
    y_q_up = go(remote(q_ref, qg.at[y, 0], ysend.at[0], yrecv.at[0], y_up))
    y_g_dn = go(remote(g_ref, qg.at[y, 1], ysend.at[2], yrecv.at[2], y_dn))
    y_g_up = go(remote(g_ref, qg.at[y, 1], ysend.at[1], yrecv.at[1], y_up))
    y_q_dn = go(remote(q_ref, qg.at[y, 0], ysend.at[3], yrecv.at[3], y_dn))
    locals_q = []
    for part, ref in ((0, q_ref), (1, g_ref)):
        copy = pltpu.make_async_copy(ref, qg.at[y, part], lsem.at[2 + part])
        copy.start()
        locals_q.append(copy)
    for copy in locals_kv:
        copy.wait()
    x_send(0, z, kg.at[first + z, h])
    for step in (1, 2, 3):
        for part in (0, 1):
            for way in (0, 1):
                sent_z[way, step, part].wait_recv()
                if step < 3 or part == way:
                    sent_z[way, step + 1, part] = z_send(way, step + 1, part)
        for way in (0, 1):
            block = (z - step + NZ) % NZ if way == 0 else (z + step) % NZ
            x_send(2 * step - 1 + way, block, kg.at[first + block, h])
        if step == 2:
            y_q_up.wait_recv()
            q_on = qg.at[(y + NY - 1) % NY, 0]
            y_fwd_up = go(remote(q_on, q_on, ysend.at[4], yrecv.at[4], y_up))
            y_g_dn.wait_recv()
            g_on = qg.at[(y + 1) % NY, 1]
            y_fwd_dn = go(remote(g_on, g_on, ysend.at[5], yrecv.at[5], y_dn))
    sent_z[0, 4, 0].wait_recv()
    sent_z[1, 4, 1].wait_recv()
    block = (z + NZ // 2) % NZ
    x_send(7, block, kg.at[first + block, h])
    for copy in (y_g_up, y_q_dn, y_fwd_up, y_fwd_dn):
        copy.wait_recv()
    for copy in sent_x:
        copy.wait_recv()
    for copy in started:
        copy.wait_send()
    for copy in locals_q:
        copy.wait()


def gather(q, g, k, v):
    any_spec = pl.BlockSpec(memory_space=pl.ANY)
    dma = pltpu.SemaphoreType.DMA
    return pl.pallas_call(
        gather_kernel,
        out_shape=(
            jax.ShapeDtypeStruct((NY, 2, 2 * ROWS, DH), BF16),
            jax.ShapeDtypeStruct((XLO * NZ, 2, BLK, DH), BF16),
        ),
        in_specs=[any_spec] * 4,
        out_specs=(any_spec, any_spec),
        scratch_shapes=[dma((4,)), dma((6,)), dma((6,)), dma((2, 4, 2)), dma((2, 4, 2)), dma((2, 8)), dma((2, 8))],
        compiler_params=pltpu.CompilerParams(collective_id=0, has_side_effects=True),
        name="gather_rows",
    )(q, g, k, v)


def order_keys(spans, y, table, order, place, counts):
    def clear(p, _):
        table[p] = -1
        return 0

    lax.fori_loop(0, SPANS, clear, 0, unroll=8)
    for i in range(KRUNS):
        block, half = i // 2, i % 2
        table[spans[(((block // NZ) * NY + y) * NZ + block % NZ) * 2 + half]] = i

    def walk(p, n):
        counts[p] = n
        order[n] = table[p]
        place[n] = p * RUN
        return n + jnp.where(table[p] >= 0, 1, 0)

    lax.fori_loop(0, SPANS, walk, 0, unroll=8)
    counts[SPANS] = KRUNS
    for i in range(TILE):
        place[KRUNS + i] = FAR


def sort_keys(kg, order, ks, vs):
    def move(i, _):
        run = order[i]
        dst = pl.ds(pl.multiple_of(i * RUN, RUN), RUN)
        src = pl.ds(pl.multiple_of((run % 2) * RUN, RUN), RUN)
        ks[dst, :] = kg[run // 2, 0, src, :]
        vs[dst, :] = kg[run // 2, 1, src, :]
        return 0

    lax.fori_loop(0, KRUNS, move, 0)
    tail = pl.ds(KRUNS * RUN, TILE * RUN)
    ks[tail, :] = jnp.zeros((TILE * RUN, DH), BF16)
    vs[tail, :] = jnp.zeros((TILE * RUN, DH), BF16)


def query_rows(q_run, spans, lengths, counts, xl, z):
    span = spans[((xl * NY + q_run // 2) * NZ + z) * 2 + q_run % 2]
    low = span * RUN
    pos = low + lax.broadcasted_iota(jnp.int32, (1, ROWS), 1) // HEADS_HERE
    start = jnp.zeros((1, ROWS), jnp.int32)
    first = 0
    end = 0
    for d in range(DOCS):
        end = end + lengths[d]
        first = jnp.where(end <= low, end, first)
        start = jnp.where(pos >= end, end, start)
    low_run = counts[first // RUN]
    high_run = counts[span + 1]
    return pos, start, low_run, (high_run - low_run + TILE - 1) // TILE


def masked_scores(ks, q, row, run, place, pos, start):
    scores = lax.dot_general(ks[pl.ds(row, TILE * RUN), :], q, (((1,), (1,)), ((), ())), preferred_element_type=F32)
    offset = lax.broadcasted_iota(jnp.int32, (RUN, ROWS), 0)
    parts = []
    for u in range(TILE):
        base = place[run + u]
        seen = (offset <= pos - base) & (offset >= start - base)
        parts.append(jnp.where(seen, scores[u * RUN : (u + 1) * RUN] * (SCALING * LOG2E), NEGATIVE))
    return jnp.concatenate(parts, axis=0)


def forward_kernel(spans, lengths, qg, kg, stats, out, table, order, place, counts, ks, vs, held):
    h, xl, y, z = here()
    order_keys(spans, y, table, order, place, counts)
    sort_keys(kg, order, ks, vs)

    def one_run(q_run, _):
        pos, start, low_run, tiles = query_rows(q_run, spans, lengths, counts, xl, z)
        rows = pl.ds(pl.multiple_of((q_run % 2) * ROWS, ROWS), ROWS)
        q = qg[q_run // 2, 0, rows, :]
        g = qg[q_run // 2, 1, rows, :]

        def score(t, top):
            run = low_run + t * TILE
            row = pl.multiple_of(run * RUN, RUN)
            s = masked_scores(ks, q, row, run, place, pos, start)
            held[t] = s
            return jnp.maximum(top, jnp.max(s, axis=0, keepdims=True))

        top = lax.fori_loop(0, tiles, score, jnp.full((1, ROWS), FLOOR, F32))

        def weigh(t, state):
            total, inner, acc = state
            row = pl.multiple_of((low_run + t * TILE) * RUN, RUN)
            v = vs[pl.ds(row, TILE * RUN), :]
            raw = jnp.exp2(held[t] - top)
            gw = lax.dot_general(v, g, (((1,), (1,)), ((), ())), preferred_element_type=F32)
            total = total + jnp.sum(raw, axis=0, keepdims=True)
            inner = inner + jnp.sum(raw * gw, axis=0, keepdims=True)
            acc = acc + lax.dot_general(v, raw.astype(BF16), (((0,), (0,)), ((), ())), preferred_element_type=F32)
            return total, inner, acc

        zero = jnp.zeros((1, ROWS), F32)
        total, inner, acc = lax.fori_loop(0, tiles, weigh, (zero, zero, jnp.zeros((DH, ROWS), F32)))
        stats[q_run] = jnp.concatenate([top, total, inner, jnp.zeros((5, ROWS), F32)], axis=0)
        out[q_run] = acc
        return 0

    lax.fori_loop(0, QRUNS, one_run, 0)


SMEM_SCRATCH = [
    pltpu.SMEM((SPANS,), jnp.int32),
    pltpu.SMEM((KRUNS + TILE,), jnp.int32),
    pltpu.SMEM((KRUNS + TILE,), jnp.int32),
    pltpu.SMEM((SPANS + 1,), jnp.int32),
]
SORTED = (KRUNS + TILE) * RUN


def forward(spans, lengths, qg, kg):
    smem = pl.BlockSpec(memory_space=pltpu.SMEM)
    vmem = pl.BlockSpec(memory_space=pltpu.VMEM)
    return pl.pallas_call(
        forward_kernel,
        out_shape=(
            jax.ShapeDtypeStruct((QRUNS, 8, ROWS), F32),
            jax.ShapeDtypeStruct((QRUNS, DH, ROWS), F32),
        ),
        in_specs=[smem, smem, vmem, vmem],
        out_specs=(vmem, vmem),
        scratch_shapes=SMEM_SCRATCH
        + [
            pltpu.VMEM((SORTED, DH), BF16),
            pltpu.VMEM((SORTED, DH), BF16),
            pltpu.VMEM((KRUNS // TILE, TILE * RUN, ROWS), F32),
        ],
        compiler_params=pltpu.CompilerParams(vmem_limit_bytes=40 << 20),
        name="forward_stats",
    )(spans, lengths, qg, kg)


def exchange_kernel(mine, out, lsem, send, recv):
    h, xl, y, z = here()
    x = h * XLO + xl
    targets = [device(x, (y + d) % NY, z) for d in range(1, NY)]
    meet(targets)
    copies = []
    for d, target in enumerate(targets):
        copy = remote(mine, out.at[y], send.at[d], recv.at[d], target)
        copy.start()
        copies.append(copy)
    own = pltpu.make_async_copy(mine, out.at[y], lsem)
    own.start()
    own.wait()
    for copy in copies:
        copy.wait()


def exchange(stats):
    vmem = pl.BlockSpec(memory_space=pltpu.VMEM)
    dma = pltpu.SemaphoreType.DMA
    return pl.pallas_call(
        exchange_kernel,
        out_shape=jax.ShapeDtypeStruct((NY,) + stats.shape, F32),
        in_specs=[vmem],
        out_specs=vmem,
        scratch_shapes=[dma, dma((NY - 1,)), dma((NY - 1,))],
        compiler_params=pltpu.CompilerParams(collective_id=1, has_side_effects=True),
        name="exchange_stats",
    )(stats)


def backward_kernel(
    spans, lengths, qg, kg, stats, acc_out, rows_out, keys_out, table, order, place, counts, ks, vs, key_acc, value_acc
):
    h, xl, y, z = here()
    order_keys(spans, y, table, order, place, counts)
    sort_keys(kg, order, ks, vs)
    key_acc[...] = jnp.zeros_like(key_acc)
    value_acc[...] = jnp.zeros_like(value_acc)

    def one_run(q_run, _):
        pos, start, low_run, tiles = query_rows(q_run, spans, lengths, counts, xl, z)
        rows = pl.ds(pl.multiple_of((q_run % 2) * ROWS, ROWS), ROWS)
        q = qg[q_run // 2, 0, rows, :]
        g = qg[q_run // 2, 1, rows, :]
        each = [stats[i, q_run] for i in range(NY)]
        tops = [e[0:1] for e in each]
        top = jnp.maximum(jnp.maximum(tops[0], tops[1]), jnp.maximum(tops[2], tops[3]))
        shares = [jnp.exp2(t - top) for t in tops]
        total = sum(e[1:2] * s for e, s in zip(each, shares))
        inner = sum(e[2:3] * s for e, s in zip(each, shares)) / total
        log_total = top + jnp.log(total) * LOG2E
        own_top = stats[y, q_run][0:1]

        def tile(t, grad):
            run = low_run + t * TILE
            row = pl.multiple_of(run * RUN, RUN)
            here_rows = pl.ds(row, TILE * RUN)
            s = masked_scores(ks, q, row, run, place, pos, start)
            weights = jnp.exp2(s - log_total)
            gw = lax.dot_general(vs[here_rows, :], g, (((1,), (1,)), ((), ())), preferred_element_type=F32)
            gs = (weights * (gw - inner)).astype(BF16)
            value_acc[here_rows, :] += jnp.dot(weights.astype(BF16), g, preferred_element_type=F32)
            key_acc[here_rows, :] += jnp.dot(gs, q, preferred_element_type=F32)
            return grad + lax.dot_general(ks[here_rows, :], gs, (((0,), (0,)), ((), ())), preferred_element_type=F32)

        grad = lax.fori_loop(0, tiles, tile, jnp.zeros((DH, ROWS), F32))
        attended = acc_out[q_run] * jnp.exp2(own_top - log_total)
        rows_out[q_run // 2, 0, rows, :] = attended.T.astype(BF16)
        rows_out[q_run // 2, 1, rows, :] = (grad * SCALING).T.astype(BF16)
        return 0

    lax.fori_loop(0, QRUNS, one_run, 0)

    def put(i, _):
        run = order[i]
        src = pl.ds(pl.multiple_of(i * RUN, RUN), RUN)
        dst = pl.ds(pl.multiple_of((run % 2) * RUN, RUN), RUN)
        keys_out[run // 2, 0, dst, :] = (key_acc[src, :] * SCALING).astype(BF16)
        keys_out[run // 2, 1, dst, :] = value_acc[src, :].astype(BF16)
        return 0

    lax.fori_loop(0, KRUNS, put, 0)


def backward(spans, lengths, qg, kg, stats, acc):
    smem = pl.BlockSpec(memory_space=pltpu.SMEM)
    vmem = pl.BlockSpec(memory_space=pltpu.VMEM)
    return pl.pallas_call(
        backward_kernel,
        out_shape=(
            jax.ShapeDtypeStruct((NY, 2, 2 * ROWS, DH), BF16),
            jax.ShapeDtypeStruct((XLO * NZ, 2, BLK, DH), BF16),
        ),
        in_specs=[smem, smem, vmem, vmem, vmem, vmem],
        out_specs=(vmem, vmem),
        scratch_shapes=SMEM_SCRATCH
        + [
            pltpu.VMEM((SORTED, DH), BF16),
            pltpu.VMEM((SORTED, DH), BF16),
            pltpu.VMEM((SORTED, DH), F32),
            pltpu.VMEM((SORTED, DH), F32),
        ],
        compiler_params=pltpu.CompilerParams(vmem_limit_bytes=40 << 20),
        name="backward_terms",
    )(spans, lengths, qg, kg, stats, acc)


def reduce_kernel(
    rows, keys, att, qgrad, kgrad, vgrad,
    ybuf, ysum, xbuf, xsum, zbuf, zown, zsum, last, ysend, yrecv, xsend, xrecv, zsend, zrecv, hsend, hrecv,
):
    h, xl, y, z = here()
    x = h * XLO + xl
    half = NZ // 2
    y_up, y_dn = device(x, (y + 1) % NY, z), device(x, (y + NY - 1) % NY, z)
    x_up, x_dn, x_far = (device((x + d) % NX, y, z) for d in (1, NX - 1, 2))
    z_all = [device(x, y, (z + d) % NZ) for d in range(1, NZ)]
    meet([y_up, y_dn, x_up, x_dn, x_far] + z_all)
    started = []

    def go(copy):
        copy.start()
        started.append(copy)
        return copy

    def piece(ring):
        return (ring % XLO) * NZ, ring // XLO

    up, dn, far = (x + 1) % NX, (x + NX - 1) % NX, (x + 2) % NX
    far_first, far_part = piece(far)
    up_first, up_part = piece(up)
    dn_first, dn_part = piece(dn)
    my_first, my_part = piece(x)
    lo, hi = pl.ds(0, half), pl.ds(half, half)
    x_a = go(remote(keys.at[pl.ds(far_first, half), far_part], xbuf.at[0], xsend.at[0], xrecv.at[0], x_up))
    x_b = go(remote(keys.at[pl.ds(far_first + half, half), far_part], xbuf.at[1], xsend.at[1], xrecv.at[1], x_dn))
    y_far = (y + 2) % NY
    y_a = go(remote(rows.at[y_far, 0], ybuf.at[0], ysend.at[0], yrecv.at[0], y_up))
    y_b = go(remote(rows.at[y_far, 1], ybuf.at[1], ysend.at[1], yrecv.at[1], y_dn))
    x_c = go(remote(keys.at[pl.ds(up_first + half, half), up_part], xbuf.at[2], xsend.at[2], xrecv.at[2], x_up))
    x_d = go(remote(keys.at[pl.ds(dn_first, half), dn_part], xbuf.at[3], xsend.at[3], xrecv.at[3], x_dn))
    y_c = go(remote(rows.at[(y + 1) % NY, 1], ybuf.at[2], ysend.at[2], yrecv.at[2], y_up))
    y_d = go(remote(rows.at[(y + NY - 1) % NY, 0], ybuf.at[3], ysend.at[3], yrecv.at[3], y_dn))
    x_a.wait_recv()
    xsum[0] = (xbuf[0].astype(F32) + keys[pl.ds(up_first, half), up_part].astype(F32)).astype(BF16)
    x_e = go(remote(xsum.at[0], xbuf.at[4], xsend.at[4], xrecv.at[4], x_up))
    x_b.wait_recv()
    xsum[1] = (xbuf[1].astype(F32) + keys[pl.ds(dn_first + half, half), dn_part].astype(F32)).astype(BF16)
    x_f = go(remote(xsum.at[1], xbuf.at[5], xsend.at[5], xrecv.at[5], x_dn))
    y_a.wait_recv()
    ysum[0] = (ybuf[0].astype(F32) + rows[(y + 1) % NY, 0].astype(F32)).astype(BF16)
    y_e = go(remote(ysum.at[0], ybuf.at[4], ysend.at[4], yrecv.at[4], y_up))
    y_b.wait_recv()
    ysum[1] = (ybuf[1].astype(F32) + rows[(y + NY - 1) % NY, 1].astype(F32)).astype(BF16)
    y_f = go(remote(ysum.at[1], ybuf.at[5], ysend.at[5], yrecv.at[5], y_dn))
    x_d.wait_recv()
    x_e.wait_recv()
    zown[lo] = keys[pl.ds(my_first, half), my_part].astype(F32) + xbuf[3].astype(F32) + xbuf[4].astype(F32)
    x_c.wait_recv()
    x_f.wait_recv()
    zown[hi] = keys[pl.ds(my_first + half, half), my_part].astype(F32) + xbuf[2].astype(F32) + xbuf[5].astype(F32)
    zsum[...] = zown[...].astype(BF16)
    z_copies = []
    for d in (4, 3, 5, 2, 6, 1, 7):
        block = (z + d) % NZ
        z_copies.append(
            go(remote(zsum.at[block], zbuf.at[d - 1], zsend.at[d - 1], zrecv.at[d - 1], z_all[d - 1]))
        )
    y_d.wait_recv()
    y_e.wait_recv()
    att[...] = (rows[y, 0].astype(F32) + ybuf[3].astype(F32) + ybuf[4].astype(F32)).astype(BF16)
    y_c.wait_recv()
    y_f.wait_recv()
    qgrad[...] = (rows[y, 1].astype(F32) + ybuf[2].astype(F32) + ybuf[5].astype(F32)).astype(BF16)
    total = zown[z]
    for copy in z_copies:
        copy.wait_recv()
    for d in range(NZ - 1):
        total = total + zbuf[d].astype(F32)
    last[0] = total.astype(BF16)
    final = go(remote(last.at[0], last.at[1], hsend, hrecv, x_far))
    final.wait_recv()
    mine, other = last[0], last[1]
    kgrad[...] = jnp.where(h == 0, mine, other)
    vgrad[...] = jnp.where(h == 0, other, mine)
    for copy in started:
        copy.wait_send()


def reduce(rows, keys):
    vmem = pl.BlockSpec(memory_space=pltpu.VMEM)
    dma = pltpu.SemaphoreType.DMA
    half = NZ // 2
    return pl.pallas_call(
        reduce_kernel,
        out_shape=(
            jax.ShapeDtypeStruct((2 * ROWS, DH), BF16),
            jax.ShapeDtypeStruct((2 * ROWS, DH), BF16),
            jax.ShapeDtypeStruct((BLK, DH), BF16),
            jax.ShapeDtypeStruct((BLK, DH), BF16),
        ),
        in_specs=[vmem, vmem],
        out_specs=(vmem,) * 4,
        scratch_shapes=[
            pltpu.VMEM((6, 2 * ROWS, DH), BF16),
            pltpu.VMEM((2, 2 * ROWS, DH), BF16),
            pltpu.VMEM((6, half, BLK, DH), BF16),
            pltpu.VMEM((2, half, BLK, DH), BF16),
            pltpu.VMEM((NZ - 1, BLK, DH), BF16),
            pltpu.VMEM((NZ, BLK, DH), F32),
            pltpu.VMEM((NZ, BLK, DH), BF16),
            pltpu.VMEM((2, BLK, DH), BF16),
            dma((6,)), dma((6,)), dma((6,)), dma((6,)), dma((NZ - 1,)), dma((NZ - 1,)), dma, dma,
        ],
        compiler_params=pltpu.CompilerParams(collective_id=2, has_side_effects=True, vmem_limit_bytes=40 << 20),
        name="reduce_terms",
    )(rows, keys)


def body(queries, key_rows, value_rows, out_grad, doc_lengths, balance):
    flat = (2 * ROWS, DH)
    spans = balance.reshape(SPANS, RUN)[:, 0] // RUN
    qg, kg = gather(queries.reshape(flat), out_grad.reshape(flat), key_rows, value_rows)
    stats, acc = forward(spans, doc_lengths, qg, kg)
    stats = exchange(stats)
    rows, keys = backward(spans, doc_lengths, qg, kg, stats, acc)
    attended, query_grad, key_grad, value_grad = reduce(rows, keys)
    return attended.reshape(queries.shape), query_grad.reshape(queries.shape), key_grad, value_grad


def solution(mesh):
    return jax.shard_map(
        body,
        mesh=mesh,
        in_specs=(
            P(("seq", "ctx"), "head", None),
            P(("seq", "ctx"), None),
            P(("seq", "ctx"), None),
            P(("seq", "ctx"), "head", None),
            P("seq"),
            P("seq"),
        ),
        out_specs=(
            P(("seq", "ctx"), "head", None),
            P(("seq", "ctx"), "head", None),
            P(("seq", "ctx"), None),
            P(("seq", "ctx"), None),
        ),
        check_vma=False,
    )
```

```python
import math

import jax
import jax.numpy as jnp
from jax import lax
from jax.experimental import pallas as pl
from jax.experimental.pallas import tpu as pltpu
from jax.sharding import PartitionSpec as P

NX, NY, NZ = 4, 4, 8
XLO = 2
RUN = 64
DH = 128
HEADS_HERE = 4
ROWS = RUN * HEADS_HERE
BLK = 2 * RUN
KRUNS = XLO * NZ * 2
QRUNS = NY * 2
TILE = 4
SPANS = 128
QTAB = 40
DOCS = 8
NEGATIVE = -1e30
FLOOR = -1e29
FAR = 1 << 20
SCALING = 1.0 / math.sqrt(DH)
LOG2E = 1.0 / math.log(2.0)
MESH = pl.DeviceIdType.MESH
F32 = jnp.float32
BF16 = jnp.bfloat16


def here():
    c = lax.axis_index("ctx")
    h = lax.axis_index("head")
    return h, c // (NY * NZ), (c // NZ) % NY, c % NZ


def device(x, y, z):
    return {"ctx": ((x % XLO) * NY + y) * NZ + z, "head": x // XLO}


def meet(targets):
    barrier = pltpu.get_barrier_semaphore()
    for target in targets:
        pl.semaphore_signal(barrier, inc=1, device_id=target, device_id_type=MESH)
    pl.semaphore_wait(barrier, len(targets))


def remote(src, dst, send, recv, target):
    return pltpu.make_async_remote_copy(
        src_ref=src, dst_ref=dst, send_sem=send, recv_sem=recv, device_id=target, device_id_type=MESH
    )


def tables(bal, lengths, tab, row_tab, xl, y, z):
    lane = lax.broadcasted_iota(jnp.int32, (1, SPANS), 1)
    slabs = [bal[pl.ds(pl.multiple_of((i * NY + y) * NZ, NZ), NZ), :] for i in range(XLO)]
    held = [slab[:, half * RUN : half * RUN + 1] // RUN for half in (0, 1) for slab in slabs]
    held = jnp.concatenate(held, axis=0)
    index = lax.broadcasted_iota(jnp.int32, (KRUNS, 1), 0)
    match = held == lane
    has = jnp.sum(jnp.where(match, 1, 0), axis=0, keepdims=True)
    which = jnp.sum(jnp.where(match, index, 0), axis=0, keepdims=True)
    before = jnp.sum(jnp.where(held < lane, 1, 0), axis=0, keepdims=True)
    rank = jnp.where(has > 0, before, -1)
    pick = lax.broadcasted_iota(jnp.int32, (QTAB, 1), 0)
    hit = rank == pick
    place = jnp.sum(jnp.where(hit, lane * RUN, 0), axis=1, keepdims=True)
    order = jnp.sum(jnp.where(hit, which, 0), axis=1, keepdims=True)
    place = jnp.where(pick < KRUNS, place, FAR)
    tab[pl.ds(0, QTAB), :] = jnp.where(lane == 0, place, order)
    q_rows = [bal[pl.ds((xl * NY + i) * NZ + z, 1), :] for i in range(NY)]
    low = jnp.concatenate([r[:, half * RUN : half * RUN + 1] for r in q_rows for half in (0, 1)], axis=0)
    pos = low + lax.broadcasted_iota(jnp.int32, (QRUNS, ROWS), 1) // HEADS_HERE
    start = jnp.zeros((QRUNS, ROWS), jnp.int32)
    first = jnp.zeros((QRUNS, 1), jnp.int32)
    end = 0
    for d in range(DOCS):
        end = end + lengths[d]
        first = jnp.where(low >= end, end, first)
        start = jnp.where(pos >= end, end, start)
    row_tab[0] = pos
    row_tab[1] = start
    low_run = jnp.sum(jnp.where((lane < first // RUN) & (has > 0), 1, 0), axis=1, keepdims=True)
    high_run = jnp.sum(jnp.where((lane <= low // RUN) & (has > 0), 1, 0), axis=1, keepdims=True)
    tiles = (high_run - low_run + TILE - 1) // TILE
    tab[pl.ds(QTAB, QRUNS), :] = jnp.where(lane == 0, low_run, tiles)


def gather_kernel(
    q_ref, g_ref, k_ref, v_ref, bal_ref, len_ref, qg, kg, tab, row_tab, bal, lengths, lsem, ysend, yrecv, zsend, zrecv, xsend, xrecv
):
    h, xl, y, z = here()
    x = h * XLO + xl
    first = xl * NZ
    y_up, y_dn = device(x, (y + 1) % NY, z), device(x, (y + NY - 1) % NY, z)
    z_to = {d: device(x, y, (z + d + NZ) % NZ) for d in (1, 2, -1, -2)}
    x_up, x_dn = device((x + 1) % NX, y, z), device((x + NX - 1) % NX, y, z)
    meet([y_up, y_dn, x_up, x_dn] + list(z_to.values()))
    kv = (k_ref, v_ref)
    started = []

    def go(copy):
        copy.start()
        started.append(copy)
        return copy

    sent_z = {}

    def z_send(sign, hops, dist, part):
        block = (z - sign * (dist - hops) + NZ) % NZ
        dst = kg.at[first + block, part]
        src = kv[part] if dist == hops else dst
        way = 0 if sign > 0 else 1
        sems = zsend.at[way, dist - 1, part], zrecv.at[way, dist - 1, part]
        sent_z[sign, dist, part] = go(remote(src, dst, *sems, z_to[sign * hops]))

    sent_x = []

    def x_send(slot, block):
        dst = kg.at[first + block, h]
        for side, target in ((0, x_up), (1, x_dn)):
            sent_x.append(go(remote(dst, dst, xsend.at[side, slot], xrecv.at[side, slot], target)))

    def local(src, dst, slot):
        copy = pltpu.make_async_copy(src, dst, lsem.at[slot])
        copy.start()
        return copy

    own_tab = [local(bal_ref, bal, 4), local(len_ref, lengths, 5)]
    for part in (0, 1):
        for sign in (1, -1):
            z_send(sign, 2, 2, part)
    y_q_up = go(remote(q_ref, qg.at[y, 0], ysend.at[0], yrecv.at[0], y_up))
    y_g_dn = go(remote(g_ref, qg.at[y, 1], ysend.at[2], yrecv.at[2], y_dn))
    own_kv = [local(kv[part], kg.at[first + z, part], part) for part in (0, 1)]
    for part in (0, 1):
        for sign in (1, -1):
            z_send(sign, 1, 1, part)
    y_g_up = go(remote(g_ref, qg.at[y, 1], ysend.at[1], yrecv.at[1], y_up))
    y_q_dn = go(remote(q_ref, qg.at[y, 0], ysend.at[3], yrecv.at[3], y_dn))
    own_q = [local(ref, qg.at[y, part], 2 + part) for part, ref in ((0, q_ref), (1, g_ref))]
    for copy in own_kv:
        copy.wait()
    x_send(0, z)
    for copy in own_tab:
        copy.wait()
    tables(bal, lengths, tab, row_tab, xl, y, z)
    for part in (0, 1):
        for sign in (1, -1):
            sent_z[sign, 2, part].wait_recv()
            z_send(sign, 1, 3, part)
            if part == (0 if sign > 0 else 1):
                z_send(sign, 2, 4, part)
    x_send(1, (z - 2 + NZ) % NZ)
    x_send(2, (z + 2) % NZ)
    y_q_up.wait_recv()
    q_on = qg.at[(y + NY - 1) % NY, 0]
    y_fwd_up = go(remote(q_on, q_on, ysend.at[4], yrecv.at[4], y_up))
    y_g_dn.wait_recv()
    g_on = qg.at[(y + 1) % NY, 1]
    y_fwd_dn = go(remote(g_on, g_on, ysend.at[5], yrecv.at[5], y_dn))
    slot = 3
    for dist in (1, 3):
        for sign in (1, -1):
            for part in (0, 1):
                sent_z[sign, dist, part].wait_recv()
            x_send(slot, (z - sign * dist + NZ) % NZ)
            slot += 1
    sent_z[1, 4, 0].wait_recv()
    sent_z[-1, 4, 1].wait_recv()
    x_send(7, (z + NZ // 2) % NZ)
    for copy in (y_g_up, y_q_dn, y_fwd_up, y_fwd_dn):
        copy.wait_recv()
    for copy in sent_x:
        copy.wait_recv()
    for copy in started:
        copy.wait_send()
    for copy in own_q:
        copy.wait()


def gather(q, g, k, v, bal, lengths):
    hbm = pl.BlockSpec(memory_space=pltpu.HBM)
    vmem = pl.BlockSpec(memory_space=pltpu.VMEM)
    dma = pltpu.SemaphoreType.DMA
    return pl.pallas_call(
        gather_kernel,
        out_shape=(
            jax.ShapeDtypeStruct((NY, 2, 2 * ROWS, DH), BF16),
            jax.ShapeDtypeStruct((XLO * NZ, 2, BLK, DH), BF16),
            jax.ShapeDtypeStruct((QTAB + QRUNS, SPANS), jnp.int32),
            jax.ShapeDtypeStruct((2, QRUNS, ROWS), jnp.int32),
        ),
        in_specs=[hbm] * 6,
        out_specs=(vmem,) * 4,
        scratch_shapes=[
            pltpu.VMEM((SPANS // 2, BLK), jnp.int32),
            pltpu.SMEM((DOCS,), jnp.int32),
            dma((6,)), dma((6,)), dma((6,)), dma((2, 4, 2)), dma((2, 4, 2)), dma((2, 8)), dma((2, 8)),
        ],
        compiler_params=pltpu.CompilerParams(collective_id=0, has_side_effects=True, vmem_limit_bytes=8 << 20),
        name="gather_rows",
    )(*(pltpu.with_memory_space_constraint(a, pltpu.HBM) for a in (q, g, k, v, bal, lengths)))


def tile_runs(tab, low_run, t):
    runs = [low_run + t * TILE + u for u in range(TILE)]
    return [tab[r, 1] for r in runs], [tab[r, 0] for r in runs]


def run_rows(index):
    return index % (XLO * NZ), pl.ds(pl.multiple_of(index // (XLO * NZ) * RUN, RUN), RUN)


def tile_rows(kg, indices, part):
    pieces = []
    for index in indices:
        block, rows = run_rows(index)
        pieces.append(kg[block, part, rows, :])
    return jnp.concatenate(pieces, axis=0)


def masked_scores(k, q, places, pos, start):
    scores = lax.dot_general(k, q, (((1,), (1,)), ((), ())), preferred_element_type=F32)
    offset = lax.broadcasted_iota(jnp.int32, (RUN, ROWS), 0)
    parts = []
    for u, base in enumerate(places):
        seen = (offset <= pos - base) & (offset >= start - base)
        parts.append(jnp.where(seen, scores[u * RUN : (u + 1) * RUN] * (SCALING * LOG2E), NEGATIVE))
    return jnp.concatenate(parts, axis=0)


def forward_kernel(tab, row_tab, qg, kg, stats, out, held):
    def one_run(q_run, _):
        low_run, tiles = tab[QTAB + q_run, 0], tab[QTAB + q_run, 1]
        pos, start = row_tab[0, pl.ds(q_run, 1), :], row_tab[1, pl.ds(q_run, 1), :]
        rows = pl.ds(pl.multiple_of((q_run % 2) * ROWS, ROWS), ROWS)
        q = qg[q_run // 2, 0, rows, :]
        g = qg[q_run // 2, 1, rows, :]

        def score(t, top):
            indices, places = tile_runs(tab, low_run, t)
            s = masked_scores(tile_rows(kg, indices, 0), q, places, pos, start)
            held[t] = s
            return jnp.maximum(top, jnp.max(s, axis=0, keepdims=True))

        top = lax.fori_loop(0, tiles, score, jnp.full((1, ROWS), FLOOR, F32))

        def weigh(t, state):
            total, inner, acc = state
            indices, _ = tile_runs(tab, low_run, t)
            v = tile_rows(kg, indices, 1)
            raw = jnp.exp2(held[t] - top)
            gw = lax.dot_general(v, g, (((1,), (1,)), ((), ())), preferred_element_type=F32)
            total = total + jnp.sum(raw, axis=0, keepdims=True)
            inner = inner + jnp.sum(raw * gw, axis=0, keepdims=True)
            acc = acc + lax.dot_general(v, raw.astype(BF16), (((0,), (0,)), ((), ())), preferred_element_type=F32)
            return total, inner, acc

        zero = jnp.zeros((1, ROWS), F32)
        total, inner, acc = lax.fori_loop(0, tiles, weigh, (zero, zero, jnp.zeros((DH, ROWS), F32)))
        stats[q_run] = jnp.concatenate([top, total, inner, jnp.zeros((5, ROWS), F32)], axis=0)
        out[q_run] = acc
        return 0

    lax.fori_loop(0, QRUNS, one_run, 0)


def forward(tab, row_tab, qg, kg):
    smem = pl.BlockSpec(memory_space=pltpu.SMEM)
    vmem = pl.BlockSpec(memory_space=pltpu.VMEM)
    return pl.pallas_call(
        forward_kernel,
        out_shape=(
            jax.ShapeDtypeStruct((QRUNS, 8, ROWS), F32),
            jax.ShapeDtypeStruct((QRUNS, DH, ROWS), F32),
        ),
        in_specs=[smem, vmem, vmem, vmem],
        out_specs=(vmem, vmem),
        scratch_shapes=[pltpu.VMEM((KRUNS // TILE, TILE * RUN, ROWS), F32)],
        compiler_params=pltpu.CompilerParams(vmem_limit_bytes=16 << 20),
        name="forward_stats",
    )(tab, row_tab, qg, kg)


def exchange_kernel(mine, out, lsem, send, recv):
    h, xl, y, z = here()
    x = h * XLO + xl
    targets = [device(x, (y + d) % NY, z) for d in range(1, NY)]
    meet(targets)
    copies = []
    for d, target in enumerate(targets):
        copy = remote(mine, out.at[y], send.at[d], recv.at[d], target)
        copy.start()
        copies.append(copy)
    own = pltpu.make_async_copy(mine, out.at[y], lsem)
    own.start()
    own.wait()
    for copy in copies:
        copy.wait()


def exchange(stats):
    vmem = pl.BlockSpec(memory_space=pltpu.VMEM)
    dma = pltpu.SemaphoreType.DMA
    return pl.pallas_call(
        exchange_kernel,
        out_shape=jax.ShapeDtypeStruct((NY,) + stats.shape, F32),
        in_specs=[vmem],
        out_specs=vmem,
        scratch_shapes=[dma, dma((NY - 1,)), dma((NY - 1,))],
        compiler_params=pltpu.CompilerParams(collective_id=1, has_side_effects=True, vmem_limit_bytes=1 << 20),
        name="exchange_stats",
    )(stats)


def backward_kernel(tab, row_tab, qg, kg, stats, acc_out, own, rows_out, keys_out, key_acc, value_acc):
    key_acc[...] = jnp.zeros_like(key_acc)
    value_acc[...] = jnp.zeros_like(value_acc)

    def one_run(q_run, _):
        low_run, tiles = tab[QTAB + q_run, 0], tab[QTAB + q_run, 1]
        pos, start = row_tab[0, pl.ds(q_run, 1), :], row_tab[1, pl.ds(q_run, 1), :]
        rows = pl.ds(pl.multiple_of((q_run % 2) * ROWS, ROWS), ROWS)
        q = qg[q_run // 2, 0, rows, :]
        g = qg[q_run // 2, 1, rows, :]
        each = [stats[i, q_run] for i in range(NY)]
        tops = [e[0:1] for e in each]
        top = jnp.maximum(jnp.maximum(tops[0], tops[1]), jnp.maximum(tops[2], tops[3]))
        shares = [jnp.exp2(t - top) for t in tops]
        total = sum(e[1:2] * s for e, s in zip(each, shares))
        inner = sum(e[2:3] * s for e, s in zip(each, shares)) / total
        log_total = top + jnp.log(total) * LOG2E
        own_top = own[q_run][0:1]

        def tile(t, grad):
            indices, places = tile_runs(tab, low_run, t)
            k = tile_rows(kg, indices, 0)
            s = masked_scores(k, q, places, pos, start)
            weights = jnp.exp2(s - log_total)
            gw = lax.dot_general(
                tile_rows(kg, indices, 1), g, (((1,), (1,)), ((), ())), preferred_element_type=F32
            )
            gs = (weights * (gw - inner)).astype(BF16)
            value_part = jnp.dot(weights.astype(BF16), g, preferred_element_type=F32)
            key_part = jnp.dot(gs, q, preferred_element_type=F32)
            for u, index in enumerate(indices):
                block, to = run_rows(index)
                value_acc[block, to, :] += value_part[u * RUN : (u + 1) * RUN]
                key_acc[block, to, :] += key_part[u * RUN : (u + 1) * RUN]
            return grad + lax.dot_general(k, gs, (((0,), (0,)), ((), ())), preferred_element_type=F32)

        grad = lax.fori_loop(0, tiles, tile, jnp.zeros((DH, ROWS), F32))
        attended = acc_out[q_run] * jnp.exp2(own_top - log_total)
        rows_out[q_run // 2, 0, rows, :] = attended.T.astype(BF16)
        rows_out[q_run // 2, 1, rows, :] = (grad * SCALING).T.astype(BF16)
        return 0

    lax.fori_loop(0, QRUNS, one_run, 0)
    for block in range(XLO * NZ):
        keys_out[block, 0] = (key_acc[block] * SCALING).astype(BF16)
        keys_out[block, 1] = value_acc[block].astype(BF16)


def backward(tab, row_tab, qg, kg, stats, acc, own):
    smem = pl.BlockSpec(memory_space=pltpu.SMEM)
    vmem = pl.BlockSpec(memory_space=pltpu.VMEM)
    return pl.pallas_call(
        backward_kernel,
        out_shape=(
            jax.ShapeDtypeStruct((NY, 2, 2 * ROWS, DH), BF16),
            jax.ShapeDtypeStruct((XLO * NZ, 2, BLK, DH), BF16),
        ),
        in_specs=[smem] + [vmem] * 6,
        out_specs=(vmem, vmem),
        scratch_shapes=[pltpu.VMEM((XLO * NZ, BLK, DH), F32), pltpu.VMEM((XLO * NZ, BLK, DH), F32)],
        compiler_params=pltpu.CompilerParams(vmem_limit_bytes=16 << 20),
        name="backward_terms",
    )(tab, row_tab, qg, kg, stats, acc, own)


def reduce_kernel(
    rows, keys, att, qgrad, kgrad, vgrad,
    ybuf, ysum, xbuf, xsum, zbuf, zown, zsum, last, ysend, yrecv, xsend, xrecv, zsend, zrecv, hsend, hrecv,
):
    h, xl, y, z = here()
    x = h * XLO + xl
    half = NZ // 2
    y_up, y_dn = device(x, (y + 1) % NY, z), device(x, (y + NY - 1) % NY, z)
    x_up, x_dn, x_far = (device((x + d) % NX, y, z) for d in (1, NX - 1, 2))
    z_all = [device(x, y, (z + d) % NZ) for d in range(1, NZ)]
    meet([y_up, y_dn, x_up, x_dn, x_far] + z_all)
    started = []

    def go(copy):
        copy.start()
        started.append(copy)
        return copy

    def piece(ring):
        return (ring % XLO) * NZ, ring // XLO

    up, dn, far = (x + 1) % NX, (x + NX - 1) % NX, (x + 2) % NX
    far_first, far_part = piece(far)
    up_first, up_part = piece(up)
    dn_first, dn_part = piece(dn)
    my_first, my_part = piece(x)
    lo, hi = pl.ds(0, half), pl.ds(half, half)
    x_a = go(remote(keys.at[pl.ds(far_first, half), far_part], xbuf.at[0], xsend.at[0], xrecv.at[0], x_up))
    x_b = go(remote(keys.at[pl.ds(far_first + half, half), far_part], xbuf.at[1], xsend.at[1], xrecv.at[1], x_dn))
    y_far = (y + 2) % NY
    y_a = go(remote(rows.at[y_far, 0], ybuf.at[0], ysend.at[0], yrecv.at[0], y_up))
    y_b = go(remote(rows.at[y_far, 1], ybuf.at[1], ysend.at[1], yrecv.at[1], y_dn))
    x_c = go(remote(keys.at[pl.ds(up_first + half, half), up_part], xbuf.at[2], xsend.at[2], xrecv.at[2], x_up))
    x_d = go(remote(keys.at[pl.ds(dn_first, half), dn_part], xbuf.at[3], xsend.at[3], xrecv.at[3], x_dn))
    y_c = go(remote(rows.at[(y + 1) % NY, 1], ybuf.at[2], ysend.at[2], yrecv.at[2], y_up))
    y_d = go(remote(rows.at[(y + NY - 1) % NY, 0], ybuf.at[3], ysend.at[3], yrecv.at[3], y_dn))
    x_a.wait_recv()
    xsum[0] = (xbuf[0].astype(F32) + keys[pl.ds(up_first, half), up_part].astype(F32)).astype(BF16)
    x_e = go(remote(xsum.at[0], xbuf.at[4], xsend.at[4], xrecv.at[4], x_up))
    x_b.wait_recv()
    xsum[1] = (xbuf[1].astype(F32) + keys[pl.ds(dn_first + half, half), dn_part].astype(F32)).astype(BF16)
    x_f = go(remote(xsum.at[1], xbuf.at[5], xsend.at[5], xrecv.at[5], x_dn))
    y_a.wait_recv()
    ysum[0] = (ybuf[0].astype(F32) + rows[(y + 1) % NY, 0].astype(F32)).astype(BF16)
    y_e = go(remote(ysum.at[0], ybuf.at[4], ysend.at[4], yrecv.at[4], y_up))
    y_b.wait_recv()
    ysum[1] = (ybuf[1].astype(F32) + rows[(y + NY - 1) % NY, 1].astype(F32)).astype(BF16)
    y_f = go(remote(ysum.at[1], ybuf.at[5], ysend.at[5], yrecv.at[5], y_dn))
    x_d.wait_recv()
    x_e.wait_recv()
    zown[lo] = keys[pl.ds(my_first, half), my_part].astype(F32) + xbuf[3].astype(F32) + xbuf[4].astype(F32)
    x_c.wait_recv()
    x_f.wait_recv()
    zown[hi] = keys[pl.ds(my_first + half, half), my_part].astype(F32) + xbuf[2].astype(F32) + xbuf[5].astype(F32)
    zsum[...] = zown[...].astype(BF16)
    z_copies = []
    for d in (4, 3, 5, 2, 6, 1, 7):
        block = (z + d) % NZ
        z_copies.append(
            go(remote(zsum.at[block], zbuf.at[d - 1], zsend.at[d - 1], zrecv.at[d - 1], z_all[d - 1]))
        )
    y_d.wait_recv()
    y_e.wait_recv()
    att[...] = (rows[y, 0].astype(F32) + ybuf[3].astype(F32) + ybuf[4].astype(F32)).astype(BF16)
    y_c.wait_recv()
    y_f.wait_recv()
    qgrad[...] = (rows[y, 1].astype(F32) + ybuf[2].astype(F32) + ybuf[5].astype(F32)).astype(BF16)
    total = zown[z]
    for copy in z_copies:
        copy.wait_recv()
    for d in range(NZ - 1):
        total = total + zbuf[d].astype(F32)
    last[0] = total.astype(BF16)
    final = go(remote(last.at[0], last.at[1], hsend, hrecv, x_far))
    final.wait_recv()
    mine, other = last[0], last[1]
    kgrad[...] = jnp.where(h == 0, mine, other)
    vgrad[...] = jnp.where(h == 0, other, mine)
    for copy in started:
        copy.wait_send()


def reduce(rows, keys):
    vmem = pl.BlockSpec(memory_space=pltpu.VMEM)
    dma = pltpu.SemaphoreType.DMA
    half = NZ // 2
    return pl.pallas_call(
        reduce_kernel,
        out_shape=(
            jax.ShapeDtypeStruct((2 * ROWS, DH), BF16),
            jax.ShapeDtypeStruct((2 * ROWS, DH), BF16),
            jax.ShapeDtypeStruct((BLK, DH), BF16),
            jax.ShapeDtypeStruct((BLK, DH), BF16),
        ),
        in_specs=[vmem, vmem],
        out_specs=(vmem,) * 4,
        scratch_shapes=[
            pltpu.VMEM((6, 2 * ROWS, DH), BF16),
            pltpu.VMEM((2, 2 * ROWS, DH), BF16),
            pltpu.VMEM((6, half, BLK, DH), BF16),
            pltpu.VMEM((2, half, BLK, DH), BF16),
            pltpu.VMEM((NZ - 1, BLK, DH), BF16),
            pltpu.VMEM((NZ, BLK, DH), F32),
            pltpu.VMEM((NZ, BLK, DH), BF16),
            pltpu.VMEM((2, BLK, DH), BF16),
            dma((6,)), dma((6,)), dma((6,)), dma((6,)), dma((NZ - 1,)), dma((NZ - 1,)), dma, dma,
        ],
        compiler_params=pltpu.CompilerParams(collective_id=2, has_side_effects=True, vmem_limit_bytes=16 << 20),
        name="reduce_terms",
    )(rows, keys)


def store_kernel(*refs):
    count = len(refs) // 2
    copies = [pltpu.make_async_copy(refs[i], refs[count + i], refs[-1].at[i]) for i in range(count)]
    for copy in copies:
        copy.start()
    for copy in copies:
        copy.wait()


def store(*arrays):
    return pl.pallas_call(
        store_kernel,
        out_shape=tuple(jax.ShapeDtypeStruct(a.shape, a.dtype) for a in arrays),
        in_specs=[pl.BlockSpec(memory_space=pltpu.VMEM)] * len(arrays),
        out_specs=(pl.BlockSpec(memory_space=pl.ANY),) * len(arrays),
        scratch_shapes=[pltpu.SemaphoreType.DMA((len(arrays),))],
        compiler_params=pltpu.CompilerParams(vmem_limit_bytes=1 << 20),
        name="store_outputs",
    )(*arrays)


def body(queries, key_rows, value_rows, out_grad, doc_lengths, balance):
    flat = (2 * ROWS, DH)
    bal = balance.reshape(SPANS // 2, BLK)
    qg, kg, tab, row_tab = gather(
        queries.reshape(flat), out_grad.reshape(flat), key_rows, value_rows, bal, doc_lengths
    )
    own, acc = forward(tab, row_tab, qg, kg)
    stats = exchange(own)
    rows, keys = backward(tab, row_tab, qg, kg, stats, acc, own)
    attended, query_grad, key_grad, value_grad = store(*reduce(rows, keys))
    return attended.reshape(queries.shape), query_grad.reshape(queries.shape), key_grad, value_grad


def solution(mesh):
    return jax.shard_map(
        body,
        mesh=mesh,
        in_specs=(
            P(("seq", "ctx"), "head", None),
            P(("seq", "ctx"), None),
            P(("seq", "ctx"), None),
            P(("seq", "ctx"), "head", None),
            P("seq"),
            P("seq"),
        ),
        out_specs=(
            P(("seq", "ctx"), "head", None),
            P(("seq", "ctx"), "head", None),
            P(("seq", "ctx"), None),
            P(("seq", "ctx"), None),
        ),
        check_vma=False,
    )
```

```python
import math

import jax
import jax.numpy as jnp
from jax import lax
from jax.experimental import pallas as pl
from jax.experimental.pallas import tpu as pltpu
from jax.sharding import PartitionSpec as P

NX, NY, NZ = 4, 4, 8
XLO = 2
RUN = 64
DH = 128
HEADS_HERE = 4
ROWS = RUN * HEADS_HERE
BLK = 2 * RUN
KRUNS = XLO * NZ * 2
QRUNS = NY * 2
TILE = 4
SPANS = 128
ITEMS = QRUNS * (KRUNS // TILE)
DOCS = 8
NEGATIVE = -1e30
FLOOR = -1e29
FAR = 1 << 20
SCALING = 1.0 / math.sqrt(DH)
LOG2E = 1.0 / math.log(2.0)
MESH = pl.DeviceIdType.MESH
F32 = jnp.float32
BF16 = jnp.bfloat16


def here():
    c = lax.axis_index("ctx")
    h = lax.axis_index("head")
    return h, c // (NY * NZ), (c // NZ) % NY, c % NZ


def device(x, y, z):
    return {"ctx": ((x % XLO) * NY + y) * NZ + z, "head": x // XLO}


def greet(targets):
    barrier = pltpu.get_barrier_semaphore()
    for target in targets:
        pl.semaphore_signal(barrier, inc=1, device_id=target, device_id_type=MESH)
    return lambda: pl.semaphore_wait(barrier, len(targets))


def remote(src, dst, send, recv, target):
    return pltpu.make_async_remote_copy(
        src_ref=src, dst_ref=dst, send_sem=send, recv_sem=recv, device_id=target, device_id_type=MESH
    )


def tables(bal, lengths, tab, row_tab, xl, y, z):
    lane = lax.broadcasted_iota(jnp.int32, (1, SPANS), 1)
    slabs = [bal[pl.ds(pl.multiple_of((i * NY + y) * NZ, NZ), NZ), :] for i in range(XLO)]
    held = [slab[:, half * RUN : half * RUN + 1] // RUN for half in (0, 1) for slab in slabs]
    held = jnp.concatenate(held, axis=0)
    index = lax.broadcasted_iota(jnp.int32, (KRUNS, 1), 0)
    match = held == lane
    has = jnp.sum(jnp.where(match, 1, 0), axis=0, keepdims=True)
    which = jnp.sum(jnp.where(match, index, 0), axis=0, keepdims=True)
    before = jnp.sum(jnp.where(held < lane, 1, 0), axis=0, keepdims=True)
    rank = jnp.where(has > 0, before, -1)
    hit = jnp.where(rank == lax.broadcasted_iota(jnp.int32, (SPANS, 1), 0), 1.0, 0.0).astype(BF16)
    row = lax.broadcasted_iota(jnp.int32, (8, 1), 0)
    found = jnp.where(row == 0, lane, jnp.where(row == 1, which, 0)).astype(F32).astype(BF16)
    sorted_runs = lax.dot_general(found, hit, (((1,), (1,)), ((), ())), preferred_element_type=F32)
    sorted_runs = jnp.where((row == 0) & (lane >= KRUNS), F32(FAR // RUN), sorted_runs).astype(jnp.int32)
    q_rows = [bal[pl.ds((xl * NY + i) * NZ + z, 1), :] for i in range(NY)]
    low = jnp.concatenate([r[:, half * RUN : half * RUN + 1] for r in q_rows for half in (0, 1)], axis=0)
    pos = low + lax.broadcasted_iota(jnp.int32, (QRUNS, ROWS), 1) // HEADS_HERE
    start = jnp.zeros((QRUNS, ROWS), jnp.int32)
    first = jnp.zeros((QRUNS, 1), jnp.int32)
    end = 0
    for d in range(DOCS):
        end = end + lengths[d]
        first = jnp.where(low >= end, end, first)
        start = jnp.where(pos >= end, end, start)
    row_tab[0] = pos
    row_tab[1] = start
    low_run = jnp.sum(jnp.where((lane < first // RUN) & (has > 0), 1, 0), axis=1, keepdims=True)
    high_run = jnp.sum(jnp.where((lane <= low // RUN) & (has > 0), 1, 0), axis=1, keepdims=True)
    tiles = jnp.maximum((high_run - low_run + TILE - 1) // TILE, 1)
    own_lane = lax.broadcasted_iota(jnp.int32, (QRUNS, 1), 0) == lane
    low_row = jnp.sum(jnp.where(own_lane, low_run, 0), axis=0, keepdims=True)
    tiles_row = jnp.sum(jnp.where(own_lane, tiles, 0), axis=0, keepdims=True)
    tab[...] = jnp.where(row == 2, low_row, jnp.where(row == 3, tiles_row, sorted_runs))


def gather_kernel(
    q_ref, g_ref, k_ref, v_ref, bal_ref, len_ref, qg, kg, tab, row_tab, bal, lengths, lsem, ysend, yrecv, zsend, zrecv, xsend, xrecv
):
    h, xl, y, z = here()
    x = h * XLO + xl
    first = xl * NZ
    y_up, y_dn = device(x, (y + 1) % NY, z), device(x, (y + NY - 1) % NY, z)
    z_to = {d: device(x, y, (z + d + NZ) % NZ) for d in (1, 2, -1, -2)}
    x_up, x_dn = device((x + 1) % NX, y, z), device((x + NX - 1) % NX, y, z)
    meet = greet([y_up, y_dn, x_up, x_dn] + list(z_to.values()))
    kv = (k_ref, v_ref)
    started = []

    def go(copy):
        copy.start()
        started.append(copy)
        return copy

    sent_z = {}

    def z_send(sign, hops, dist, part):
        block = (z - sign * (dist - hops) + NZ) % NZ
        dst = kg.at[first + block, part]
        src = kv[part] if dist == hops else dst
        way = 0 if sign > 0 else 1
        sems = zsend.at[way, dist - 1, part], zrecv.at[way, dist - 1, part]
        sent_z[sign, dist, part] = go(remote(src, dst, *sems, z_to[sign * hops]))

    sent_x = []

    def x_send(slot, block):
        dst = kg.at[first + block, h]
        for side, target in ((0, x_up), (1, x_dn)):
            sent_x.append(go(remote(dst, dst, xsend.at[side, slot], xrecv.at[side, slot], target)))

    def local(src, dst, slot):
        copy = pltpu.make_async_copy(src, dst, lsem.at[slot])
        copy.start()
        return copy

    own_kv = [local(kv[part], kg.at[first + z, part], part) for part in (0, 1)]
    own_tab = [local(bal_ref, bal, 4), local(len_ref, lengths, 5)]
    meet()
    for part in (0, 1):
        for sign in (1, -1):
            z_send(sign, 2, 2, part)
    y_q_up = go(remote(q_ref, qg.at[y, 0], ysend.at[0], yrecv.at[0], y_up))
    y_g_dn = go(remote(g_ref, qg.at[y, 1], ysend.at[2], yrecv.at[2], y_dn))
    for part in (0, 1):
        for sign in (1, -1):
            z_send(sign, 1, 1, part)
    y_g_up = go(remote(g_ref, qg.at[y, 1], ysend.at[1], yrecv.at[1], y_up))
    y_q_dn = go(remote(q_ref, qg.at[y, 0], ysend.at[3], yrecv.at[3], y_dn))
    own_q = [local(ref, qg.at[y, part], 2 + part) for part, ref in ((0, q_ref), (1, g_ref))]
    for copy in own_kv:
        copy.wait()
    x_send(0, z)
    for copy in own_tab:
        copy.wait()
    tables(bal, lengths, tab, row_tab, xl, y, z)
    for part in (0, 1):
        for sign in (1, -1):
            sent_z[sign, 2, part].wait_recv()
            z_send(sign, 1, 3, part)
            if part == (0 if sign > 0 else 1):
                z_send(sign, 2, 4, part)
    x_send(1, (z - 2 + NZ) % NZ)
    x_send(2, (z + 2) % NZ)
    y_q_up.wait_recv()
    q_on = qg.at[(y + NY - 1) % NY, 0]
    y_fwd_up = go(remote(q_on, q_on, ysend.at[4], yrecv.at[4], y_up))
    y_g_dn.wait_recv()
    g_on = qg.at[(y + 1) % NY, 1]
    y_fwd_dn = go(remote(g_on, g_on, ysend.at[5], yrecv.at[5], y_dn))
    slot = 3
    for dist in (1, 3):
        for sign in (1, -1):
            for part in (0, 1):
                sent_z[sign, dist, part].wait_recv()
            x_send(slot, (z - sign * dist + NZ) % NZ)
            slot += 1
    sent_z[1, 4, 0].wait_recv()
    sent_z[-1, 4, 1].wait_recv()
    x_send(7, (z + NZ // 2) % NZ)
    for copy in (y_g_up, y_q_dn, y_fwd_up, y_fwd_dn):
        copy.wait_recv()
    for copy in sent_x:
        copy.wait_recv()
    for copy in started:
        copy.wait_send()
    for copy in own_q:
        copy.wait()


def gather(q, g, k, v, bal, lengths):
    hbm = pl.BlockSpec(memory_space=pltpu.HBM)
    vmem = pl.BlockSpec(memory_space=pltpu.VMEM)
    dma = pltpu.SemaphoreType.DMA
    return pl.pallas_call(
        gather_kernel,
        out_shape=(
            jax.ShapeDtypeStruct((NY, 2, 2 * ROWS, DH), BF16),
            jax.ShapeDtypeStruct((XLO * NZ, 2, BLK, DH), BF16),
            jax.ShapeDtypeStruct((8, SPANS), jnp.int32),
            jax.ShapeDtypeStruct((2, QRUNS, ROWS), jnp.int32),
        ),
        in_specs=[hbm] * 6,
        out_specs=(vmem,) * 4,
        scratch_shapes=[
            pltpu.VMEM((SPANS // 2, BLK), jnp.int32),
            pltpu.SMEM((DOCS,), jnp.int32),
            dma((6,)), dma((6,)), dma((6,)), dma((2, 4, 2)), dma((2, 4, 2)), dma((2, 8)), dma((2, 8)),
        ],
        compiler_params=pltpu.CompilerParams(collective_id=0, has_side_effects=True, vmem_limit_bytes=8 << 20),
        name="gather_rows",
    )(*(pltpu.with_memory_space_constraint(a, pltpu.HBM) for a in (q, g, k, v, bal, lengths)))


def tile_runs(tab, low_run, t):
    runs = [low_run + t * TILE + u for u in range(TILE)]
    return [tab[1, r] for r in runs], [tab[0, r] * RUN for r in runs]


def run_rows(index):
    return index % (XLO * NZ), pl.ds(pl.multiple_of(index // (XLO * NZ) * RUN, RUN), RUN)


def tile_rows(kg, indices, part):
    pieces = []
    for index in indices:
        block, rows = run_rows(index)
        pieces.append(kg[block, part, rows, :])
    return jnp.concatenate(pieces, axis=0)


def masked_scores(k, q, places, pos, start):
    scores = lax.dot_general(k, q, (((1,), (1,)), ((), ())), preferred_element_type=F32)
    offset = lax.broadcasted_iota(jnp.int32, (RUN, ROWS), 0)
    parts = []
    for u, base in enumerate(places):
        seen = (offset <= pos - base) & (offset >= start - base)
        parts.append(jnp.where(seen, scores[u * RUN : (u + 1) * RUN] * (SCALING * LOG2E), NEGATIVE))
    return jnp.concatenate(parts, axis=0)


def each_item(tab, process):
    total = sum(tab[3, i] for i in range(QRUNS))

    def step(i, state):
        q_run, t = state
        for u in range(2):
            process(q_run, t, 2 * i + u)
            more = (t + 1 < tab[3, q_run]) | (q_run == QRUNS - 1)
            q_run, t = jnp.where(more, q_run, q_run + 1), jnp.where(more, t + 1, 0)
        return q_run, t

    lax.fori_loop(0, (total + 1) // 2, step, (0, 0))


def query_rows(qg, q_run, part):
    return qg[q_run // 2, part, pl.ds(pl.multiple_of((q_run % 2) * ROWS, ROWS), ROWS), :]


def forward_kernel(tab, row_tab, qg, kg, stats, out, held, held_gw):
    stats[0] = jnp.full((QRUNS, ROWS), FLOOR, F32)
    stats[1] = jnp.zeros((QRUNS, ROWS), F32)
    stats[2] = jnp.zeros((QRUNS, ROWS), F32)
    out[...] = jnp.zeros_like(out)

    def process(q_run, t, item):
        at = pl.ds(q_run, 1)
        indices, places = tile_runs(tab, tab[2, q_run], t)
        s = masked_scores(
            tile_rows(kg, indices, 0), query_rows(qg, q_run, 0), places, row_tab[0, at, :], row_tab[1, at, :]
        )
        held[item] = s
        v = tile_rows(kg, indices, 1)
        gw = lax.dot_general(
            v, query_rows(qg, q_run, 1), (((1,), (1,)), ((), ())), preferred_element_type=F32
        )
        held_gw[item] = gw
        top = jnp.maximum(jnp.max(s, axis=0, keepdims=True), FLOOR)
        raw = jnp.exp2(s - top)
        total = jnp.sum(raw, axis=0, keepdims=True)
        inner = jnp.sum(raw * gw, axis=0, keepdims=True)
        acc = lax.dot_general(v, raw.astype(BF16), (((0,), (0,)), ((), ())), preferred_element_type=F32)
        old_top = stats[0, at, :]
        new_top = jnp.maximum(old_top, top)
        old_share, share = jnp.exp2(old_top - new_top), jnp.exp2(top - new_top)
        stats[0, at, :] = new_top
        stats[1, at, :] = stats[1, at, :] * old_share + total * share
        stats[2, at, :] = stats[2, at, :] * old_share + inner * share
        out[q_run] = out[q_run] * old_share + acc * share

    each_item(tab, process)


def forward(tab, row_tab, qg, kg):
    smem = pl.BlockSpec(memory_space=pltpu.SMEM)
    vmem = pl.BlockSpec(memory_space=pltpu.VMEM)
    return pl.pallas_call(
        forward_kernel,
        out_shape=(
            jax.ShapeDtypeStruct((3, QRUNS, ROWS), F32),
            jax.ShapeDtypeStruct((QRUNS, DH, ROWS), F32),
            jax.ShapeDtypeStruct((ITEMS, TILE * RUN, ROWS), F32),
            jax.ShapeDtypeStruct((ITEMS, TILE * RUN, ROWS), F32),
        ),
        in_specs=[smem, vmem, vmem, vmem],
        out_specs=(vmem,) * 4,
        compiler_params=pltpu.CompilerParams(vmem_limit_bytes=8 << 20),
        name="forward_stats",
    )(tab, row_tab, qg, kg)


def exchange_kernel(mine, out, lsem, send, recv):
    h, xl, y, z = here()
    x = h * XLO + xl
    targets = [device(x, (y + d) % NY, z) for d in range(1, NY)]
    greet(targets)()
    copies = []
    for d, target in enumerate(targets):
        copy = remote(mine, out.at[y], send.at[d], recv.at[d], target)
        copy.start()
        copies.append(copy)
    own = pltpu.make_async_copy(mine, out.at[y], lsem)
    own.start()
    own.wait()
    for copy in copies:
        copy.wait()


def exchange(stats):
    vmem = pl.BlockSpec(memory_space=pltpu.VMEM)
    dma = pltpu.SemaphoreType.DMA
    return pl.pallas_call(
        exchange_kernel,
        out_shape=jax.ShapeDtypeStruct((NY,) + stats.shape, F32),
        in_specs=[vmem],
        out_specs=vmem,
        scratch_shapes=[dma, dma((NY - 1,)), dma((NY - 1,))],
        compiler_params=pltpu.CompilerParams(collective_id=1, has_side_effects=True, vmem_limit_bytes=1 << 20),
        name="exchange_stats",
    )(stats)


def backward_kernel(
    tab, qg, kg, stats, held, held_gw, share_out, grad_acc, kv_acc, row_stats
):
    y = here()[2]
    kv_acc[...] = jnp.zeros_like(kv_acc)
    grad_acc[...] = jnp.zeros_like(grad_acc)
    top = jnp.maximum(jnp.maximum(stats[0, 0], stats[1, 0]), jnp.maximum(stats[2, 0], stats[3, 0]))
    shares = [jnp.exp2(stats[i, 0] - top) for i in range(NY)]
    total = sum(stats[i, 1] * shares[i] for i in range(NY))
    log_total = top + jnp.log(total) * LOG2E
    row_stats[0] = log_total
    row_stats[1] = sum(stats[i, 2] * shares[i] for i in range(NY)) / total
    share_out[...] = jnp.exp2(stats[y, 0] - log_total)

    def process(q_run, t, item):
        at = pl.ds(q_run, 1)
        indices, _ = tile_runs(tab, tab[2, q_run], t)
        weights = jnp.exp2(held[item] - row_stats[0, at, :])
        gs = (weights * (held_gw[item] - row_stats[1, at, :])).astype(BF16)
        value_part = jnp.dot(weights.astype(BF16), query_rows(qg, q_run, 1), preferred_element_type=F32)
        key_part = jnp.dot(gs, query_rows(qg, q_run, 0), preferred_element_type=F32)
        grad = lax.dot_general(
            tile_rows(kg, indices, 0), gs, (((0,), (0,)), ((), ())), preferred_element_type=F32
        )
        for u, index in enumerate(indices):
            block, to = run_rows(index)
            kv_acc[1, block, to, :] += value_part[u * RUN : (u + 1) * RUN]
            kv_acc[0, block, to, :] += key_part[u * RUN : (u + 1) * RUN]
        grad_acc[q_run] += grad

    each_item(tab, process)


def backward(tab, qg, kg, stats, held, held_gw):
    smem = pl.BlockSpec(memory_space=pltpu.SMEM)
    vmem = pl.BlockSpec(memory_space=pltpu.VMEM)
    return pl.pallas_call(
        backward_kernel,
        out_shape=(
            jax.ShapeDtypeStruct((QRUNS, ROWS), F32),
            jax.ShapeDtypeStruct((QRUNS, DH, ROWS), F32),
            jax.ShapeDtypeStruct((2, XLO * NZ, BLK, DH), F32),
        ),
        in_specs=[smem] + [vmem] * 5,
        out_specs=(vmem,) * 3,
        scratch_shapes=[pltpu.VMEM((2, QRUNS, ROWS), F32)],
        compiler_params=pltpu.CompilerParams(vmem_limit_bytes=8 << 20),
        name="backward_terms",
    )(tab, qg, kg, stats, held, held_gw)


AHEAD = (4, 3, 2, 1)
BEHIND = (5, 6, 7, 0)


def reduce_kernel(
    acc, share, grad, kv, att, qgrad, kgrad, vgrad,
    rows, ybuf, ysum, xout, xbuf, xsum, zsum, zbuf, last,
    ysend, yrecv, xsend, xrecv, zsend, zrecv, hsend, hrecv,
):
    h, xl, y, z = here()
    x = h * XLO + xl
    y_up, y_dn = device(x, (y + 1) % NY, z), device(x, (y + NY - 1) % NY, z)
    x_to = tuple(device((x + d) % NX, y, z) for d in (1, NX - 1, 2))
    z_all = [device(x, y, (z + d) % NZ) for d in range(1, NZ)]
    meet = greet([y_up, y_dn, *x_to, *z_all])
    started = []

    def go(copy):
        copy.start()
        started.append(copy)
        return copy

    def term(step, offset):
        ring = (x + step) % NX
        part = ring // XLO
        block = kv[part, (ring % XLO) * NZ + (z + offset) % NZ]
        return block * jnp.where(part == 0, F32(SCALING), F32(1.0))

    def put_rows(yy):
        for half in (0, 1):
            q_run = yy * 2 + half
            to = pl.ds(half * ROWS, ROWS)
            rows[yy, 0, to, :] = (acc[q_run] * share[pl.ds(q_run, 1), :]).T.astype(BF16)
            rows[yy, 1, to, :] = (grad[q_run] * SCALING).T.astype(BF16)

    def x_copy(kind, way, i, src):
        return go(remote(src, xbuf.at[kind, way, i], xsend.at[kind, way, i], xrecv.at[kind, way, i], x_to[way]))

    offsets = (AHEAD, BEHIND)
    sent = {}
    for i in range(4):
        for way in (0, 1):
            xout[0, way, i] = term(2, offsets[way][i]).astype(BF16)
    meet()
    for i in range(4):
        for way in (0, 1):
            sent[0, way, i] = x_copy(0, way, i, xout.at[0, way, i])
    y_far, y_next, y_prev = (y + 2) % NY, (y + 1) % NY, (y + NY - 1) % NY
    put_rows(y_far)
    y_a = go(remote(rows.at[y_far, 0], ybuf.at[0], ysend.at[0], yrecv.at[0], y_up))
    y_b = go(remote(rows.at[y_far, 1], ybuf.at[1], ysend.at[1], yrecv.at[1], y_dn))
    for i in range(4):
        for way in (0, 1):
            xout[1, way, i] = term(1 if way == 0 else 3, offsets[1 - way][i]).astype(BF16)
            sent[1, way, i] = x_copy(1, way, i, xout.at[1, way, i])
    put_rows(y_next)
    put_rows(y_prev)
    y_c = go(remote(rows.at[y_next, 1], ybuf.at[2], ysend.at[2], yrecv.at[2], y_up))
    y_d = go(remote(rows.at[y_prev, 0], ybuf.at[3], ysend.at[3], yrecv.at[3], y_dn))
    for i in range(4):
        for way in (0, 1):
            sent[0, way, i].wait_recv()
            own = term(1 if way == 0 else 3, offsets[way][i])
            xsum[way, i] = (xbuf[0, way, i].astype(F32) + own).astype(BF16)
            sent[2, way, i] = x_copy(2, way, i, xsum.at[way, i])
    y_a.wait_recv()
    ysum[0] = (ybuf[0].astype(F32) + rows[y_next, 0].astype(F32)).astype(BF16)
    y_e = go(remote(ysum.at[0], ybuf.at[4], ysend.at[4], yrecv.at[4], y_up))
    y_b.wait_recv()
    ysum[1] = (ybuf[1].astype(F32) + rows[y_prev, 1].astype(F32)).astype(BF16)
    y_f = go(remote(ysum.at[1], ybuf.at[5], ysend.at[5], yrecv.at[5], y_dn))
    total = None
    z_copies = []
    for i in range(4):
        for way in (0, 1):
            sent[2, way, i].wait_recv()
            sent[1, 1 - way, i].wait_recv()
            offset = offsets[way][i]
            block = term(0, offset) + xbuf[2, way, i].astype(F32) + xbuf[1, 1 - way, i].astype(F32)
            if offset == 0:
                total = block
            else:
                zsum[offset - 1] = block.astype(BF16)
                z_copies.append(
                    go(
                        remote(
                            zsum.at[offset - 1], zbuf.at[offset - 1],
                            zsend.at[offset - 1], zrecv.at[offset - 1], z_all[offset - 1],
                        )
                    )
                )
    put_rows(y)
    y_d.wait_recv()
    y_e.wait_recv()
    att[...] = (rows[y, 0].astype(F32) + ybuf[3].astype(F32) + ybuf[4].astype(F32)).astype(BF16)
    y_c.wait_recv()
    y_f.wait_recv()
    qgrad[...] = (rows[y, 1].astype(F32) + ybuf[2].astype(F32) + ybuf[5].astype(F32)).astype(BF16)
    for copy in z_copies:
        copy.wait_recv()
    for d in range(NZ - 1):
        total = total + zbuf[d].astype(F32)
    last[0] = total.astype(BF16)
    final = go(remote(last.at[0], last.at[1], hsend, hrecv, x_to[2]))
    final.wait_recv()
    mine, other = last[0], last[1]
    kgrad[...] = jnp.where(h == 0, mine, other)
    vgrad[...] = jnp.where(h == 0, other, mine)
    for copy in started:
        copy.wait_send()


def reduce(acc, share, grad, kv):
    vmem = pl.BlockSpec(memory_space=pltpu.VMEM)
    dma = pltpu.SemaphoreType.DMA
    block = (BLK, DH)
    return pl.pallas_call(
        reduce_kernel,
        out_shape=(
            jax.ShapeDtypeStruct((2 * ROWS, DH), BF16),
            jax.ShapeDtypeStruct((2 * ROWS, DH), BF16),
            jax.ShapeDtypeStruct(block, BF16),
            jax.ShapeDtypeStruct(block, BF16),
        ),
        in_specs=[vmem] * 4,
        out_specs=(vmem,) * 4,
        scratch_shapes=[
            pltpu.VMEM((NY, 2, 2 * ROWS, DH), BF16),
            pltpu.VMEM((6, 2 * ROWS, DH), BF16),
            pltpu.VMEM((2, 2 * ROWS, DH), BF16),
            pltpu.VMEM((2, 2, 4) + block, BF16),
            pltpu.VMEM((3, 2, 4) + block, BF16),
            pltpu.VMEM((2, 4) + block, BF16),
            pltpu.VMEM((NZ - 1,) + block, BF16),
            pltpu.VMEM((NZ - 1,) + block, BF16),
            pltpu.VMEM((2,) + block, BF16),
            dma((6,)), dma((6,)), dma((3, 2, 4)), dma((3, 2, 4)), dma((NZ - 1,)), dma((NZ - 1,)), dma, dma,
        ],
        compiler_params=pltpu.CompilerParams(collective_id=2, has_side_effects=True, vmem_limit_bytes=8 << 20),
        name="reduce_terms",
    )(acc, share, grad, kv)


def store_kernel(*refs):
    count = len(refs) // 2
    copies = [pltpu.make_async_copy(refs[i], refs[count + i], refs[-1].at[i]) for i in range(count)]
    for copy in copies:
        copy.start()
    for copy in copies:
        copy.wait()


def store(*arrays):
    return pl.pallas_call(
        store_kernel,
        out_shape=tuple(jax.ShapeDtypeStruct(a.shape, a.dtype) for a in arrays),
        in_specs=[pl.BlockSpec(memory_space=pltpu.VMEM)] * len(arrays),
        out_specs=(pl.BlockSpec(memory_space=pl.ANY),) * len(arrays),
        scratch_shapes=[pltpu.SemaphoreType.DMA((len(arrays),))],
        compiler_params=pltpu.CompilerParams(vmem_limit_bytes=1 << 20),
        name="store_outputs",
    )(*arrays)


def body(queries, key_rows, value_rows, out_grad, doc_lengths, balance):
    flat = (2 * ROWS, DH)
    bal = balance.reshape(SPANS // 2, BLK)
    qg, kg, tab, row_tab = gather(
        queries.reshape(flat), out_grad.reshape(flat), key_rows, value_rows, bal, doc_lengths
    )
    own, acc, held, held_gw = forward(tab, row_tab, qg, kg)
    share, grad, kv = backward(tab, qg, kg, exchange(own), held, held_gw)
    attended, query_grad, key_grad, value_grad = store(*reduce(acc, share, grad, kv))
    return attended.reshape(queries.shape), query_grad.reshape(queries.shape), key_grad, value_grad


def solution(mesh):
    return jax.shard_map(
        body,
        mesh=mesh,
        in_specs=(
            P(("seq", "ctx"), "head", None),
            P(("seq", "ctx"), None),
            P(("seq", "ctx"), None),
            P(("seq", "ctx"), "head", None),
            P("seq"),
            P("seq"),
        ),
        out_specs=(
            P(("seq", "ctx"), "head", None),
            P(("seq", "ctx"), "head", None),
            P(("seq", "ctx"), None),
            P(("seq", "ctx"), None),
        ),
        check_vma=False,
    )
```

```python
import functools
import math

import jax
import jax.numpy as jnp
from jax import lax
from jax.experimental import pallas as pl
from jax.experimental.pallas import tpu as pltpu
from jax.sharding import PartitionSpec as P

NX, NY, NZ = 4, 4, 8
XLO = 2
RUN = 64
DH = 128
HEADS_HERE = 4
ROWS = RUN * HEADS_HERE
BLK = 2 * RUN
KRUNS = XLO * NZ * 2
QRUNS = NY * 2
TILE = 4
SPANS = 128
ITEMS = QRUNS * (KRUNS // TILE - 1)
UNROLL = 4
DOCS = 8
NEGATIVE = -1e30
FLOOR = -1e29
FAR = 1 << 20
SCALING = 1.0 / math.sqrt(DH)
LOG2E = 1.0 / math.log(2.0)
MESH = pl.DeviceIdType.MESH
F32 = jnp.float32
BF16 = jnp.bfloat16


def here():
    c = lax.axis_index("ctx")
    h = lax.axis_index("head")
    return h, c // (NY * NZ), (c // NZ) % NY, c % NZ


def device(x, y, z):
    return {"ctx": ((x % XLO) * NY + y) * NZ + z, "head": x // XLO}


def greet(targets):
    barrier = pltpu.get_barrier_semaphore()
    for target in targets:
        pl.semaphore_signal(barrier, inc=1, device_id=target, device_id_type=MESH)
    return lambda: pl.semaphore_wait(barrier, len(targets))


def remote(src, dst, send, recv, target):
    return pltpu.make_async_remote_copy(
        src_ref=src, dst_ref=dst, send_sem=send, recv_sem=recv, device_id=target, device_id_type=MESH
    )


def tables(bal, lengths, tab, row_tab, xl, y, z):
    lane = lax.broadcasted_iota(jnp.int32, (1, SPANS), 1)
    slabs = [bal[pl.ds(pl.multiple_of((i * NY + y) * NZ, NZ), NZ), :] for i in range(XLO)]
    held = [slab[:, half * RUN : half * RUN + 1] // RUN for half in (0, 1) for slab in slabs]
    held = jnp.concatenate(held, axis=0)
    index = lax.broadcasted_iota(jnp.int32, (KRUNS, 1), 0)
    match = held == lane
    has = jnp.sum(jnp.where(match, 1, 0), axis=0, keepdims=True)
    which = jnp.sum(jnp.where(match, index, 0), axis=0, keepdims=True)
    before = jnp.sum(jnp.where(held < lane, 1, 0), axis=0, keepdims=True)
    rank = jnp.where(has > 0, before, -1)
    hit = jnp.where(rank == lax.broadcasted_iota(jnp.int32, (SPANS, 1), 0), 1.0, 0.0).astype(BF16)
    row = lax.broadcasted_iota(jnp.int32, (8, 1), 0)
    block, half = which % (XLO * NZ), which // (XLO * NZ)
    found = jnp.where(row == 0, lane, jnp.where(row == 1, block, jnp.where(row == 6, half, 0)))
    found = found.astype(F32).astype(BF16)
    sorted_runs = lax.dot_general(found, hit, (((1,), (1,)), ((), ())), preferred_element_type=F32)
    sorted_runs = jnp.where((row == 0) & (lane >= KRUNS), F32(FAR // RUN), sorted_runs).astype(jnp.int32)
    q_rows = [bal[pl.ds((xl * NY + i) * NZ + z, 1), :] for i in range(NY)]
    low = jnp.concatenate([r[:, half * RUN : half * RUN + 1] for r in q_rows for half in (0, 1)], axis=0)
    pos = low + lax.broadcasted_iota(jnp.int32, (QRUNS, ROWS), 1) // HEADS_HERE
    start = jnp.zeros((QRUNS, ROWS), jnp.int32)
    first = jnp.zeros((QRUNS, 1), jnp.int32)
    end = 0
    for d in range(DOCS):
        end = end + lengths[d]
        first = jnp.where(low >= end, end, first)
        start = jnp.where(pos >= end, end, start)
    row_tab[0] = pos
    row_tab[1] = start
    low_run = jnp.sum(jnp.where((lane < first // RUN) & (has > 0), 1, 0), axis=1, keepdims=True)
    high_run = jnp.sum(jnp.where((lane <= low // RUN) & (has > 0), 1, 0), axis=1, keepdims=True)
    tiles = jnp.maximum((high_run - low_run + TILE - 1) // TILE, 1)
    own_lane = lax.broadcasted_iota(jnp.int32, (QRUNS, 1), 0) == lane
    low_row = jnp.sum(jnp.where(own_lane, low_run, 0), axis=0, keepdims=True)
    more = tiles - 1
    upper = lax.broadcasted_iota(jnp.int32, (QRUNS, 1), 0) >= lax.broadcasted_iota(jnp.int32, (1, SPANS), 1)
    more_row = jnp.sum(jnp.where(own_lane, more, 0), axis=0, keepdims=True)
    ends = jnp.sum(jnp.where(upper, more_row, 0), axis=1, keepdims=True)
    passed = lane >= ends
    run_row = jnp.minimum(jnp.sum(jnp.where(passed, 1, 0), axis=0, keepdims=True), QRUNS - 1)
    tile_row = lane + 1 - jnp.sum(jnp.where(passed, more, 0), axis=0, keepdims=True)
    count = jnp.sum(more, axis=0, keepdims=True)
    tile_row = jnp.where(lane >= count, KRUNS // TILE, tile_row)
    values = [None, None, low_row, run_row, tile_row, jnp.where(lane == 0, count, 0)]
    out = sorted_runs
    for i in range(2, 6):
        out = jnp.where(row == i, values[i], out)
    tab[...] = out


def gather_kernel(
    q_ref, g_ref, k_ref, v_ref, bal_ref, len_ref, qg, kg, tab, row_tab, bal, lengths, lsem, ysend, yrecv, zsend, zrecv, xsend, xrecv
):
    h, xl, y, z = here()
    x = h * XLO + xl
    first = xl * NZ
    y_up, y_dn = device(x, (y + 1) % NY, z), device(x, (y + NY - 1) % NY, z)
    z_to = {d: device(x, y, (z + d + NZ) % NZ) for d in (1, 2, -1, -2)}
    x_up, x_dn = device((x + 1) % NX, y, z), device((x + NX - 1) % NX, y, z)
    meet = greet([y_up, y_dn, x_up, x_dn] + list(z_to.values()))
    kv = (k_ref, v_ref)
    started = []

    def go(copy):
        copy.start()
        started.append(copy)
        return copy

    sent_z = {}

    def z_send(sign, hops, dist, part):
        block = (z - sign * (dist - hops) + NZ) % NZ
        dst = kg.at[first + block, part]
        src = kv[part] if dist == hops else dst
        way = 0 if sign > 0 else 1
        sems = zsend.at[way, dist - 1, part], zrecv.at[way, dist - 1, part]
        sent_z[sign, dist, part] = go(remote(src, dst, *sems, z_to[sign * hops]))

    sent_x = []

    def x_send(slot, block):
        dst = kg.at[first + block, h]
        for side, target in ((0, x_up), (1, x_dn)):
            sent_x.append(go(remote(dst, dst, xsend.at[side, slot], xrecv.at[side, slot], target)))

    def local(src, dst, slot):
        copy = pltpu.make_async_copy(src, dst, lsem.at[slot])
        copy.start()
        return copy

    own_kv = [local(kv[part], kg.at[first + z, part], part) for part in (0, 1)]
    own_tab = [local(bal_ref, bal, 4), local(len_ref, lengths, 5)]
    meet()
    for part in (0, 1):
        for sign in (1, -1):
            z_send(sign, 2, 2, part)
    y_q_up = go(remote(q_ref, qg.at[y, 0], ysend.at[0], yrecv.at[0], y_up))
    y_g_dn = go(remote(g_ref, qg.at[y, 1], ysend.at[2], yrecv.at[2], y_dn))
    for part in (0, 1):
        for sign in (1, -1):
            z_send(sign, 1, 1, part)
    y_g_up = go(remote(g_ref, qg.at[y, 1], ysend.at[1], yrecv.at[1], y_up))
    y_q_dn = go(remote(q_ref, qg.at[y, 0], ysend.at[3], yrecv.at[3], y_dn))
    own_q = [local(ref, qg.at[y, part], 2 + part) for part, ref in ((0, q_ref), (1, g_ref))]
    for copy in own_kv:
        copy.wait()
    x_send(0, z)
    for copy in own_tab:
        copy.wait()
    tables(bal, lengths, tab, row_tab, xl, y, z)
    for part in (0, 1):
        for sign in (1, -1):
            sent_z[sign, 2, part].wait_recv()
            z_send(sign, 1, 3, part)
            if part == (0 if sign > 0 else 1):
                z_send(sign, 2, 4, part)
    x_send(1, (z - 2 + NZ) % NZ)
    x_send(2, (z + 2) % NZ)
    y_q_up.wait_recv()
    q_on = qg.at[(y + NY - 1) % NY, 0]
    y_fwd_up = go(remote(q_on, q_on, ysend.at[4], yrecv.at[4], y_up))
    y_g_dn.wait_recv()
    g_on = qg.at[(y + 1) % NY, 1]
    y_fwd_dn = go(remote(g_on, g_on, ysend.at[5], yrecv.at[5], y_dn))
    slot = 3
    for dist in (1, 3):
        for sign in (1, -1):
            for part in (0, 1):
                sent_z[sign, dist, part].wait_recv()
            x_send(slot, (z - sign * dist + NZ) % NZ)
            slot += 1
    sent_z[1, 4, 0].wait_recv()
    sent_z[-1, 4, 1].wait_recv()
    x_send(7, (z + NZ // 2) % NZ)
    for copy in (y_g_up, y_q_dn, y_fwd_up, y_fwd_dn):
        copy.wait_recv()
    for copy in sent_x:
        copy.wait_recv()
    for copy in started:
        copy.wait_send()
    for copy in own_q:
        copy.wait()


def gather(q, g, k, v, bal, lengths):
    hbm = pl.BlockSpec(memory_space=pltpu.HBM)
    vmem = pl.BlockSpec(memory_space=pltpu.VMEM)
    dma = pltpu.SemaphoreType.DMA
    return pl.pallas_call(
        gather_kernel,
        out_shape=(
            jax.ShapeDtypeStruct((NY, 2, 2 * ROWS, DH), BF16),
            jax.ShapeDtypeStruct((XLO * NZ, 2, 2, RUN, DH), BF16),
            jax.ShapeDtypeStruct((8, SPANS), jnp.int32),
            jax.ShapeDtypeStruct((2, QRUNS, ROWS), jnp.int32),
        ),
        in_specs=[hbm] * 6,
        out_specs=(vmem,) * 4,
        scratch_shapes=[
            pltpu.VMEM((SPANS // 2, BLK), jnp.int32),
            pltpu.SMEM((DOCS,), jnp.int32),
            dma((6,)), dma((6,)), dma((6,)), dma((2, 4, 2)), dma((2, 4, 2)), dma((2, 8)), dma((2, 8)),
        ],
        compiler_params=pltpu.CompilerParams(collective_id=0, has_side_effects=True, vmem_limit_bytes=8 << 20),
        name="gather_rows",
    )(*(pltpu.with_memory_space_constraint(a, pltpu.HBM) for a in (q, g, k, v, bal, lengths)))


def tile_runs(tab, low_run, t):
    runs = [low_run + t * TILE + u for u in range(TILE)]
    return [(tab[1, r], tab[6, r]) for r in runs], [tab[0, r] * RUN for r in runs]


def tile_rows(kg, indices, part):
    return jnp.concatenate([kg[block, part, half] for block, half in indices], axis=0)


def masked_scores(k, q, places, pos, start):
    scores = lax.dot_general(k, q, (((1,), (1,)), ((), ())), preferred_element_type=F32)
    offset = lax.broadcasted_iota(jnp.int32, (RUN, ROWS), 0)
    parts = []
    for u, base in enumerate(places):
        seen = (offset <= pos - base) & (offset >= start - base)
        parts.append(jnp.where(seen, scores[u * RUN : (u + 1) * RUN] * (SCALING * LOG2E), NEGATIVE))
    return jnp.concatenate(parts, axis=0)


def together(process, items):
    for end in [process(*item) for item in items]:
        end()


def first_tiles(process):
    def step(i, _):
        together(process, [(UNROLL * i + u, 0, UNROLL * i + u) for u in range(UNROLL)])
        return 0

    lax.fori_loop(0, QRUNS // UNROLL, step, 0)


def further_tiles(tab, process):
    def step(i, _):
        slots = [UNROLL * i + u for u in range(UNROLL)]
        together(process, [(tab[3, slot], tab[4, slot], slot) for slot in slots])
        return 0

    lax.fori_loop(0, (tab[5, 0] + UNROLL - 1) // UNROLL, step, 0)


def query_rows(qg, q_run, part):
    return qg[q_run // 2, part, pl.ds(pl.multiple_of((q_run % 2) * ROWS, ROWS), ROWS), :]


def forward_tile(tab, row_tab, qg, kg, held, held_gw, combine):
    def process(q_run, t, slot):
        at = pl.ds(q_run, 1)
        indices, places = tile_runs(tab, tab[2, q_run], t)
        s = masked_scores(
            tile_rows(kg, indices, 0), query_rows(qg, q_run, 0), places, row_tab[0, at, :], row_tab[1, at, :]
        )
        held[slot] = s
        v = tile_rows(kg, indices, 1)
        gw = lax.dot_general(
            v, query_rows(qg, q_run, 1), (((1,), (1,)), ((), ())), preferred_element_type=F32
        )
        held_gw[slot] = gw
        top = jnp.maximum(jnp.max(s, axis=0, keepdims=True), FLOOR)
        raw = jnp.exp2(s - top)
        total = jnp.sum(raw, axis=0, keepdims=True)
        inner = jnp.sum(raw * gw, axis=0, keepdims=True)
        acc = lax.dot_general(v, raw.astype(BF16), (((0,), (0,)), ((), ())), preferred_element_type=F32)
        return lambda: combine(q_run, top, total, inner, acc)

    return process


def combined(old, old_acc, top, total, inner, acc):
    new_top = jnp.maximum(old[0], top)
    old_share, share = jnp.exp2(old[0] - new_top), jnp.exp2(top - new_top)
    stats = new_top, old[1] * old_share + total * share, old[2] * old_share + inner * share
    return stats, old_acc * old_share + acc * share


def forward_kernel(tab, row_tab, qg, kg, stats, out, held, held_gw):
    stats[0] = jnp.full((QRUNS, ROWS), FLOOR, F32)
    stats[1] = jnp.zeros((QRUNS, ROWS), F32)
    stats[2] = jnp.zeros((QRUNS, ROWS), F32)
    out[...] = jnp.zeros_like(out)

    def combine(q_run, *new):
        at = pl.ds(q_run, 1)
        rows, out[q_run] = combined([stats[i, at, :] for i in range(3)], out[q_run], *new)
        for i in range(3):
            stats[i, at, :] = rows[i]

    further_tiles(tab, forward_tile(tab, row_tab, qg, kg, held, held_gw, combine))


def forward(tab, row_tab, qg, kg):
    smem = pl.BlockSpec(memory_space=pltpu.SMEM)
    vmem = pl.BlockSpec(memory_space=pltpu.VMEM)
    return pl.pallas_call(
        forward_kernel,
        out_shape=(
            jax.ShapeDtypeStruct((3, QRUNS, ROWS), F32),
            jax.ShapeDtypeStruct((QRUNS, DH, ROWS), F32),
            jax.ShapeDtypeStruct((ITEMS, TILE * RUN, ROWS), F32),
            jax.ShapeDtypeStruct((ITEMS, TILE * RUN, ROWS), F32),
        ),
        in_specs=[smem, vmem, vmem, vmem],
        out_specs=(vmem,) * 4,
        compiler_params=pltpu.CompilerParams(vmem_limit_bytes=8 << 20),
        name="forward_stats",
    )(tab, row_tab, qg, kg)


def exchange_kernel(tab, row_tab, qg, kg, part, part_acc, out, acc_out, held, held_gw, mine, lsem, send, recv):
    h, xl, y, z = here()
    x = h * XLO + xl
    targets = [device(x, (y + d) % NY, z) for d in range(1, NY)]
    meet = greet(targets)

    def combine(q_run, *new):
        at = pl.ds(q_run, 1)
        rows, acc_out[q_run] = combined([part[i, at, :] for i in range(3)], part_acc[q_run], *new)
        for i in range(3):
            mine[i, at, :] = rows[i]

    first_tiles(forward_tile(tab, row_tab, qg, kg, held, held_gw, combine))
    meet()
    copies = []
    for d, target in enumerate(targets):
        copy = remote(mine, out.at[y], send.at[d], recv.at[d], target)
        copy.start()
        copies.append(copy)
    own = pltpu.make_async_copy(mine, out.at[y], lsem)
    own.start()
    own.wait()
    for copy in copies:
        copy.wait()


def exchange(tab, row_tab, qg, kg, part, part_acc):
    smem = pl.BlockSpec(memory_space=pltpu.SMEM)
    vmem = pl.BlockSpec(memory_space=pltpu.VMEM)
    dma = pltpu.SemaphoreType.DMA
    return pl.pallas_call(
        exchange_kernel,
        out_shape=(
            jax.ShapeDtypeStruct((NY,) + part.shape, F32),
            jax.ShapeDtypeStruct(part_acc.shape, F32),
            jax.ShapeDtypeStruct((QRUNS, TILE * RUN, ROWS), F32),
            jax.ShapeDtypeStruct((QRUNS, TILE * RUN, ROWS), F32),
        ),
        in_specs=[smem] + [vmem] * 5,
        out_specs=(vmem,) * 4,
        scratch_shapes=[pltpu.VMEM(part.shape, F32), dma, dma((NY - 1,)), dma((NY - 1,))],
        compiler_params=pltpu.CompilerParams(collective_id=1, has_side_effects=True, vmem_limit_bytes=8 << 20),
        name="exchange_stats",
    )(tab, row_tab, qg, kg, part, part_acc)


def backward_kernel(
    tab, qg, kg, stats, held, held_gw, more, more_gw, share_out, grad_acc, kv_acc, row_stats
):
    y = here()[2]
    kv_acc[...] = jnp.zeros_like(kv_acc)
    grad_acc[...] = jnp.zeros_like(grad_acc)
    top = jnp.maximum(jnp.maximum(stats[0, 0], stats[1, 0]), jnp.maximum(stats[2, 0], stats[3, 0]))
    shares = [jnp.exp2(stats[i, 0] - top) for i in range(NY)]
    total = sum(stats[i, 1] * shares[i] for i in range(NY))
    log_total = top + jnp.log(total) * LOG2E
    row_stats[0] = log_total
    row_stats[1] = sum(stats[i, 2] * shares[i] for i in range(NY)) / total
    share_out[...] = jnp.exp2(stats[y, 0] - log_total)

    def process(held, held_gw, q_run, t, slot):
        at = pl.ds(q_run, 1)
        indices, _ = tile_runs(tab, tab[2, q_run], t)
        weights = jnp.exp2(held[slot] - row_stats[0, at, :])
        gs = (weights * (held_gw[slot] - row_stats[1, at, :])).astype(BF16)
        value_part = jnp.dot(weights.astype(BF16), query_rows(qg, q_run, 1), preferred_element_type=F32)
        key_part = jnp.dot(gs, query_rows(qg, q_run, 0), preferred_element_type=F32)
        grad = lax.dot_general(
            tile_rows(kg, indices, 0), gs, (((0,), (0,)), ((), ())), preferred_element_type=F32
        )

        def end():
            for u, (block, half) in enumerate(indices):
                kv_acc[1, block, half] += value_part[u * RUN : (u + 1) * RUN]
                kv_acc[0, block, half] += key_part[u * RUN : (u + 1) * RUN]
            grad_acc[q_run] += grad

        return end

    first_tiles(functools.partial(process, held, held_gw))
    further_tiles(tab, functools.partial(process, more, more_gw))


def backward(tab, qg, kg, stats, held, held_gw, more, more_gw):
    smem = pl.BlockSpec(memory_space=pltpu.SMEM)
    vmem = pl.BlockSpec(memory_space=pltpu.VMEM)
    return pl.pallas_call(
        backward_kernel,
        out_shape=(
            jax.ShapeDtypeStruct((QRUNS, ROWS), F32),
            jax.ShapeDtypeStruct((QRUNS, DH, ROWS), F32),
            jax.ShapeDtypeStruct((2, XLO * NZ, 2, RUN, DH), F32),
        ),
        in_specs=[smem] + [vmem] * 7,
        out_specs=(vmem,) * 3,
        scratch_shapes=[pltpu.VMEM((2, QRUNS, ROWS), F32)],
        compiler_params=pltpu.CompilerParams(vmem_limit_bytes=8 << 20),
        name="backward_terms",
    )(tab, qg, kg, stats, held, held_gw, more, more_gw)


AHEAD = (4, 3, 2)
BEHIND = (5, 6)
LATE = AHEAD + BEHIND


def reduce_kernel(
    acc, share, grad, kv, att, qgrad, kgrad, vgrad,
    rows, ybuf, ysum, nout, nbuf, oout, obuf, xout, xbuf, xsum, zsum, zbuf, last,
    ysend, yrecv, nsend, nrecv, osend, orecv, xsend, xrecv, zsend, zrecv, hsend, hrecv,
):
    h, xl, y, z = here()
    x = h * XLO + xl
    y_up, y_dn = device(x, (y + 1) % NY, z), device(x, (y + NY - 1) % NY, z)
    x_to = tuple(device((x + d) % NX, y, z) for d in (1, 2, 3))
    z_to = {d: device(x, y, (z + d) % NZ) for d in range(1, NZ)}
    meet = greet([*z_to.values(), x_to[1], x_to[0], x_to[2], y_up, y_dn])
    started = []

    def go(copy):
        copy.start()
        started.append(copy)
        return copy

    def scaled(part, block):
        return kv[part, block] * jnp.where(part == 0, F32(SCALING), F32(1.0))

    def term(step, offset):
        ring = (x + step) % NX
        return scaled(ring // XLO, (ring % XLO) * NZ + (z + offset) % NZ)

    def near_term(step):
        ring = (x + step) % NX
        sides = [nbuf[side, ring % XLO, ring // XLO].astype(F32) for side in (0, 1)]
        return term(step, 0) + sides[0] + sides[1]

    def put_rows(yy):
        for half in (0, 1):
            q_run = yy * 2 + half
            to = pl.ds(half * ROWS, ROWS)
            rows[yy, 0, to, :] = (acc[q_run] * share[pl.ds(q_run, 1), :]).T.astype(BF16)
            rows[yy, 1, to, :] = (grad[q_run] * SCALING).T.astype(BF16)

    def x_copy(kind, way, i, src):
        target = x_to[0] if way == 0 else x_to[2]
        return go(remote(src, xbuf.at[kind, way, i], xsend.at[kind, way, i], xrecv.at[kind, way, i], target))

    offsets = (AHEAD, BEHIND)
    sent = {}
    for side, offset in ((0, 1), (1, NZ - 1)):
        for lo in range(XLO):
            for part in (0, 1):
                nout[side, lo, part] = scaled(part, lo * NZ + (z + offset) % NZ).astype(BF16)
    for way in (0, 1):
        for i, offset in enumerate(offsets[way]):
            xout[0, way, i] = term(2, offset).astype(BF16)
    meet()
    near = []
    for lo in range(XLO):
        for side, offset in ((0, 1), (1, NZ - 1)):
            sems = nsend.at[side, lo], nrecv.at[side, lo]
            near.append(go(remote(nout.at[side, lo], nbuf.at[side, lo], *sems, z_to[offset])))
    for i in range(len(AHEAD)):
        for way in (0, 1):
            if i < len(offsets[way]):
                sent[0, way, i] = x_copy(0, way, i, xout.at[0, way, i])
    y_far, y_next, y_prev = (y + 2) % NY, (y + 1) % NY, (y + NY - 1) % NY
    put_rows(y_far)
    y_a = go(remote(rows.at[y_far, 0], ybuf.at[0], ysend.at[0], yrecv.at[0], y_up))
    y_b = go(remote(rows.at[y_far, 1], ybuf.at[1], ysend.at[1], yrecv.at[1], y_dn))
    for i in range(len(AHEAD)):
        for way in (0, 1):
            if i < len(offsets[1 - way]):
                xout[1, way, i] = term(1 if way == 0 else 3, offsets[1 - way][i]).astype(BF16)
                sent[1, way, i] = x_copy(1, way, i, xout.at[1, way, i])
    put_rows(y_next)
    put_rows(y_prev)
    y_c = go(remote(rows.at[y_next, 1], ybuf.at[2], ysend.at[2], yrecv.at[2], y_up))
    y_d = go(remote(rows.at[y_prev, 0], ybuf.at[3], ysend.at[3], yrecv.at[3], y_dn))
    for i in range(len(AHEAD)):
        for way in (0, 1):
            if i < len(offsets[way]):
                sent[0, way, i].wait_recv()
                own = term(1 if way == 0 else 3, offsets[way][i])
                xsum[way, i] = (xbuf[0, way, i].astype(F32) + own).astype(BF16)
                sent[2, way, i] = x_copy(2, way, i, xsum.at[way, i])
    for copy in near:
        copy.wait_recv()
    across = []
    for step in (2, 1, 3):
        oout[step - 1] = near_term(step).astype(BF16)
        sems = osend.at[step - 1], orecv.at[step - 1]
        across.append(go(remote(oout.at[step - 1], obuf.at[step - 1], *sems, x_to[step - 1])))
    z_copies = []
    for i in range(len(AHEAD)):
        for way in (0, 1):
            if i < len(offsets[way]):
                sent[2, way, i].wait_recv()
                sent[1, 1 - way, i].wait_recv()
                offset = offsets[way][i]
                slot = LATE.index(offset)
                block = term(0, offset) + xbuf[2, way, i].astype(F32) + xbuf[1, 1 - way, i].astype(F32)
                zsum[slot] = block.astype(BF16)
                sems = zsend.at[slot], zrecv.at[slot]
                z_copies.append(go(remote(zsum.at[slot], zbuf.at[slot], *sems, z_to[offset])))
    y_a.wait_recv()
    ysum[0] = (ybuf[0].astype(F32) + rows[y_next, 0].astype(F32)).astype(BF16)
    y_e = go(remote(ysum.at[0], ybuf.at[4], ysend.at[4], yrecv.at[4], y_up))
    y_b.wait_recv()
    ysum[1] = (ybuf[1].astype(F32) + rows[y_prev, 1].astype(F32)).astype(BF16)
    y_f = go(remote(ysum.at[1], ybuf.at[5], ysend.at[5], yrecv.at[5], y_dn))
    put_rows(y)
    total = near_term(0)
    for copy in across:
        copy.wait_recv()
    total = total + obuf[0].astype(F32) + obuf[1].astype(F32) + obuf[2].astype(F32)
    for copy in z_copies:
        copy.wait_recv()
    for slot in range(len(LATE)):
        total = total + zbuf[slot].astype(F32)
    last[0] = total.astype(BF16)
    final = go(remote(last.at[0], last.at[1], hsend, hrecv, x_to[1]))
    y_d.wait_recv()
    y_e.wait_recv()
    att[...] = (rows[y, 0].astype(F32) + ybuf[3].astype(F32) + ybuf[4].astype(F32)).astype(BF16)
    y_c.wait_recv()
    y_f.wait_recv()
    qgrad[...] = (rows[y, 1].astype(F32) + ybuf[2].astype(F32) + ybuf[5].astype(F32)).astype(BF16)
    final.wait_recv()
    mine, other = last[0], last[1]
    kgrad[...] = jnp.where(h == 0, mine, other)
    vgrad[...] = jnp.where(h == 0, other, mine)
    for copy in started:
        copy.wait_send()


def reduce(acc, share, grad, kv):
    vmem = pl.BlockSpec(memory_space=pltpu.VMEM)
    dma = pltpu.SemaphoreType.DMA
    block = (BLK, DH)
    late = len(LATE)
    return pl.pallas_call(
        reduce_kernel,
        out_shape=(
            jax.ShapeDtypeStruct((2 * ROWS, DH), BF16),
            jax.ShapeDtypeStruct((2 * ROWS, DH), BF16),
            jax.ShapeDtypeStruct(block, BF16),
            jax.ShapeDtypeStruct(block, BF16),
        ),
        in_specs=[vmem] * 4,
        out_specs=(vmem,) * 4,
        scratch_shapes=[
            pltpu.VMEM((NY, 2, 2 * ROWS, DH), BF16),
            pltpu.VMEM((6, 2 * ROWS, DH), BF16),
            pltpu.VMEM((2, 2 * ROWS, DH), BF16),
            pltpu.VMEM((2, XLO, 2) + block, BF16),
            pltpu.VMEM((2, XLO, 2) + block, BF16),
            pltpu.VMEM((3,) + block, BF16),
            pltpu.VMEM((3,) + block, BF16),
            pltpu.VMEM((2, 2, 3) + block, BF16),
            pltpu.VMEM((3, 2, 3) + block, BF16),
            pltpu.VMEM((2, 3) + block, BF16),
            pltpu.VMEM((late,) + block, BF16),
            pltpu.VMEM((late,) + block, BF16),
            pltpu.VMEM((2,) + block, BF16),
            dma((6,)), dma((6,)), dma((2, XLO)), dma((2, XLO)), dma((3,)), dma((3,)),
            dma((3, 2, 3)), dma((3, 2, 3)), dma((late,)), dma((late,)), dma, dma,
        ],
        compiler_params=pltpu.CompilerParams(collective_id=2, has_side_effects=True, vmem_limit_bytes=10 << 20),
        name="reduce_terms",
    )(acc, share, grad, kv)


def store_kernel(*refs):
    count = len(refs) // 2
    copies = [pltpu.make_async_copy(refs[i], refs[count + i], refs[-1].at[i]) for i in range(count)]
    for copy in copies:
        copy.start()
    for copy in copies:
        copy.wait()


def store(*arrays):
    return pl.pallas_call(
        store_kernel,
        out_shape=tuple(jax.ShapeDtypeStruct(a.shape, a.dtype) for a in arrays),
        in_specs=[pl.BlockSpec(memory_space=pltpu.VMEM)] * len(arrays),
        out_specs=(pl.BlockSpec(memory_space=pl.ANY),) * len(arrays),
        scratch_shapes=[pltpu.SemaphoreType.DMA((len(arrays),))],
        compiler_params=pltpu.CompilerParams(vmem_limit_bytes=1 << 20),
        name="store_outputs",
    )(*arrays)


def body(queries, key_rows, value_rows, out_grad, doc_lengths, balance):
    flat = (2 * ROWS, DH)
    bal = balance.reshape(SPANS // 2, BLK)
    qg, kg, tab, row_tab = gather(
        queries.reshape(flat),
        out_grad.reshape(flat),
        key_rows.reshape(2, RUN, DH),
        value_rows.reshape(2, RUN, DH),
        bal,
        doc_lengths,
    )
    part, part_acc, more, more_gw = forward(tab, row_tab, qg, kg)
    stats, acc, held, held_gw = exchange(tab, row_tab, qg, kg, part, part_acc)
    share, grad, kv = backward(tab, qg, kg, stats, held, held_gw, more, more_gw)
    kv = kv.reshape(2, XLO * NZ, BLK, DH)
    attended, query_grad, key_grad, value_grad = store(*reduce(acc, share, grad, kv))
    return attended.reshape(queries.shape), query_grad.reshape(queries.shape), key_grad, value_grad


def solution(mesh):
    return jax.shard_map(
        body,
        mesh=mesh,
        in_specs=(
            P(("seq", "ctx"), "head", None),
            P(("seq", "ctx"), None),
            P(("seq", "ctx"), None),
            P(("seq", "ctx"), "head", None),
            P("seq"),
            P("seq"),
        ),
        out_specs=(
            P(("seq", "ctx"), "head", None),
            P(("seq", "ctx"), "head", None),
            P(("seq", "ctx"), None),
            P(("seq", "ctx"), None),
        ),
        check_vma=False,
    )
```

```python
import functools
import math

import jax
import jax.numpy as jnp
from jax import lax
from jax.experimental import pallas as pl
from jax.experimental.pallas import tpu as pltpu
from jax.sharding import PartitionSpec as P

NX, NY, NZ = 4, 4, 8
XLO = 2
RUN = 64
DH = 128
HEADS_HERE = 4
ROWS = RUN * HEADS_HERE
BLK = 2 * RUN
KRUNS = XLO * NZ * 2
QRUNS = NY * 2
TILE = 4
SPANS = 128
ITEMS = QRUNS * (KRUNS // TILE - 1)
UNROLL = 4
DOCS = 8
NEGATIVE = -1e30
FLOOR = -1e29
FAR = 1 << 20
SCALING = 1.0 / math.sqrt(DH)
LOG2E = 1.0 / math.log(2.0)
MESH = pl.DeviceIdType.MESH
F32 = jnp.float32
BF16 = jnp.bfloat16


def here():
    c = lax.axis_index("ctx")
    h = lax.axis_index("head")
    return h, c // (NY * NZ), (c // NZ) % NY, c % NZ


def device(x, y, z):
    return {"ctx": ((x % XLO) * NY + y) * NZ + z, "head": x // XLO}


def greet(targets):
    barrier = pltpu.get_barrier_semaphore()
    for target in targets:
        pl.semaphore_signal(barrier, inc=1, device_id=target, device_id_type=MESH)
    return lambda: pl.semaphore_wait(barrier, len(targets))


def remote(src, dst, send, recv, target):
    return pltpu.make_async_remote_copy(
        src_ref=src, dst_ref=dst, send_sem=send, recv_sem=recv, device_id=target, device_id_type=MESH
    )


def tables(bal, lengths, tab, row_tab, xl, y, z):
    lane = lax.broadcasted_iota(jnp.int32, (1, SPANS), 1)
    slabs = [bal[pl.ds(pl.multiple_of((i * NY + y) * NZ, NZ), NZ), :] for i in range(XLO)]
    held = [slab[:, half * RUN : half * RUN + 1] // RUN for half in (0, 1) for slab in slabs]
    held = jnp.concatenate(held, axis=0)
    index = lax.broadcasted_iota(jnp.int32, (KRUNS, 1), 0)
    match = held == lane
    has = jnp.sum(jnp.where(match, 1, 0), axis=0, keepdims=True)
    which = jnp.sum(jnp.where(match, index, 0), axis=0, keepdims=True)
    before = jnp.sum(jnp.where(held < lane, 1, 0), axis=0, keepdims=True)
    rank = jnp.where(has > 0, before, -1)
    hit = jnp.where(rank == lax.broadcasted_iota(jnp.int32, (SPANS, 1), 0), 1.0, 0.0).astype(BF16)
    row = lax.broadcasted_iota(jnp.int32, (8, 1), 0)
    block, half = which % (XLO * NZ), which // (XLO * NZ)
    found = jnp.where(row == 0, lane, jnp.where(row == 1, block, jnp.where(row == 6, half, 0)))
    found = found.astype(F32).astype(BF16)
    sorted_runs = lax.dot_general(found, hit, (((1,), (1,)), ((), ())), preferred_element_type=F32)
    sorted_runs = jnp.where((row == 0) & (lane >= KRUNS), F32(FAR // RUN), sorted_runs).astype(jnp.int32)
    q_rows = [bal[pl.ds((xl * NY + i) * NZ + z, 1), :] for i in range(NY)]
    low = jnp.concatenate([r[:, half * RUN : half * RUN + 1] for r in q_rows for half in (0, 1)], axis=0)
    pos = low + lax.broadcasted_iota(jnp.int32, (QRUNS, ROWS), 1) // HEADS_HERE
    start = jnp.zeros((QRUNS, ROWS), jnp.int32)
    first = jnp.zeros((QRUNS, 1), jnp.int32)
    end = 0
    for d in range(DOCS):
        end = end + lengths[d]
        first = jnp.where(low >= end, end, first)
        start = jnp.where(pos >= end, end, start)
    row_tab[0] = pos
    row_tab[1] = start
    low_run = jnp.sum(jnp.where((lane < first // RUN) & (has > 0), 1, 0), axis=1, keepdims=True)
    high_run = jnp.sum(jnp.where((lane <= low // RUN) & (has > 0), 1, 0), axis=1, keepdims=True)
    tiles = jnp.maximum((high_run - low_run + TILE - 1) // TILE, 1)
    own_lane = lax.broadcasted_iota(jnp.int32, (QRUNS, 1), 0) == lane
    low_row = jnp.sum(jnp.where(own_lane, low_run, 0), axis=0, keepdims=True)
    more = tiles - 1
    upper = lax.broadcasted_iota(jnp.int32, (QRUNS, 1), 0) >= lax.broadcasted_iota(jnp.int32, (1, SPANS), 1)
    more_row = jnp.sum(jnp.where(own_lane, more, 0), axis=0, keepdims=True)
    ends = jnp.sum(jnp.where(upper, more_row, 0), axis=1, keepdims=True)
    passed = lane >= ends
    run_row = jnp.minimum(jnp.sum(jnp.where(passed, 1, 0), axis=0, keepdims=True), QRUNS - 1)
    tile_row = lane + 1 - jnp.sum(jnp.where(passed, more, 0), axis=0, keepdims=True)
    count = jnp.sum(more, axis=0, keepdims=True)
    tile_row = jnp.where(lane >= count, KRUNS // TILE, tile_row)
    values = [None, None, low_row, run_row, tile_row, jnp.where(lane == 0, count, 0)]
    out = sorted_runs
    for i in range(2, 6):
        out = jnp.where(row == i, values[i], out)
    tab[...] = out


def gather_kernel(
    q_ref, g_ref, k_ref, v_ref, bal_ref, len_ref, qg, kg, tab, row_tab, zeros_acc, zeros_grad, zeros_kv, bal, lengths, lsem, ysend, yrecv, zsend, zrecv, xsend, xrecv
):
    h, xl, y, z = here()
    x = h * XLO + xl
    first = xl * NZ
    y_up, y_dn = device(x, (y + 1) % NY, z), device(x, (y + NY - 1) % NY, z)
    z_to = {d: device(x, y, (z + d + NZ) % NZ) for d in (1, 2, -1, -2)}
    x_up, x_dn = device((x + 1) % NX, y, z), device((x + NX - 1) % NX, y, z)
    meet = greet([y_up, y_dn, x_up, x_dn] + list(z_to.values()))
    kv = (k_ref, v_ref)
    started = []

    def go(copy):
        copy.start()
        started.append(copy)
        return copy

    sent_z = {}

    def z_send(sign, hops, dist, part):
        block = (z - sign * (dist - hops) + NZ) % NZ
        dst = kg.at[first + block, part]
        src = kv[part] if dist == hops else dst
        way = 0 if sign > 0 else 1
        sems = zsend.at[way, dist - 1, part], zrecv.at[way, dist - 1, part]
        sent_z[sign, dist, part] = go(remote(src, dst, *sems, z_to[sign * hops]))

    sent_x = []

    def x_send(slot, block):
        dst = kg.at[first + block, h]
        for side, target in ((0, x_up), (1, x_dn)):
            sent_x.append(go(remote(dst, dst, xsend.at[side, slot], xrecv.at[side, slot], target)))

    def local(src, dst, slot):
        copy = pltpu.make_async_copy(src, dst, lsem.at[slot])
        copy.start()
        return copy

    own_kv = [local(kv[part], kg.at[first + z, part], part) for part in (0, 1)]
    own_tab = [local(bal_ref, bal, 4), local(len_ref, lengths, 5)]
    meet()
    for part in (0, 1):
        for sign in (1, -1):
            z_send(sign, 2, 2, part)
    y_q_up = go(remote(q_ref, qg.at[y, 0], ysend.at[0], yrecv.at[0], y_up))
    y_g_dn = go(remote(g_ref, qg.at[y, 1], ysend.at[2], yrecv.at[2], y_dn))
    for part in (0, 1):
        for sign in (1, -1):
            z_send(sign, 1, 1, part)
    y_g_up = go(remote(g_ref, qg.at[y, 1], ysend.at[1], yrecv.at[1], y_up))
    y_q_dn = go(remote(q_ref, qg.at[y, 0], ysend.at[3], yrecv.at[3], y_dn))
    own_q = [local(ref, qg.at[y, part], 2 + part) for part, ref in ((0, q_ref), (1, g_ref))]
    for copy in own_kv:
        copy.wait()
    x_send(0, z)
    for copy in own_tab:
        copy.wait()
    tables(bal, lengths, tab, row_tab, xl, y, z)
    for ref in (zeros_acc, zeros_grad, zeros_kv):
        ref[...] = jnp.zeros_like(ref)
    for part in (0, 1):
        for sign in (1, -1):
            sent_z[sign, 2, part].wait_recv()
            z_send(sign, 1, 3, part)
            if part == (0 if sign > 0 else 1):
                z_send(sign, 2, 4, part)
    x_send(1, (z - 2 + NZ) % NZ)
    x_send(2, (z + 2) % NZ)
    y_q_up.wait_recv()
    q_on = qg.at[(y + NY - 1) % NY, 0]
    y_fwd_up = go(remote(q_on, q_on, ysend.at[4], yrecv.at[4], y_up))
    y_g_dn.wait_recv()
    g_on = qg.at[(y + 1) % NY, 1]
    y_fwd_dn = go(remote(g_on, g_on, ysend.at[5], yrecv.at[5], y_dn))
    slot = 3
    for dist in (1, 3):
        for sign in (1, -1):
            for part in (0, 1):
                sent_z[sign, dist, part].wait_recv()
            x_send(slot, (z - sign * dist + NZ) % NZ)
            slot += 1
    sent_z[1, 4, 0].wait_recv()
    sent_z[-1, 4, 1].wait_recv()
    x_send(7, (z + NZ // 2) % NZ)
    for copy in (y_g_up, y_q_dn, y_fwd_up, y_fwd_dn):
        copy.wait_recv()
    for copy in sent_x:
        copy.wait_recv()
    for copy in started:
        copy.wait_send()
    for copy in own_q:
        copy.wait()


ZEROS = (
    jax.ShapeDtypeStruct((QRUNS, DH, ROWS), F32),
    jax.ShapeDtypeStruct((QRUNS, DH, ROWS), F32),
    jax.ShapeDtypeStruct((2, XLO * NZ, 2, RUN, DH), F32),
)


def gather(q, g, k, v, bal, lengths):
    hbm = pl.BlockSpec(memory_space=pltpu.HBM)
    vmem = pl.BlockSpec(memory_space=pltpu.VMEM)
    dma = pltpu.SemaphoreType.DMA
    return pl.pallas_call(
        gather_kernel,
        out_shape=(
            jax.ShapeDtypeStruct((NY, 2, 2 * ROWS, DH), BF16),
            jax.ShapeDtypeStruct((XLO * NZ, 2, 2, RUN, DH), BF16),
            jax.ShapeDtypeStruct((8, SPANS), jnp.int32),
            jax.ShapeDtypeStruct((2, QRUNS, ROWS), jnp.int32),
            *ZEROS,
        ),
        in_specs=[hbm] * 6,
        out_specs=(vmem,) * 7,
        scratch_shapes=[
            pltpu.VMEM((SPANS // 2, BLK), jnp.int32),
            pltpu.SMEM((DOCS,), jnp.int32),
            dma((6,)), dma((6,)), dma((6,)), dma((2, 4, 2)), dma((2, 4, 2)), dma((2, 8)), dma((2, 8)),
        ],
        compiler_params=pltpu.CompilerParams(collective_id=0, has_side_effects=True, vmem_limit_bytes=8 << 20),
        name="gather_rows",
    )(*(pltpu.with_memory_space_constraint(a, pltpu.HBM) for a in (q, g, k, v, bal, lengths)))


def tile_runs(tab, low_run, t):
    runs = [low_run + t * TILE + u for u in range(TILE)]
    return [(tab[1, r], tab[6, r]) for r in runs], [tab[0, r] * RUN for r in runs]


def tile_rows(kg, indices, part):
    return jnp.concatenate([kg[block, part, half] for block, half in indices], axis=0)


def masked_scores(k, q, places, pos, start):
    scores = lax.dot_general(k, q, (((1,), (1,)), ((), ())), preferred_element_type=F32)
    offset = lax.broadcasted_iota(jnp.int32, (RUN, ROWS), 0)
    parts = []
    for u, base in enumerate(places):
        seen = (offset <= pos - base) & (offset >= start - base)
        parts.append(jnp.where(seen, scores[u * RUN : (u + 1) * RUN] * (SCALING * LOG2E), NEGATIVE))
    return jnp.concatenate(parts, axis=0)


def together(process, items):
    for end in [process(*item) for item in items]:
        end()


def first_tiles(process):
    def step(i, _):
        together(process, [(UNROLL * i + u, 0, UNROLL * i + u) for u in range(UNROLL)])
        return 0

    lax.fori_loop(0, QRUNS // UNROLL, step, 0)


def further_tiles(tab, process):
    def step(i, _):
        slots = [UNROLL * i + u for u in range(UNROLL)]
        together(process, [(tab[3, slot], tab[4, slot], slot) for slot in slots])
        return 0

    lax.fori_loop(0, (tab[5, 0] + UNROLL - 1) // UNROLL, step, 0)


def query_rows(qg, q_run, part):
    return qg[q_run // 2, part, pl.ds(pl.multiple_of((q_run % 2) * ROWS, ROWS), ROWS), :]


def forward_tile(tab, row_tab, qg, kg, held, held_gw, combine):
    def process(q_run, t, slot):
        at = pl.ds(q_run, 1)
        indices, places = tile_runs(tab, tab[2, q_run], t)
        s = masked_scores(
            tile_rows(kg, indices, 0), query_rows(qg, q_run, 0), places, row_tab[0, at, :], row_tab[1, at, :]
        )
        held[slot] = s
        v = tile_rows(kg, indices, 1)
        gw = lax.dot_general(
            v, query_rows(qg, q_run, 1), (((1,), (1,)), ((), ())), preferred_element_type=F32
        )
        held_gw[slot] = gw
        top = jnp.maximum(jnp.max(s, axis=0, keepdims=True), FLOOR)
        raw = jnp.exp2(s - top)
        total = jnp.sum(raw, axis=0, keepdims=True)
        inner = jnp.sum(raw * gw, axis=0, keepdims=True)
        acc = lax.dot_general(v, raw.astype(BF16), (((0,), (0,)), ((), ())), preferred_element_type=F32)
        return lambda: combine(q_run, top, total, inner, acc)

    return process


def combined(old, old_acc, top, total, inner, acc):
    new_top = jnp.maximum(old[0], top)
    old_share, share = jnp.exp2(old[0] - new_top), jnp.exp2(top - new_top)
    stats = new_top, old[1] * old_share + total * share, old[2] * old_share + inner * share
    return stats, old_acc * old_share + acc * share


def forward_kernel(tab, row_tab, qg, kg, zeros, stats, out, held, held_gw):
    stats[0] = jnp.full((QRUNS, ROWS), FLOOR, F32)
    stats[1] = jnp.zeros((QRUNS, ROWS), F32)
    stats[2] = jnp.zeros((QRUNS, ROWS), F32)

    def combine(q_run, *new):
        at = pl.ds(q_run, 1)
        rows, out[q_run] = combined([stats[i, at, :] for i in range(3)], out[q_run], *new)
        for i in range(3):
            stats[i, at, :] = rows[i]

    further_tiles(tab, forward_tile(tab, row_tab, qg, kg, held, held_gw, combine))


def forward(tab, row_tab, qg, kg, zeros):
    smem = pl.BlockSpec(memory_space=pltpu.SMEM)
    vmem = pl.BlockSpec(memory_space=pltpu.VMEM)
    return pl.pallas_call(
        forward_kernel,
        out_shape=(
            jax.ShapeDtypeStruct((3, QRUNS, ROWS), F32),
            jax.ShapeDtypeStruct((QRUNS, DH, ROWS), F32),
            jax.ShapeDtypeStruct((ITEMS, TILE * RUN, ROWS), F32),
            jax.ShapeDtypeStruct((ITEMS, TILE * RUN, ROWS), F32),
        ),
        in_specs=[smem] + [vmem] * 4,
        out_specs=(vmem,) * 4,
        input_output_aliases={4: 1},
        compiler_params=pltpu.CompilerParams(vmem_limit_bytes=8 << 20),
        name="forward_stats",
    )(tab, row_tab, qg, kg, zeros)


def exchange_kernel(tab, row_tab, qg, kg, part, part_acc, out, acc_out, held, held_gw, mine, lsem, send, recv):
    h, xl, y, z = here()
    x = h * XLO + xl
    targets = [device(x, (y + d) % NY, z) for d in range(1, NY)]
    meet = greet(targets)

    def combine(q_run, *new):
        at = pl.ds(q_run, 1)
        rows, acc_out[q_run] = combined([part[i, at, :] for i in range(3)], part_acc[q_run], *new)
        for i in range(3):
            mine[i, at, :] = rows[i]

    first_tiles(forward_tile(tab, row_tab, qg, kg, held, held_gw, combine))
    meet()
    copies = []
    for d, target in enumerate(targets):
        copy = remote(mine, out.at[y], send.at[d], recv.at[d], target)
        copy.start()
        copies.append(copy)
    own = pltpu.make_async_copy(mine, out.at[y], lsem)
    own.start()
    own.wait()
    for copy in copies:
        copy.wait()


def exchange(tab, row_tab, qg, kg, part, part_acc):
    smem = pl.BlockSpec(memory_space=pltpu.SMEM)
    vmem = pl.BlockSpec(memory_space=pltpu.VMEM)
    dma = pltpu.SemaphoreType.DMA
    return pl.pallas_call(
        exchange_kernel,
        out_shape=(
            jax.ShapeDtypeStruct((NY,) + part.shape, F32),
            jax.ShapeDtypeStruct(part_acc.shape, F32),
            jax.ShapeDtypeStruct((QRUNS, TILE * RUN, ROWS), F32),
            jax.ShapeDtypeStruct((QRUNS, TILE * RUN, ROWS), F32),
        ),
        in_specs=[smem] + [vmem] * 5,
        out_specs=(vmem,) * 4,
        scratch_shapes=[pltpu.VMEM(part.shape, F32), dma, dma((NY - 1,)), dma((NY - 1,))],
        compiler_params=pltpu.CompilerParams(collective_id=1, has_side_effects=True, vmem_limit_bytes=8 << 20),
        name="exchange_stats",
    )(tab, row_tab, qg, kg, part, part_acc)


def backward_kernel(
    tab, qg, kg, stats, held, held_gw, more, more_gw, zeros_grad, zeros_kv, share_out, grad_acc, kv_acc, row_stats
):
    y = here()[2]
    top = jnp.maximum(jnp.maximum(stats[0, 0], stats[1, 0]), jnp.maximum(stats[2, 0], stats[3, 0]))
    shares = [jnp.exp2(stats[i, 0] - top) for i in range(NY)]
    total = sum(stats[i, 1] * shares[i] for i in range(NY))
    log_total = top + jnp.log(total) * LOG2E
    row_stats[0] = log_total
    row_stats[1] = sum(stats[i, 2] * shares[i] for i in range(NY)) / total
    share_out[...] = jnp.exp2(stats[y, 0] - log_total)

    def process(held, held_gw, q_run, t, slot):
        at = pl.ds(q_run, 1)
        indices, _ = tile_runs(tab, tab[2, q_run], t)
        weights = jnp.exp2(held[slot] - row_stats[0, at, :])
        gs = (weights * (held_gw[slot] - row_stats[1, at, :])).astype(BF16)
        value_part = jnp.dot(weights.astype(BF16), query_rows(qg, q_run, 1), preferred_element_type=F32)
        key_part = jnp.dot(gs, query_rows(qg, q_run, 0), preferred_element_type=F32)
        grad = lax.dot_general(
            tile_rows(kg, indices, 0), gs, (((0,), (0,)), ((), ())), preferred_element_type=F32
        )

        def end():
            for u, (block, half) in enumerate(indices):
                kv_acc[1, block, half] += value_part[u * RUN : (u + 1) * RUN]
                kv_acc[0, block, half] += key_part[u * RUN : (u + 1) * RUN]
            grad_acc[q_run] += grad

        return end

    first_tiles(functools.partial(process, held, held_gw))
    further_tiles(tab, functools.partial(process, more, more_gw))


def backward(tab, qg, kg, stats, held, held_gw, more, more_gw, zeros_grad, zeros_kv):
    smem = pl.BlockSpec(memory_space=pltpu.SMEM)
    vmem = pl.BlockSpec(memory_space=pltpu.VMEM)
    return pl.pallas_call(
        backward_kernel,
        out_shape=(
            jax.ShapeDtypeStruct((QRUNS, ROWS), F32),
            jax.ShapeDtypeStruct((QRUNS, DH, ROWS), F32),
            jax.ShapeDtypeStruct((2, XLO * NZ, 2, RUN, DH), F32),
        ),
        in_specs=[smem] + [vmem] * 9,
        out_specs=(vmem,) * 3,
        input_output_aliases={8: 1, 9: 2},
        scratch_shapes=[pltpu.VMEM((2, QRUNS, ROWS), F32)],
        compiler_params=pltpu.CompilerParams(vmem_limit_bytes=8 << 20),
        name="backward_terms",
    )(tab, qg, kg, stats, held, held_gw, more, more_gw, zeros_grad, zeros_kv)


AHEAD = (4, 3, 2)
BEHIND = (5, 6)
LATE = AHEAD + BEHIND


def reduce_kernel(
    acc, share, grad, kv, att, qgrad, kgrad, vgrad,
    rows, ybuf, ysum, nout, nbuf, oout, obuf, xout, xbuf, xsum, zsum, zbuf, last,
    ysend, yrecv, nsend, nrecv, osend, orecv, xsend, xrecv, zsend, zrecv, hsend, hrecv, z_word, x_word, z_far_word,
):
    h, xl, y, z = here()
    x = h * XLO + xl
    y_up, y_dn = device(x, (y + 1) % NY, z), device(x, (y + NY - 1) % NY, z)
    x_to = tuple(device((x + d) % NX, y, z) for d in (1, 2, 3))
    z_to = {d: device(x, y, (z + d) % NZ) for d in range(1, NZ)}
    z_near = ((0, z_to[1]), (1, z_to[NZ - 1]))
    x_near = ((0, x_to[0]), (1, x_to[2]))
    meet = greet([z_to[1], z_to[NZ - 1], x_to[0], x_to[2], y_up, y_dn])

    def tell(sem, targets):
        for side, target in targets:
            pl.semaphore_signal(sem.at[side], inc=1, device_id=target, device_id_type=MESH)

    def hear(sem):
        for side in (0, 1):
            pl.semaphore_wait(sem.at[side], 1)

    started = []

    def go(copy):
        copy.start()
        started.append(copy)
        return copy

    def scaled(part, block):
        return kv[part, block] * jnp.where(part == 0, F32(SCALING), F32(1.0))

    def term(step, offset):
        ring = (x + step) % NX
        return scaled(ring // XLO, (ring % XLO) * NZ + (z + offset) % NZ)

    def near_term(step):
        ring = (x + step) % NX
        sides = [nbuf[side, ring % XLO, ring // XLO].astype(F32) for side in (0, 1)]
        return term(step, 0) + sides[0] + sides[1]

    def put_rows(yy):
        for half in (0, 1):
            q_run = yy * 2 + half
            to = pl.ds(half * ROWS, ROWS)
            rows[yy, 0, to, :] = (acc[q_run] * share[pl.ds(q_run, 1), :]).T.astype(BF16)
            rows[yy, 1, to, :] = (grad[q_run] * SCALING).T.astype(BF16)

    def x_copy(kind, way, i, src):
        target = x_to[0] if way == 0 else x_to[2]
        return go(remote(src, xbuf.at[kind, way, i], xsend.at[kind, way, i], xrecv.at[kind, way, i], target))

    offsets = (AHEAD, BEHIND)
    sent = {}
    for side, offset in ((0, 1), (1, NZ - 1)):
        for lo in range(XLO):
            for part in (0, 1):
                nout[side, lo, part] = scaled(part, lo * NZ + (z + offset) % NZ).astype(BF16)
    for way in (0, 1):
        for i, offset in enumerate(offsets[way]):
            xout[0, way, i] = term(2, offset).astype(BF16)
    meet()
    tell(z_word, z_near)
    tell(x_word, x_near)
    near = []
    for lo in range(XLO):
        for side, offset in ((0, 1), (1, NZ - 1)):
            sems = nsend.at[side, lo], nrecv.at[side, lo]
            near.append(go(remote(nout.at[side, lo], nbuf.at[side, lo], *sems, z_to[offset])))
    for i in range(len(AHEAD)):
        for way in (0, 1):
            if i < len(offsets[way]):
                sent[0, way, i] = x_copy(0, way, i, xout.at[0, way, i])
    for i in range(len(AHEAD)):
        for way in (0, 1):
            if i < len(offsets[1 - way]):
                xout[1, way, i] = term(1 if way == 0 else 3, offsets[1 - way][i]).astype(BF16)
                sent[1, way, i] = x_copy(1, way, i, xout.at[1, way, i])
    y_far, y_next, y_prev = (y + 2) % NY, (y + 1) % NY, (y + NY - 1) % NY
    put_rows(y_far)
    y_a = go(remote(rows.at[y_far, 0], ybuf.at[0], ysend.at[0], yrecv.at[0], y_up))
    y_b = go(remote(rows.at[y_far, 1], ybuf.at[1], ysend.at[1], yrecv.at[1], y_dn))
    hear(z_word)
    tell(z_far_word, ((0, z_to[2]), (1, z_to[NZ - 2])))
    for i in range(len(AHEAD)):
        for way in (0, 1):
            if i < len(offsets[way]):
                sent[0, way, i].wait_recv()
                own = term(1 if way == 0 else 3, offsets[way][i])
                xsum[way, i] = (xbuf[0, way, i].astype(F32) + own).astype(BF16)
                sent[2, way, i] = x_copy(2, way, i, xsum.at[way, i])
    for copy in near:
        copy.wait_recv()
    hear(x_word)
    across = []
    for step in (2, 1, 3):
        oout[step - 1] = near_term(step).astype(BF16)
        sems = osend.at[step - 1], orecv.at[step - 1]
        across.append(go(remote(oout.at[step - 1], obuf.at[step - 1], *sems, x_to[step - 1])))
    put_rows(y_next)
    put_rows(y_prev)
    y_c = go(remote(rows.at[y_next, 1], ybuf.at[2], ysend.at[2], yrecv.at[2], y_up))
    y_d = go(remote(rows.at[y_prev, 0], ybuf.at[3], ysend.at[3], yrecv.at[3], y_dn))
    z_copies = []
    hear(z_far_word)
    for i in range(len(AHEAD)):
        for way in (0, 1):
            if i < len(offsets[way]):
                sent[2, way, i].wait_recv()
                sent[1, 1 - way, i].wait_recv()
                offset = offsets[way][i]
                slot = LATE.index(offset)
                block = term(0, offset) + xbuf[2, way, i].astype(F32) + xbuf[1, 1 - way, i].astype(F32)
                zsum[slot] = block.astype(BF16)
                sems = zsend.at[slot], zrecv.at[slot]
                z_copies.append(go(remote(zsum.at[slot], zbuf.at[slot], *sems, z_to[offset])))
    y_a.wait_recv()
    ysum[0] = (ybuf[0].astype(F32) + rows[y_next, 0].astype(F32)).astype(BF16)
    y_e = go(remote(ysum.at[0], ybuf.at[4], ysend.at[4], yrecv.at[4], y_up))
    y_b.wait_recv()
    ysum[1] = (ybuf[1].astype(F32) + rows[y_prev, 1].astype(F32)).astype(BF16)
    y_f = go(remote(ysum.at[1], ybuf.at[5], ysend.at[5], yrecv.at[5], y_dn))
    put_rows(y)
    total = near_term(0)
    for copy in across:
        copy.wait_recv()
    total = total + obuf[0].astype(F32) + obuf[1].astype(F32) + obuf[2].astype(F32)
    for copy in z_copies:
        copy.wait_recv()
    for slot in range(len(LATE)):
        total = total + zbuf[slot].astype(F32)
    last[0] = total.astype(BF16)
    final = go(remote(last.at[0], last.at[1], hsend, hrecv, x_to[1]))
    y_d.wait_recv()
    y_e.wait_recv()
    att[...] = (rows[y, 0].astype(F32) + ybuf[3].astype(F32) + ybuf[4].astype(F32)).astype(BF16)
    y_c.wait_recv()
    y_f.wait_recv()
    qgrad[...] = (rows[y, 1].astype(F32) + ybuf[2].astype(F32) + ybuf[5].astype(F32)).astype(BF16)
    final.wait_recv()
    mine, other = last[0], last[1]
    kgrad[...] = jnp.where(h == 0, mine, other)
    vgrad[...] = jnp.where(h == 0, other, mine)
    for copy in started:
        copy.wait_send()


def reduce(acc, share, grad, kv):
    vmem = pl.BlockSpec(memory_space=pltpu.VMEM)
    dma = pltpu.SemaphoreType.DMA
    block = (BLK, DH)
    late = len(LATE)
    word = pltpu.SemaphoreType.REGULAR((2,))
    return pl.pallas_call(
        reduce_kernel,
        out_shape=(
            jax.ShapeDtypeStruct((2 * ROWS, DH), BF16),
            jax.ShapeDtypeStruct((2 * ROWS, DH), BF16),
            jax.ShapeDtypeStruct(block, BF16),
            jax.ShapeDtypeStruct(block, BF16),
        ),
        in_specs=[vmem] * 4,
        out_specs=(vmem,) * 4,
        scratch_shapes=[
            pltpu.VMEM((NY, 2, 2 * ROWS, DH), BF16),
            pltpu.VMEM((6, 2 * ROWS, DH), BF16),
            pltpu.VMEM((2, 2 * ROWS, DH), BF16),
            pltpu.VMEM((2, XLO, 2) + block, BF16),
            pltpu.VMEM((2, XLO, 2) + block, BF16),
            pltpu.VMEM((3,) + block, BF16),
            pltpu.VMEM((3,) + block, BF16),
            pltpu.VMEM((2, 2, 3) + block, BF16),
            pltpu.VMEM((3, 2, 3) + block, BF16),
            pltpu.VMEM((2, 3) + block, BF16),
            pltpu.VMEM((late,) + block, BF16),
            pltpu.VMEM((late,) + block, BF16),
            pltpu.VMEM((2,) + block, BF16),
            dma((6,)), dma((6,)), dma((2, XLO)), dma((2, XLO)), dma((3,)), dma((3,)),
            dma((3, 2, 3)), dma((3, 2, 3)), dma((late,)), dma((late,)), dma, dma, word, word, word,
        ],
        compiler_params=pltpu.CompilerParams(collective_id=2, has_side_effects=True, vmem_limit_bytes=10 << 20),
        name="reduce_terms",
    )(acc, share, grad, kv)


def store_kernel(*refs):
    count = len(refs) // 2
    copies = [pltpu.make_async_copy(refs[i], refs[count + i], refs[-1].at[i]) for i in range(count)]
    for copy in copies:
        copy.start()
    for copy in copies:
        copy.wait()


def store(*arrays):
    return pl.pallas_call(
        store_kernel,
        out_shape=tuple(jax.ShapeDtypeStruct(a.shape, a.dtype) for a in arrays),
        in_specs=[pl.BlockSpec(memory_space=pltpu.VMEM)] * len(arrays),
        out_specs=(pl.BlockSpec(memory_space=pl.ANY),) * len(arrays),
        scratch_shapes=[pltpu.SemaphoreType.DMA((len(arrays),))],
        compiler_params=pltpu.CompilerParams(vmem_limit_bytes=1 << 20),
        name="store_outputs",
    )(*arrays)


def body(queries, key_rows, value_rows, out_grad, doc_lengths, balance):
    flat = (2 * ROWS, DH)
    bal = balance.reshape(SPANS // 2, BLK)
    qg, kg, tab, row_tab, zeros_acc, zeros_grad, zeros_kv = gather(
        queries.reshape(flat),
        out_grad.reshape(flat),
        key_rows.reshape(2, RUN, DH),
        value_rows.reshape(2, RUN, DH),
        bal,
        doc_lengths,
    )
    part, part_acc, more, more_gw = forward(tab, row_tab, qg, kg, zeros_acc)
    stats, acc, held, held_gw = exchange(tab, row_tab, qg, kg, part, part_acc)
    share, grad, kv = backward(
        tab, qg, kg, stats, held, held_gw, more, more_gw, zeros_grad, zeros_kv
    )
    kv = kv.reshape(2, XLO * NZ, BLK, DH)
    attended, query_grad, key_grad, value_grad = store(*reduce(acc, share, grad, kv))
    return attended.reshape(queries.shape), query_grad.reshape(queries.shape), key_grad, value_grad


def solution(mesh):
    return jax.shard_map(
        body,
        mesh=mesh,
        in_specs=(
            P(("seq", "ctx"), "head", None),
            P(("seq", "ctx"), None),
            P(("seq", "ctx"), None),
            P(("seq", "ctx"), "head", None),
            P("seq"),
            P("seq"),
        ),
        out_specs=(
            P(("seq", "ctx"), "head", None),
            P(("seq", "ctx"), "head", None),
            P(("seq", "ctx"), None),
            P(("seq", "ctx"), None),
        ),
        check_vma=False,
    )
```

```python
import functools
import math

import jax
import jax.numpy as jnp
from jax import lax
from jax.experimental import pallas as pl
from jax.experimental.pallas import tpu as pltpu
from jax.sharding import PartitionSpec as P

NX, NY, NZ = 4, 4, 8
XLO = 2
RUN = 64
DH = 128
HEADS_HERE = 4
ROWS = RUN * HEADS_HERE
BLK = 2 * RUN
KRUNS = XLO * NZ * 2
QRUNS = NY * 2
TILE = 4
SPANS = 128
ITEMS = QRUNS * (KRUNS // TILE - 1)
DOCS = 8
NEGATIVE = -1e30
FLOOR = -1e29
FAR = 1 << 20
SCALING = 1.0 / math.sqrt(DH)
LOG2E = 1.0 / math.log(2.0)
MESH = pl.DeviceIdType.MESH
F32 = jnp.float32
BF16 = jnp.bfloat16


def here():
    c = lax.axis_index("ctx")
    h = lax.axis_index("head")
    return h, c // (NY * NZ), (c // NZ) % NY, c % NZ


def device(x, y, z):
    return {"ctx": ((x % XLO) * NY + y) * NZ + z, "head": x // XLO}


def greet(targets):
    barrier = pltpu.get_barrier_semaphore()
    for target in targets:
        pl.semaphore_signal(barrier, inc=1, device_id=target, device_id_type=MESH)
    return lambda: pl.semaphore_wait(barrier, len(targets))


def remote(src, dst, send, recv, target):
    return pltpu.make_async_remote_copy(
        src_ref=src, dst_ref=dst, send_sem=send, recv_sem=recv, device_id=target, device_id_type=MESH
    )


def tables(bal, lengths, tab, row_tab, xl, y, z):
    lane = lax.broadcasted_iota(jnp.int32, (1, SPANS), 1)
    slabs = [bal[pl.ds(pl.multiple_of((i * NY + y) * NZ, NZ), NZ), :] for i in range(XLO)]
    held = [slab[:, half * RUN : half * RUN + 1] // RUN for half in (0, 1) for slab in slabs]
    held = jnp.concatenate(held, axis=0)
    index = lax.broadcasted_iota(jnp.int32, (KRUNS, 1), 0)
    match = held == lane
    has = jnp.sum(jnp.where(match, 1, 0), axis=0, keepdims=True)
    which = jnp.sum(jnp.where(match, index, 0), axis=0, keepdims=True)
    before = jnp.sum(jnp.where(held < lane, 1, 0), axis=0, keepdims=True)
    rank = jnp.where(has > 0, before, -1)
    hit = jnp.where(rank == lax.broadcasted_iota(jnp.int32, (SPANS, 1), 0), 1.0, 0.0).astype(BF16)
    row = lax.broadcasted_iota(jnp.int32, (8, 1), 0)
    block, half = which % (XLO * NZ), which // (XLO * NZ)
    found = jnp.where(row == 0, lane, jnp.where(row == 1, block, jnp.where(row == 6, half, 0)))
    found = found.astype(F32).astype(BF16)
    sorted_runs = lax.dot_general(found, hit, (((1,), (1,)), ((), ())), preferred_element_type=F32)
    sorted_runs = jnp.where((row == 0) & (lane >= KRUNS), F32(FAR // RUN), sorted_runs).astype(jnp.int32)
    q_rows = [bal[pl.ds((xl * NY + i) * NZ + z, 1), :] for i in range(NY)]
    low = jnp.concatenate([r[:, half * RUN : half * RUN + 1] for r in q_rows for half in (0, 1)], axis=0)
    pos = low + lax.broadcasted_iota(jnp.int32, (QRUNS, ROWS), 1) // HEADS_HERE
    start = jnp.zeros((QRUNS, ROWS), jnp.int32)
    first = jnp.zeros((QRUNS, 1), jnp.int32)
    end = 0
    for d in range(DOCS):
        end = end + lengths[d]
        first = jnp.where(low >= end, end, first)
        start = jnp.where(pos >= end, end, start)
    row_tab[0] = pos
    row_tab[1] = start
    low_run = jnp.sum(jnp.where((lane < first // RUN) & (has > 0), 1, 0), axis=1, keepdims=True)
    high_run = jnp.sum(jnp.where((lane <= low // RUN) & (has > 0), 1, 0), axis=1, keepdims=True)
    tiles = jnp.maximum((high_run - low_run + TILE - 1) // TILE, 1)
    own_lane = lax.broadcasted_iota(jnp.int32, (QRUNS, 1), 0) == lane
    low_row = jnp.sum(jnp.where(own_lane, low_run, 0), axis=0, keepdims=True)
    more = tiles - 1
    upper = lax.broadcasted_iota(jnp.int32, (QRUNS, 1), 0) >= lax.broadcasted_iota(jnp.int32, (1, SPANS), 1)
    more_row = jnp.sum(jnp.where(own_lane, more, 0), axis=0, keepdims=True)
    ends = jnp.sum(jnp.where(upper, more_row, 0), axis=1, keepdims=True)
    passed = lane >= ends
    run_row = jnp.minimum(jnp.sum(jnp.where(passed, 1, 0), axis=0, keepdims=True), QRUNS - 1)
    tile_row = lane + 1 - jnp.sum(jnp.where(passed, more, 0), axis=0, keepdims=True)
    count = jnp.sum(more, axis=0, keepdims=True)
    tile_row = jnp.where(lane >= count, KRUNS // TILE, tile_row)
    values = [None, None, low_row, run_row, tile_row, jnp.where(lane == 0, count, 0)]
    out = sorted_runs
    for i in range(2, 6):
        out = jnp.where(row == i, values[i], out)
    tab[...] = out


def gather_kernel(
    q_ref, g_ref, k_ref, v_ref, bal_ref, len_ref, qg, kg, tab, row_tab, zeros_acc, zeros_grad, zeros_kv, bal, lengths, lsem, ysend, yrecv, zsend, zrecv, xsend, xrecv
):
    h, xl, y, z = here()
    x = h * XLO + xl
    first = xl * NZ
    y_up, y_dn = device(x, (y + 1) % NY, z), device(x, (y + NY - 1) % NY, z)
    z_to = {d: device(x, y, (z + d + NZ) % NZ) for d in (1, 2, -1, -2)}
    x_up, x_dn = device((x + 1) % NX, y, z), device((x + NX - 1) % NX, y, z)
    meet = greet([y_up, y_dn, x_up, x_dn] + list(z_to.values()))
    started = []

    def go(copy):
        copy.start()
        started.append(copy)
        return copy

    sent_z = {}

    def part(j):
        return (h + j) % 2

    def behind(sign, dist):
        return (z - sign * dist + NZ) % NZ

    def z_send(sign, hops, dist, j):
        ref = kg.at[first + behind(sign, dist - hops), part(j)]
        way = 0 if sign > 0 else 1
        sems = zsend.at[way, dist - 1, j], zrecv.at[way, dist - 1, j]
        sent_z[sign, dist, j] = go(remote(ref, ref, *sems, z_to[sign * hops]))

    sent_x = []

    def x_send(slot, block):
        dst = kg.at[first + block, h]
        for side, target in ((0, x_up), (1, x_dn)):
            sent_x.append(go(remote(dst, dst, xsend.at[side, slot], xrecv.at[side, slot], target)))

    def local(src, dst, slot):
        copy = pltpu.make_async_copy(src, dst, lsem.at[slot])
        copy.start()
        return copy

    own_kv = [local(ref, kg.at[first + z, i], i) for i, ref in enumerate((k_ref, v_ref))]
    own_tab = [local(bal_ref, bal, 4), local(len_ref, lengths, 5)]
    for copy in own_kv:
        copy.wait()
    meet()
    for j in (0, 1):
        for sign in (1, -1):
            z_send(sign, 2, 2, j)
    y_q_up = go(remote(q_ref, qg.at[y, 0], ysend.at[0], yrecv.at[0], y_up))
    y_g_dn = go(remote(g_ref, qg.at[y, 1], ysend.at[2], yrecv.at[2], y_dn))
    x_send(0, z)
    for sign in (1, -1):
        z_send(sign, 1, 1, 0)
    y_g_up = go(remote(g_ref, qg.at[y, 1], ysend.at[1], yrecv.at[1], y_up))
    y_q_dn = go(remote(q_ref, qg.at[y, 0], ysend.at[3], yrecv.at[3], y_dn))
    own_q = [local(ref, qg.at[y, i], 2 + i) for i, ref in enumerate((q_ref, g_ref))]
    for copy in own_tab:
        copy.wait()
    tables(bal, lengths, tab, row_tab, xl, y, z)
    for j in (0, 1):
        for sign in (1, -1):
            sent_z[sign, 2, j].wait_recv()
            if j == (0 if sign > 0 else 1):
                z_send(sign, 2, 4, j)
            z_send(sign, 1, 3, j)
            if j == 0:
                x_send(1 if sign > 0 else 2, behind(sign, 2))
    for sign in (1, -1):
        z_send(sign, 1, 1, 1)
    y_q_up.wait_recv()
    q_on = qg.at[(y + NY - 1) % NY, 0]
    y_fwd_up = go(remote(q_on, q_on, ysend.at[4], yrecv.at[4], y_up))
    y_g_dn.wait_recv()
    g_on = qg.at[(y + 1) % NY, 1]
    y_fwd_dn = go(remote(g_on, g_on, ysend.at[5], yrecv.at[5], y_dn))
    for slot, (sign, dist) in enumerate(((1, 1), (-1, 1), (1, 4), (1, 3), (-1, 3))):
        sent_z[sign, dist, 0].wait_recv()
        x_send(3 + slot, behind(sign, dist))
    for ref in (zeros_acc, zeros_grad, zeros_kv):
        ref[...] = jnp.zeros_like(ref)
    for sign, dist in ((1, 1), (-1, 1), (1, 3), (-1, 3), (-1, 4)):
        sent_z[sign, dist, 1].wait_recv()
    for copy in (y_g_up, y_q_dn, y_fwd_up, y_fwd_dn):
        copy.wait_recv()
    for copy in sent_x:
        copy.wait_recv()
    for copy in started:
        copy.wait_send()
    for copy in own_q:
        copy.wait()


ZEROS = (
    jax.ShapeDtypeStruct((QRUNS, DH, ROWS), F32),
    jax.ShapeDtypeStruct((QRUNS, DH, ROWS), F32),
    jax.ShapeDtypeStruct((2, XLO * NZ, 2, RUN, DH), F32),
)


def gather(q, g, k, v, bal, lengths):
    hbm = pl.BlockSpec(memory_space=pltpu.HBM)
    vmem = pl.BlockSpec(memory_space=pltpu.VMEM)
    dma = pltpu.SemaphoreType.DMA
    return pl.pallas_call(
        gather_kernel,
        out_shape=(
            jax.ShapeDtypeStruct((NY, 2, 2 * ROWS, DH), BF16),
            jax.ShapeDtypeStruct((XLO * NZ, 2, 2, RUN, DH), BF16),
            jax.ShapeDtypeStruct((8, SPANS), jnp.int32),
            jax.ShapeDtypeStruct((2, QRUNS, ROWS), jnp.int32),
            *ZEROS,
        ),
        in_specs=[hbm] * 6,
        out_specs=(vmem,) * 7,
        scratch_shapes=[
            pltpu.VMEM((SPANS // 2, BLK), jnp.int32),
            pltpu.SMEM((DOCS,), jnp.int32),
            dma((6,)), dma((6,)), dma((6,)), dma((2, 4, 2)), dma((2, 4, 2)), dma((2, 8)), dma((2, 8)),
        ],
        compiler_params=pltpu.CompilerParams(collective_id=0, has_side_effects=True, vmem_limit_bytes=8 << 20),
        name="gather_rows",
    )(*(pltpu.with_memory_space_constraint(a, pltpu.HBM) for a in (q, g, k, v, bal, lengths)))


def tile_runs(tab, low_run, t):
    runs = [low_run + t * TILE + u for u in range(TILE)]
    return [(tab[1, r], tab[6, r]) for r in runs], [tab[0, r] * RUN for r in runs]


def tile_rows(kg, indices, part):
    return jnp.concatenate([kg[block, part, half] for block, half in indices], axis=0)


def masked_scores(k, q, places, pos, start):
    scores = lax.dot_general(k, q, (((1,), (1,)), ((), ())), preferred_element_type=F32)
    offset = lax.broadcasted_iota(jnp.int32, (RUN, ROWS), 0)
    parts = []
    for u, base in enumerate(places):
        seen = (offset <= pos - base) & (offset >= start - base)
        parts.append(jnp.where(seen, scores[u * RUN : (u + 1) * RUN] * (SCALING * LOG2E), NEGATIVE))
    return jnp.concatenate(parts, axis=0)


def together(process, items):
    for end in [process(*item) for item in items]:
        end()


def first_tiles(process):
    together(process, [(q_run, 0, q_run) for q_run in range(QRUNS)])


def further_tiles(tab, process):
    def steps(unroll, first, count):
        def step(i, _):
            slots = [first + unroll * i + u for u in range(unroll)]
            together(process, [(tab[3, slot], tab[4, slot], slot) for slot in slots])
            return 0

        lax.fori_loop(0, count, step, 0)

    fours = tab[5, 0] // 4
    steps(4, 0, fours)
    steps(2, 4 * fours, (tab[5, 0] - 4 * fours + 1) // 2)


def query_rows(qg, q_run, part):
    return qg[q_run // 2, part, pl.ds(pl.multiple_of((q_run % 2) * ROWS, ROWS), ROWS), :]


def forward_tile(tab, row_tab, qg, kg, held, held_gw, combine):
    def process(q_run, t, slot):
        at = pl.ds(q_run, 1)
        indices, places = tile_runs(tab, tab[2, q_run], t)
        s = masked_scores(
            tile_rows(kg, indices, 0), query_rows(qg, q_run, 0), places, row_tab[0, at, :], row_tab[1, at, :]
        )
        held[slot] = s
        v = tile_rows(kg, indices, 1)
        gw = lax.dot_general(
            v, query_rows(qg, q_run, 1), (((1,), (1,)), ((), ())), preferred_element_type=F32
        )
        held_gw[slot] = gw
        top = jnp.maximum(jnp.max(s, axis=0, keepdims=True), FLOOR)
        raw = jnp.exp2(s - top)
        total = jnp.sum(raw, axis=0, keepdims=True)
        inner = jnp.sum(raw * gw, axis=0, keepdims=True)
        acc = lax.dot_general(v, raw.astype(BF16), (((0,), (0,)), ((), ())), preferred_element_type=F32)
        return lambda: combine(q_run, top, total, inner, acc)

    return process


def combined(old, old_acc, top, total, inner, acc):
    new_top = jnp.maximum(old[0], top)
    old_share, share = jnp.exp2(old[0] - new_top), jnp.exp2(top - new_top)
    stats = new_top, old[1] * old_share + total * share, old[2] * old_share + inner * share
    return stats, old_acc * old_share + acc * share


def forward_kernel(tab, row_tab, qg, kg, zeros, stats, out, held, held_gw):
    stats[0] = jnp.full((QRUNS, ROWS), FLOOR, F32)
    stats[1] = jnp.zeros((QRUNS, ROWS), F32)
    stats[2] = jnp.zeros((QRUNS, ROWS), F32)

    def combine(q_run, *new):
        at = pl.ds(q_run, 1)
        rows, out[q_run] = combined([stats[i, at, :] for i in range(3)], out[q_run], *new)
        for i in range(3):
            stats[i, at, :] = rows[i]

    further_tiles(tab, forward_tile(tab, row_tab, qg, kg, held, held_gw, combine))


def forward(tab, row_tab, qg, kg, zeros):
    smem = pl.BlockSpec(memory_space=pltpu.SMEM)
    vmem = pl.BlockSpec(memory_space=pltpu.VMEM)
    return pl.pallas_call(
        forward_kernel,
        out_shape=(
            jax.ShapeDtypeStruct((3, QRUNS, ROWS), F32),
            jax.ShapeDtypeStruct((QRUNS, DH, ROWS), F32),
            jax.ShapeDtypeStruct((ITEMS, TILE * RUN, ROWS), F32),
            jax.ShapeDtypeStruct((ITEMS, TILE * RUN, ROWS), F32),
        ),
        in_specs=[smem] + [vmem] * 4,
        out_specs=(vmem,) * 4,
        input_output_aliases={4: 1},
        compiler_params=pltpu.CompilerParams(vmem_limit_bytes=8 << 20),
        name="forward_stats",
    )(tab, row_tab, qg, kg, zeros)


def exchange_kernel(tab, row_tab, qg, kg, part, part_acc, out, acc_out, held, held_gw, mine, lsem, send, recv):
    h, xl, y, z = here()
    x = h * XLO + xl
    targets = [device(x, (y + d) % NY, z) for d in range(1, NY)]
    meet = greet(targets)

    def combine(q_run, *new):
        at = pl.ds(q_run, 1)
        rows, acc_out[q_run] = combined([part[i, at, :] for i in range(3)], part_acc[q_run], *new)
        for i in range(3):
            mine[i, at, :] = rows[i]

    first_tiles(forward_tile(tab, row_tab, qg, kg, held, held_gw, combine))
    meet()
    copies = []
    for d, target in enumerate(targets):
        copy = remote(mine, out.at[y], send.at[d], recv.at[d], target)
        copy.start()
        copies.append(copy)
    own = pltpu.make_async_copy(mine, out.at[y], lsem)
    own.start()
    own.wait()
    for copy in copies:
        copy.wait()


def exchange(tab, row_tab, qg, kg, part, part_acc):
    smem = pl.BlockSpec(memory_space=pltpu.SMEM)
    vmem = pl.BlockSpec(memory_space=pltpu.VMEM)
    dma = pltpu.SemaphoreType.DMA
    return pl.pallas_call(
        exchange_kernel,
        out_shape=(
            jax.ShapeDtypeStruct((NY,) + part.shape, F32),
            jax.ShapeDtypeStruct(part_acc.shape, F32),
            jax.ShapeDtypeStruct((QRUNS, TILE * RUN, ROWS), F32),
            jax.ShapeDtypeStruct((QRUNS, TILE * RUN, ROWS), F32),
        ),
        in_specs=[smem] + [vmem] * 5,
        out_specs=(vmem,) * 4,
        scratch_shapes=[pltpu.VMEM(part.shape, F32), dma, dma((NY - 1,)), dma((NY - 1,))],
        compiler_params=pltpu.CompilerParams(collective_id=1, has_side_effects=True, vmem_limit_bytes=8 << 20),
        name="exchange_stats",
    )(tab, row_tab, qg, kg, part, part_acc)


def backward_kernel(
    tab, qg, kg, stats, held, held_gw, more, more_gw, zeros_grad, zeros_kv, share_out, grad_acc, kv_acc, row_stats
):
    y = here()[2]
    top = jnp.maximum(jnp.maximum(stats[0, 0], stats[1, 0]), jnp.maximum(stats[2, 0], stats[3, 0]))
    shares = [jnp.exp2(stats[i, 0] - top) for i in range(NY)]
    total = sum(stats[i, 1] * shares[i] for i in range(NY))
    log_total = top + jnp.log(total) * LOG2E
    row_stats[0] = log_total
    row_stats[1] = sum(stats[i, 2] * shares[i] for i in range(NY)) / total
    share_out[...] = jnp.exp2(stats[y, 0] - log_total)

    def process(held, held_gw, q_run, t, slot):
        at = pl.ds(q_run, 1)
        indices, _ = tile_runs(tab, tab[2, q_run], t)
        weights = jnp.exp2(held[slot] - row_stats[0, at, :])
        gs = (weights * (held_gw[slot] - row_stats[1, at, :])).astype(BF16)
        value_part = jnp.dot(weights.astype(BF16), query_rows(qg, q_run, 1), preferred_element_type=F32)
        key_part = jnp.dot(gs, query_rows(qg, q_run, 0), preferred_element_type=F32)
        grad = lax.dot_general(
            tile_rows(kg, indices, 0), gs, (((0,), (0,)), ((), ())), preferred_element_type=F32
        )

        def end():
            for u, (block, half) in enumerate(indices):
                kv_acc[1, block, half] += value_part[u * RUN : (u + 1) * RUN]
                kv_acc[0, block, half] += key_part[u * RUN : (u + 1) * RUN]
            grad_acc[q_run] += grad

        return end

    first_tiles(functools.partial(process, held, held_gw))
    further_tiles(tab, functools.partial(process, more, more_gw))


def backward(tab, qg, kg, stats, held, held_gw, more, more_gw, zeros_grad, zeros_kv):
    smem = pl.BlockSpec(memory_space=pltpu.SMEM)
    vmem = pl.BlockSpec(memory_space=pltpu.VMEM)
    return pl.pallas_call(
        backward_kernel,
        out_shape=(
            jax.ShapeDtypeStruct((QRUNS, ROWS), F32),
            jax.ShapeDtypeStruct((QRUNS, DH, ROWS), F32),
            jax.ShapeDtypeStruct((2, XLO * NZ, 2, RUN, DH), F32),
        ),
        in_specs=[smem] + [vmem] * 9,
        out_specs=(vmem,) * 3,
        input_output_aliases={8: 1, 9: 2},
        scratch_shapes=[pltpu.VMEM((2, QRUNS, ROWS), F32)],
        compiler_params=pltpu.CompilerParams(vmem_limit_bytes=8 << 20),
        name="backward_terms",
    )(tab, qg, kg, stats, held, held_gw, more, more_gw, zeros_grad, zeros_kv)


AHEAD = (4, 3, 2)
BEHIND = (5, 6)
LATE = AHEAD + BEHIND


def reduce_kernel(
    acc, share, grad, kv, att, qgrad, kgrad, vgrad,
    rows, ybuf, ysum, nout, nbuf, oout, obuf, xout, xbuf, xsum, zsum, zbuf, last,
    ysend, yrecv, nsend, nrecv, osend, orecv, xsend, xrecv, zsend, zrecv, hsend, hrecv, z_word, x_word, z_far_word,
):
    h, xl, y, z = here()
    x = h * XLO + xl
    y_up, y_dn = device(x, (y + 1) % NY, z), device(x, (y + NY - 1) % NY, z)
    x_to = tuple(device((x + d) % NX, y, z) for d in (1, 2, 3))
    z_to = {d: device(x, y, (z + d) % NZ) for d in range(1, NZ)}
    z_near = ((0, z_to[1]), (1, z_to[NZ - 1]))
    x_near = ((0, x_to[0]), (1, x_to[2]))
    meet = greet([z_to[1], z_to[NZ - 1], x_to[0], x_to[2], y_up, y_dn])

    def tell(sem, targets):
        for side, target in targets:
            pl.semaphore_signal(sem.at[side], inc=1, device_id=target, device_id_type=MESH)

    def hear(sem):
        for side in (0, 1):
            pl.semaphore_wait(sem.at[side], 1)

    started = []

    def go(copy):
        copy.start()
        started.append(copy)
        return copy

    def scaled(part, block):
        return kv[part, block] * jnp.where(part == 0, F32(SCALING), F32(1.0))

    def term(step, offset):
        ring = (x + step) % NX
        return scaled(ring // XLO, (ring % XLO) * NZ + (z + offset) % NZ)

    def near_term(step):
        ring = (x + step) % NX
        sides = [nbuf[side, ring % XLO, ring // XLO].astype(F32) for side in (0, 1)]
        return term(step, 0) + sides[0] + sides[1]

    def put_rows(yy):
        for half in (0, 1):
            q_run = yy * 2 + half
            to = pl.ds(half * ROWS, ROWS)
            rows[yy, 0, to, :] = (acc[q_run] * share[pl.ds(q_run, 1), :]).T.astype(BF16)
            rows[yy, 1, to, :] = (grad[q_run] * SCALING).T.astype(BF16)

    def x_copy(kind, way, i, src):
        target = x_to[0] if way == 0 else x_to[2]
        return go(remote(src, xbuf.at[kind, way, i], xsend.at[kind, way, i], xrecv.at[kind, way, i], target))

    offsets = (AHEAD, BEHIND)
    sent = {}
    for side, offset in ((0, 1), (1, NZ - 1)):
        for lo in range(XLO):
            for part in (0, 1):
                nout[side, lo, part] = scaled(part, lo * NZ + (z + offset) % NZ).astype(BF16)
    for way in (0, 1):
        for i, offset in enumerate(offsets[way]):
            xout[0, way, i] = term(2, offset).astype(BF16)
    meet()
    tell(z_word, z_near)
    tell(x_word, x_near)
    for i in range(len(AHEAD)):
        for way in (0, 1):
            if i < len(offsets[way]):
                sent[0, way, i] = x_copy(0, way, i, xout.at[0, way, i])
    near = []
    for lo in range(XLO):
        for side, offset in ((0, 1), (1, NZ - 1)):
            sems = nsend.at[side, lo], nrecv.at[side, lo]
            near.append(go(remote(nout.at[side, lo], nbuf.at[side, lo], *sems, z_to[offset])))
    for i in range(len(AHEAD)):
        for way in (0, 1):
            if i < len(offsets[1 - way]):
                xout[1, way, i] = term(1 if way == 0 else 3, offsets[1 - way][i]).astype(BF16)
                sent[1, way, i] = x_copy(1, way, i, xout.at[1, way, i])
    y_far, y_next, y_prev = (y + 2) % NY, (y + 1) % NY, (y + NY - 1) % NY
    put_rows(y_far)
    y_a = go(remote(rows.at[y_far, 0], ybuf.at[0], ysend.at[0], yrecv.at[0], y_up))
    y_b = go(remote(rows.at[y_far, 1], ybuf.at[1], ysend.at[1], yrecv.at[1], y_dn))
    hear(z_word)
    tell(z_far_word, ((0, z_to[2]), (1, z_to[NZ - 2])))
    for i in range(len(AHEAD)):
        for way in (0, 1):
            if i < len(offsets[way]):
                sent[0, way, i].wait_recv()
                own = term(1 if way == 0 else 3, offsets[way][i])
                xsum[way, i] = (xbuf[0, way, i].astype(F32) + own).astype(BF16)
                sent[2, way, i] = x_copy(2, way, i, xsum.at[way, i])
    for copy in near:
        copy.wait_recv()
    hear(x_word)
    across = []
    for step in (2, 1, 3):
        oout[step - 1] = near_term(step).astype(BF16)
        sems = osend.at[step - 1], orecv.at[step - 1]
        across.append(go(remote(oout.at[step - 1], obuf.at[step - 1], *sems, x_to[step - 1])))
    put_rows(y_next)
    put_rows(y_prev)
    y_c = go(remote(rows.at[y_next, 1], ybuf.at[2], ysend.at[2], yrecv.at[2], y_up))
    y_d = go(remote(rows.at[y_prev, 0], ybuf.at[3], ysend.at[3], yrecv.at[3], y_dn))
    z_copies = []
    hear(z_far_word)
    for i in range(len(AHEAD)):
        for way in (0, 1):
            if i < len(offsets[way]):
                sent[2, way, i].wait_recv()
                sent[1, 1 - way, i].wait_recv()
                offset = offsets[way][i]
                slot = LATE.index(offset)
                block = term(0, offset) + xbuf[2, way, i].astype(F32) + xbuf[1, 1 - way, i].astype(F32)
                zsum[slot] = block.astype(BF16)
                sems = zsend.at[slot], zrecv.at[slot]
                z_copies.append(go(remote(zsum.at[slot], zbuf.at[slot], *sems, z_to[offset])))
    y_a.wait_recv()
    ysum[0] = (ybuf[0].astype(F32) + rows[y_next, 0].astype(F32)).astype(BF16)
    y_e = go(remote(ysum.at[0], ybuf.at[4], ysend.at[4], yrecv.at[4], y_up))
    y_b.wait_recv()
    ysum[1] = (ybuf[1].astype(F32) + rows[y_prev, 1].astype(F32)).astype(BF16)
    y_f = go(remote(ysum.at[1], ybuf.at[5], ysend.at[5], yrecv.at[5], y_dn))
    put_rows(y)
    total = near_term(0)
    for copy in across:
        copy.wait_recv()
    total = total + obuf[0].astype(F32) + obuf[1].astype(F32) + obuf[2].astype(F32)
    for copy in z_copies:
        copy.wait_recv()
    for slot in range(len(LATE)):
        total = total + zbuf[slot].astype(F32)
    last[0] = total.astype(BF16)
    final = go(remote(last.at[0], last.at[1], hsend, hrecv, x_to[1]))
    y_d.wait_recv()
    y_e.wait_recv()
    att[...] = (rows[y, 0].astype(F32) + ybuf[3].astype(F32) + ybuf[4].astype(F32)).astype(BF16)
    y_c.wait_recv()
    y_f.wait_recv()
    qgrad[...] = (rows[y, 1].astype(F32) + ybuf[2].astype(F32) + ybuf[5].astype(F32)).astype(BF16)
    final.wait_recv()
    mine, other = last[0], last[1]
    kgrad[...] = jnp.where(h == 0, mine, other)
    vgrad[...] = jnp.where(h == 0, other, mine)
    for copy in started:
        copy.wait_send()


def reduce(acc, share, grad, kv):
    vmem = pl.BlockSpec(memory_space=pltpu.VMEM)
    dma = pltpu.SemaphoreType.DMA
    block = (BLK, DH)
    late = len(LATE)
    word = pltpu.SemaphoreType.REGULAR((2,))
    return pl.pallas_call(
        reduce_kernel,
        out_shape=(
            jax.ShapeDtypeStruct((2 * ROWS, DH), BF16),
            jax.ShapeDtypeStruct((2 * ROWS, DH), BF16),
            jax.ShapeDtypeStruct(block, BF16),
            jax.ShapeDtypeStruct(block, BF16),
        ),
        in_specs=[vmem] * 4,
        out_specs=(vmem,) * 4,
        scratch_shapes=[
            pltpu.VMEM((NY, 2, 2 * ROWS, DH), BF16),
            pltpu.VMEM((6, 2 * ROWS, DH), BF16),
            pltpu.VMEM((2, 2 * ROWS, DH), BF16),
            pltpu.VMEM((2, XLO, 2) + block, BF16),
            pltpu.VMEM((2, XLO, 2) + block, BF16),
            pltpu.VMEM((3,) + block, BF16),
            pltpu.VMEM((3,) + block, BF16),
            pltpu.VMEM((2, 2, 3) + block, BF16),
            pltpu.VMEM((3, 2, 3) + block, BF16),
            pltpu.VMEM((2, 3) + block, BF16),
            pltpu.VMEM((late,) + block, BF16),
            pltpu.VMEM((late,) + block, BF16),
            pltpu.VMEM((2,) + block, BF16),
            dma((6,)), dma((6,)), dma((2, XLO)), dma((2, XLO)), dma((3,)), dma((3,)),
            dma((3, 2, 3)), dma((3, 2, 3)), dma((late,)), dma((late,)), dma, dma, word, word, word,
        ],
        compiler_params=pltpu.CompilerParams(collective_id=2, has_side_effects=True, vmem_limit_bytes=10 << 20),
        name="reduce_terms",
    )(acc, share, grad, kv)


def store_kernel(*refs):
    count = len(refs) // 2
    copies = [pltpu.make_async_copy(refs[i], refs[count + i], refs[-1].at[i]) for i in range(count)]
    for copy in copies:
        copy.start()
    for copy in copies:
        copy.wait()


def store(*arrays):
    return pl.pallas_call(
        store_kernel,
        out_shape=tuple(jax.ShapeDtypeStruct(a.shape, a.dtype) for a in arrays),
        in_specs=[pl.BlockSpec(memory_space=pltpu.VMEM)] * len(arrays),
        out_specs=(pl.BlockSpec(memory_space=pl.ANY),) * len(arrays),
        scratch_shapes=[pltpu.SemaphoreType.DMA((len(arrays),))],
        compiler_params=pltpu.CompilerParams(vmem_limit_bytes=1 << 20),
        name="store_outputs",
    )(*arrays)


def body(queries, key_rows, value_rows, out_grad, doc_lengths, balance):
    flat = (2 * ROWS, DH)
    bal = balance.reshape(SPANS // 2, BLK)
    qg, kg, tab, row_tab, zeros_acc, zeros_grad, zeros_kv = gather(
        queries.reshape(flat),
        out_grad.reshape(flat),
        key_rows.reshape(2, RUN, DH),
        value_rows.reshape(2, RUN, DH),
        bal,
        doc_lengths,
    )
    part, part_acc, more, more_gw = forward(tab, row_tab, qg, kg, zeros_acc)
    stats, acc, held, held_gw = exchange(tab, row_tab, qg, kg, part, part_acc)
    share, grad, kv = backward(
        tab, qg, kg, stats, held, held_gw, more, more_gw, zeros_grad, zeros_kv
    )
    kv = kv.reshape(2, XLO * NZ, BLK, DH)
    attended, query_grad, key_grad, value_grad = store(*reduce(acc, share, grad, kv))
    return attended.reshape(queries.shape), query_grad.reshape(queries.shape), key_grad, value_grad


def solution(mesh):
    return jax.shard_map(
        body,
        mesh=mesh,
        in_specs=(
            P(("seq", "ctx"), "head", None),
            P(("seq", "ctx"), None),
            P(("seq", "ctx"), None),
            P(("seq", "ctx"), "head", None),
            P("seq"),
            P("seq"),
        ),
        out_specs=(
            P(("seq", "ctx"), "head", None),
            P(("seq", "ctx"), "head", None),
            P(("seq", "ctx"), None),
            P(("seq", "ctx"), None),
        ),
        check_vma=False,
    )
```

```python
import functools
import math

import jax
import jax.numpy as jnp
from jax import lax
from jax.experimental import pallas as pl
from jax.experimental.pallas import tpu as pltpu
from jax.sharding import PartitionSpec as P

NX, NY, NZ = 4, 4, 8
XLO = 2
RUN = 64
DH = 128
HEADS_HERE = 4
ROWS = RUN * HEADS_HERE
BLK = 2 * RUN
KRUNS = XLO * NZ * 2
QRUNS = NY * 2
TILE = 3
SPANS = 128
MOST_TILES = (KRUNS + TILE - 1) // TILE
ITEMS = QRUNS * (MOST_TILES - 1)
DOCS = 8
NEGATIVE = -1e30
FLOOR = -1e29
FAR = 1 << 20
SCALING = 1.0 / math.sqrt(DH)
LOG2E = 1.0 / math.log(2.0)
MESH = pl.DeviceIdType.MESH
F32 = jnp.float32
BF16 = jnp.bfloat16


def here():
    c = lax.axis_index("ctx")
    h = lax.axis_index("head")
    return h, c // (NY * NZ), (c // NZ) % NY, c % NZ


def device(x, y, z):
    return {"ctx": ((x % XLO) * NY + y) * NZ + z, "head": x // XLO}


def greet(targets):
    barrier = pltpu.get_barrier_semaphore()
    for target in targets:
        pl.semaphore_signal(barrier, inc=1, device_id=target, device_id_type=MESH)
    return lambda: pl.semaphore_wait(barrier, len(targets))


def remote(src, dst, send, recv, target):
    return pltpu.make_async_remote_copy(
        src_ref=src, dst_ref=dst, send_sem=send, recv_sem=recv, device_id=target, device_id_type=MESH
    )


def tables(bal, lengths, tab, row_tab, xl, y, z):
    lane = lax.broadcasted_iota(jnp.int32, (1, SPANS), 1)
    slabs = [bal[pl.ds(pl.multiple_of((i * NY + y) * NZ, NZ), NZ), :] for i in range(XLO)]
    held = [slab[:, half * RUN : half * RUN + 1] // RUN for half in (0, 1) for slab in slabs]
    held = jnp.concatenate(held, axis=0)
    index = lax.broadcasted_iota(jnp.int32, (KRUNS, 1), 0)
    match = held == lane
    has = jnp.sum(jnp.where(match, 1, 0), axis=0, keepdims=True)
    which = jnp.sum(jnp.where(match, index, 0), axis=0, keepdims=True)
    before = jnp.sum(jnp.where(held < lane, 1, 0), axis=0, keepdims=True)
    rank = jnp.where(has > 0, before, -1)
    hit = jnp.where(rank == lax.broadcasted_iota(jnp.int32, (SPANS, 1), 0), 1.0, 0.0).astype(BF16)
    row = lax.broadcasted_iota(jnp.int32, (8, 1), 0)
    block, half = which % (XLO * NZ), which // (XLO * NZ)
    found = jnp.where(row == 0, lane, jnp.where(row == 1, block, jnp.where(row == 6, half, 0)))
    found = found.astype(F32).astype(BF16)
    sorted_runs = lax.dot_general(found, hit, (((1,), (1,)), ((), ())), preferred_element_type=F32)
    sorted_runs = jnp.where((row == 0) & (lane >= KRUNS), F32(FAR // RUN), sorted_runs).astype(jnp.int32)
    q_rows = [bal[pl.ds((xl * NY + i) * NZ + z, 1), :] for i in range(NY)]
    low = jnp.concatenate([r[:, half * RUN : half * RUN + 1] for r in q_rows for half in (0, 1)], axis=0)
    pos = low + lax.broadcasted_iota(jnp.int32, (QRUNS, ROWS), 1) // HEADS_HERE
    start = jnp.zeros((QRUNS, ROWS), jnp.int32)
    first = jnp.zeros((QRUNS, 1), jnp.int32)
    end = 0
    for d in range(DOCS):
        end = end + lengths[d]
        first = jnp.where(low >= end, end, first)
        start = jnp.where(pos >= end, end, start)
    row_tab[0] = pos
    row_tab[1] = start
    low_run = jnp.sum(jnp.where((lane < first // RUN) & (has > 0), 1, 0), axis=1, keepdims=True)
    high_run = jnp.sum(jnp.where((lane <= low // RUN) & (has > 0), 1, 0), axis=1, keepdims=True)
    tiles = jnp.maximum((high_run - low_run + TILE - 1) // TILE, 1)
    own_lane = lax.broadcasted_iota(jnp.int32, (QRUNS, 1), 0) == lane
    low_row = jnp.sum(jnp.where(own_lane, low_run, 0), axis=0, keepdims=True)
    more = tiles - 1
    upper = lax.broadcasted_iota(jnp.int32, (QRUNS, 1), 0) >= lax.broadcasted_iota(jnp.int32, (1, SPANS), 1)
    more_row = jnp.sum(jnp.where(own_lane, more, 0), axis=0, keepdims=True)
    ends = jnp.sum(jnp.where(upper, more_row, 0), axis=1, keepdims=True)
    passed = lane >= ends
    run_row = jnp.minimum(jnp.sum(jnp.where(passed, 1, 0), axis=0, keepdims=True), QRUNS - 1)
    tile_row = lane + 1 - jnp.sum(jnp.where(passed, more, 0), axis=0, keepdims=True)
    count = jnp.sum(more, axis=0, keepdims=True)
    tile_row = jnp.where(lane >= count, MOST_TILES, tile_row)
    values = [None, None, low_row, run_row, tile_row, jnp.where(lane == 0, count, 0)]
    out = sorted_runs
    for i in range(2, 6):
        out = jnp.where(row == i, values[i], out)
    tab[...] = out


def gather_kernel(
    q_ref, g_ref, k_ref, v_ref, bal_ref, len_ref, qg, kg, tab, row_tab, zeros_acc, zeros_grad, zeros_kv, bal, lengths, lsem, ysend, yrecv, zsend, zrecv, xsend, xrecv
):
    h, xl, y, z = here()
    x = h * XLO + xl
    first = xl * NZ
    y_up, y_dn = device(x, (y + 1) % NY, z), device(x, (y + NY - 1) % NY, z)
    z_to = {d: device(x, y, (z + d + NZ) % NZ) for d in (1, 2, -1, -2)}
    x_up, x_dn = device((x + 1) % NX, y, z), device((x + NX - 1) % NX, y, z)
    meet = greet([z_to[2], z_to[-2], z_to[1], z_to[-1], y_up, y_dn, x_up, x_dn])
    started = []

    def go(copy):
        copy.start()
        started.append(copy)
        return copy

    sent_z = {}

    def part(j):
        return (h + j) % 2

    def behind(sign, dist):
        return (z - sign * dist + NZ) % NZ

    def z_send(sign, hops, dist, j):
        ref = kg.at[first + behind(sign, dist - hops), part(j)]
        way = 0 if sign > 0 else 1
        sems = zsend.at[way, dist - 1, j], zrecv.at[way, dist - 1, j]
        sent_z[sign, dist, j] = go(remote(ref, ref, *sems, z_to[sign * hops]))

    sent_x = []

    def x_send(slot, block):
        dst = kg.at[first + block, h]
        for side, target in ((0, x_up), (1, x_dn)):
            sent_x.append(go(remote(dst, dst, xsend.at[side, slot], xrecv.at[side, slot], target)))

    def local(src, dst, slot):
        copy = pltpu.make_async_copy(src, dst, lsem.at[slot])
        copy.start()
        return copy

    own_kv = [local(ref, kg.at[first + z, i], i) for i, ref in enumerate((k_ref, v_ref))]
    own_tab = [local(bal_ref, bal, 4), local(len_ref, lengths, 5)]
    for copy in own_kv:
        copy.wait()
    meet()
    for j in (0, 1):
        for sign in (1, -1):
            z_send(sign, 2, 2, j)
    y_q_up = go(remote(q_ref, qg.at[y, 0], ysend.at[0], yrecv.at[0], y_up))
    y_g_dn = go(remote(g_ref, qg.at[y, 1], ysend.at[2], yrecv.at[2], y_dn))
    x_send(0, z)
    for sign in (1, -1):
        z_send(sign, 1, 1, 0)
    y_g_up = go(remote(g_ref, qg.at[y, 1], ysend.at[1], yrecv.at[1], y_up))
    y_q_dn = go(remote(q_ref, qg.at[y, 0], ysend.at[3], yrecv.at[3], y_dn))
    own_q = [local(ref, qg.at[y, i], 2 + i) for i, ref in enumerate((q_ref, g_ref))]
    for copy in own_tab:
        copy.wait()
    tables(bal, lengths, tab, row_tab, xl, y, z)
    for j in (0, 1):
        for sign in (1, -1):
            sent_z[sign, 2, j].wait_recv()
            if j == (0 if sign > 0 else 1):
                z_send(sign, 2, 4, j)
            z_send(sign, 1, 3, j)
            if j == 0:
                x_send(1 if sign > 0 else 2, behind(sign, 2))
    for sign in (1, -1):
        z_send(sign, 1, 1, 1)
    y_q_up.wait_recv()
    q_on = qg.at[(y + NY - 1) % NY, 0]
    y_fwd_up = go(remote(q_on, q_on, ysend.at[4], yrecv.at[4], y_up))
    y_g_dn.wait_recv()
    g_on = qg.at[(y + 1) % NY, 1]
    y_fwd_dn = go(remote(g_on, g_on, ysend.at[5], yrecv.at[5], y_dn))
    for slot, (sign, dist) in enumerate(((1, 1), (-1, 1), (1, 4), (1, 3), (-1, 3))):
        sent_z[sign, dist, 0].wait_recv()
        x_send(3 + slot, behind(sign, dist))
    for ref in (zeros_acc, zeros_grad, zeros_kv):
        ref[...] = jnp.zeros_like(ref)
    for sign, dist in ((1, 1), (-1, 1), (1, 3), (-1, 3), (-1, 4)):
        sent_z[sign, dist, 1].wait_recv()
    for copy in (y_g_up, y_q_dn, y_fwd_up, y_fwd_dn):
        copy.wait_recv()
    for copy in sent_x:
        copy.wait_recv()
    for copy in started:
        copy.wait_send()
    for copy in own_q:
        copy.wait()


ZEROS = (
    jax.ShapeDtypeStruct((QRUNS, DH, ROWS), F32),
    jax.ShapeDtypeStruct((QRUNS, DH, ROWS), F32),
    jax.ShapeDtypeStruct((2, XLO * NZ, 2, RUN, DH), F32),
)


def gather(q, g, k, v, bal, lengths):
    hbm = pl.BlockSpec(memory_space=pltpu.HBM)
    vmem = pl.BlockSpec(memory_space=pltpu.VMEM)
    dma = pltpu.SemaphoreType.DMA
    return pl.pallas_call(
        gather_kernel,
        out_shape=(
            jax.ShapeDtypeStruct((NY, 2, 2 * ROWS, DH), BF16),
            jax.ShapeDtypeStruct((XLO * NZ, 2, 2, RUN, DH), BF16),
            jax.ShapeDtypeStruct((8, SPANS), jnp.int32),
            jax.ShapeDtypeStruct((2, QRUNS, ROWS), jnp.int32),
            *ZEROS,
        ),
        in_specs=[hbm] * 6,
        out_specs=(vmem,) * 7,
        scratch_shapes=[
            pltpu.VMEM((SPANS // 2, BLK), jnp.int32),
            pltpu.SMEM((DOCS,), jnp.int32),
            dma((6,)), dma((6,)), dma((6,)), dma((2, 4, 2)), dma((2, 4, 2)), dma((2, 8)), dma((2, 8)),
        ],
        compiler_params=pltpu.CompilerParams(collective_id=0, has_side_effects=True, vmem_limit_bytes=8 << 20),
        name="gather_rows",
    )(*(pltpu.with_memory_space_constraint(a, pltpu.HBM) for a in (q, g, k, v, bal, lengths)))


def tile_runs(tab, low_run, t):
    runs = [low_run + t * TILE + u for u in range(TILE)]
    return [(tab[1, r], tab[6, r]) for r in runs], [tab[0, r] * RUN for r in runs]


def tile_rows(kg, indices, part):
    return jnp.concatenate([kg[block, part, half] for block, half in indices], axis=0)


def masked_scores(k, q, places, pos, start):
    scores = lax.dot_general(k, q, (((1,), (1,)), ((), ())), preferred_element_type=F32)
    offset = lax.broadcasted_iota(jnp.int32, (RUN, ROWS), 0)
    parts = []
    for u, base in enumerate(places):
        seen = (offset <= pos - base) & (offset >= start - base)
        parts.append(jnp.where(seen, scores[u * RUN : (u + 1) * RUN] * (SCALING * LOG2E), NEGATIVE))
    return jnp.concatenate(parts, axis=0)


def together(process, items):
    for end in [process(*item) for item in items]:
        end()


def first_tiles(process):
    together(process, [(q_run, 0, q_run) for q_run in range(QRUNS)])


def further_tiles(tab, process):
    def steps(unroll, first, count):
        def step(i, _):
            slots = [first + unroll * i + u for u in range(unroll)]
            together(process, [(tab[3, slot], tab[4, slot], slot) for slot in slots])
            return 0

        lax.fori_loop(0, count, step, 0)

    fours = tab[5, 0] // 4
    steps(4, 0, fours)
    steps(2, 4 * fours, (tab[5, 0] - 4 * fours + 1) // 2)


def query_rows(qg, q_run, part):
    return qg[q_run // 2, part, pl.ds(pl.multiple_of((q_run % 2) * ROWS, ROWS), ROWS), :]


def forward_tile(tab, row_tab, qg, kg, held, held_gw, combine):
    def process(q_run, t, slot):
        at = pl.ds(q_run, 1)
        indices, places = tile_runs(tab, tab[2, q_run], t)
        s = masked_scores(
            tile_rows(kg, indices, 0), query_rows(qg, q_run, 0), places, row_tab[0, at, :], row_tab[1, at, :]
        )
        held[slot] = s
        v = tile_rows(kg, indices, 1)
        gw = lax.dot_general(
            v, query_rows(qg, q_run, 1), (((1,), (1,)), ((), ())), preferred_element_type=F32
        )
        held_gw[slot] = gw
        top = jnp.maximum(jnp.max(s, axis=0, keepdims=True), FLOOR)
        raw = jnp.exp2(s - top)
        total = jnp.sum(raw, axis=0, keepdims=True)
        inner = jnp.sum(raw * gw, axis=0, keepdims=True)
        acc = lax.dot_general(v, raw.astype(BF16), (((0,), (0,)), ((), ())), preferred_element_type=F32)
        return lambda: combine(q_run, top, total, inner, acc)

    return process


def combined(old, old_acc, top, total, inner, acc):
    new_top = jnp.maximum(old[0], top)
    old_share, share = jnp.exp2(old[0] - new_top), jnp.exp2(top - new_top)
    stats = new_top, old[1] * old_share + total * share, old[2] * old_share + inner * share
    return stats, old_acc * old_share + acc * share


def forward_kernel(tab, row_tab, qg, kg, zeros, stats, out, held, held_gw):
    stats[0] = jnp.full((QRUNS, ROWS), FLOOR, F32)
    stats[1] = jnp.zeros((QRUNS, ROWS), F32)
    stats[2] = jnp.zeros((QRUNS, ROWS), F32)

    def combine(q_run, *new):
        at = pl.ds(q_run, 1)
        rows, out[q_run] = combined([stats[i, at, :] for i in range(3)], out[q_run], *new)
        for i in range(3):
            stats[i, at, :] = rows[i]

    further_tiles(tab, forward_tile(tab, row_tab, qg, kg, held, held_gw, combine))


def forward(tab, row_tab, qg, kg, zeros):
    smem = pl.BlockSpec(memory_space=pltpu.SMEM)
    vmem = pl.BlockSpec(memory_space=pltpu.VMEM)
    return pl.pallas_call(
        forward_kernel,
        out_shape=(
            jax.ShapeDtypeStruct((3, QRUNS, ROWS), F32),
            jax.ShapeDtypeStruct((QRUNS, DH, ROWS), F32),
            jax.ShapeDtypeStruct((ITEMS, TILE * RUN, ROWS), F32),
            jax.ShapeDtypeStruct((ITEMS, TILE * RUN, ROWS), F32),
        ),
        in_specs=[smem] + [vmem] * 4,
        out_specs=(vmem,) * 4,
        input_output_aliases={4: 1},
        compiler_params=pltpu.CompilerParams(vmem_limit_bytes=8 << 20),
        name="forward_stats",
    )(tab, row_tab, qg, kg, zeros)


def exchange_kernel(
    tab_ref, row_tab, qg, kg, part, part_acc, out, acc_out, held, held_gw, tab, mine, lsem, send, recv
):
    h, xl, y, z = here()
    x = h * XLO + xl
    targets = [device(x, (y + d) % NY, z) for d in (2, 1, 3)]
    meet = greet(targets)
    table = pltpu.make_async_copy(tab_ref, tab, lsem)
    table.start()
    table.wait()

    def combine(q_run, *new):
        at = pl.ds(q_run, 1)
        rows, acc_out[q_run] = combined([part[i, at, :] for i in range(3)], part_acc[q_run], *new)
        for i in range(3):
            mine[i, at, :] = rows[i]

    first_tiles(forward_tile(tab, row_tab, qg, kg, held, held_gw, combine))
    meet()
    copies = []
    for d, target in enumerate(targets):
        copy = remote(mine, out.at[y], send.at[d], recv.at[d], target)
        copy.start()
        copies.append(copy)
    own = pltpu.make_async_copy(mine, out.at[y], lsem)
    own.start()
    own.wait()
    for copy in copies:
        copy.wait()


def exchange(tab, row_tab, qg, kg, part, part_acc):
    vmem = pl.BlockSpec(memory_space=pltpu.VMEM)
    dma = pltpu.SemaphoreType.DMA
    return pl.pallas_call(
        exchange_kernel,
        out_shape=(
            jax.ShapeDtypeStruct((NY,) + part.shape, F32),
            jax.ShapeDtypeStruct(part_acc.shape, F32),
            jax.ShapeDtypeStruct((QRUNS, TILE * RUN, ROWS), F32),
            jax.ShapeDtypeStruct((QRUNS, TILE * RUN, ROWS), F32),
        ),
        in_specs=[vmem] * 6,
        out_specs=(vmem,) * 4,
        scratch_shapes=[pltpu.SMEM(tab.shape, jnp.int32), pltpu.VMEM(part.shape, F32), dma, dma((NY - 1,)), dma((NY - 1,))],
        compiler_params=pltpu.CompilerParams(collective_id=1, has_side_effects=True, vmem_limit_bytes=8 << 20),
        name="exchange_stats",
    )(tab, row_tab, qg, kg, part, part_acc)


def backward_kernel(
    tab, qg, kg, stats, held, held_gw, more, more_gw, zeros_grad, zeros_kv, share_out, grad_acc, kv_acc, row_stats
):
    y = here()[2]
    top = jnp.maximum(jnp.maximum(stats[0, 0], stats[1, 0]), jnp.maximum(stats[2, 0], stats[3, 0]))
    shares = [jnp.exp2(stats[i, 0] - top) for i in range(NY)]
    total = sum(stats[i, 1] * shares[i] for i in range(NY))
    log_total = top + jnp.log(total) * LOG2E
    row_stats[0] = log_total
    row_stats[1] = sum(stats[i, 2] * shares[i] for i in range(NY)) / total
    share_out[...] = jnp.exp2(stats[y, 0] - log_total)

    def process(held, held_gw, q_run, t, slot):
        at = pl.ds(q_run, 1)
        indices, _ = tile_runs(tab, tab[2, q_run], t)
        weights = jnp.exp2(held[slot] - row_stats[0, at, :])
        gs = (weights * (held_gw[slot] - row_stats[1, at, :])).astype(BF16)
        value_part = jnp.dot(weights.astype(BF16), query_rows(qg, q_run, 1), preferred_element_type=F32)
        key_part = jnp.dot(gs, query_rows(qg, q_run, 0), preferred_element_type=F32)
        grad = lax.dot_general(
            tile_rows(kg, indices, 0), gs, (((0,), (0,)), ((), ())), preferred_element_type=F32
        )

        def end():
            for u, (block, half) in enumerate(indices):
                kv_acc[1, block, half] += value_part[u * RUN : (u + 1) * RUN]
                kv_acc[0, block, half] += key_part[u * RUN : (u + 1) * RUN]
            grad_acc[q_run] += grad

        return end

    first_tiles(functools.partial(process, held, held_gw))
    further_tiles(tab, functools.partial(process, more, more_gw))


def backward(tab, qg, kg, stats, held, held_gw, more, more_gw, zeros_grad, zeros_kv):
    smem = pl.BlockSpec(memory_space=pltpu.SMEM)
    vmem = pl.BlockSpec(memory_space=pltpu.VMEM)
    return pl.pallas_call(
        backward_kernel,
        out_shape=(
            jax.ShapeDtypeStruct((QRUNS, ROWS), F32),
            jax.ShapeDtypeStruct((QRUNS, DH, ROWS), F32),
            jax.ShapeDtypeStruct((2, XLO * NZ, 2, RUN, DH), F32),
        ),
        in_specs=[smem] + [vmem] * 9,
        out_specs=(vmem,) * 3,
        input_output_aliases={8: 1, 9: 2},
        scratch_shapes=[pltpu.VMEM((2, QRUNS, ROWS), F32)],
        compiler_params=pltpu.CompilerParams(vmem_limit_bytes=8 << 20),
        name="backward_terms",
    )(tab, qg, kg, stats, held, held_gw, more, more_gw, zeros_grad, zeros_kv)


AHEAD = (4, 3, 2)
BEHIND = (5, 6)
LATE = AHEAD + BEHIND


def reduce_kernel(
    acc, share, grad, kv, att, qgrad, kgrad, vgrad,
    rows, ybuf, ysum, nout, nbuf, oout, obuf, xout, xbuf, xsum, zsum, zbuf, last,
    ysend, yrecv, nsend, nrecv, osend, orecv, xsend, xrecv, zsend, zrecv, hsend, hrecv, z_word, x_word, z_far_word,
):
    h, xl, y, z = here()
    x = h * XLO + xl
    y_up, y_dn = device(x, (y + 1) % NY, z), device(x, (y + NY - 1) % NY, z)
    x_to = tuple(device((x + d) % NX, y, z) for d in (1, 2, 3))
    z_to = {d: device(x, y, (z + d) % NZ) for d in range(1, NZ)}
    z_near = ((0, z_to[1]), (1, z_to[NZ - 1]))
    x_near = ((0, x_to[0]), (1, x_to[2]))
    meet = greet([z_to[1], z_to[NZ - 1], x_to[0], x_to[2], y_up, y_dn])

    def tell(sem, targets):
        for side, target in targets:
            pl.semaphore_signal(sem.at[side], inc=1, device_id=target, device_id_type=MESH)

    def hear(sem):
        for side in (0, 1):
            pl.semaphore_wait(sem.at[side], 1)

    started = []

    def go(copy):
        copy.start()
        started.append(copy)
        return copy

    def scaled(part, block):
        return kv[part, block] * jnp.where(part == 0, F32(SCALING), F32(1.0))

    def term(step, offset):
        ring = (x + step) % NX
        return scaled(ring // XLO, (ring % XLO) * NZ + (z + offset) % NZ)

    def near_term(step):
        ring = (x + step) % NX
        sides = [nbuf[side, ring % XLO, ring // XLO].astype(F32) for side in (0, 1)]
        return term(step, 0) + sides[0] + sides[1]

    def put_rows(yy):
        for half in (0, 1):
            q_run = yy * 2 + half
            to = pl.ds(half * ROWS, ROWS)
            rows[yy, 0, to, :] = (acc[q_run] * share[pl.ds(q_run, 1), :]).T.astype(BF16)
            rows[yy, 1, to, :] = (grad[q_run] * SCALING).T.astype(BF16)

    def x_copy(kind, way, i, src):
        target = x_to[0] if way == 0 else x_to[2]
        return go(remote(src, xbuf.at[kind, way, i], xsend.at[kind, way, i], xrecv.at[kind, way, i], target))

    offsets = (AHEAD, BEHIND)
    sent = {}
    for side, offset in ((0, 1), (1, NZ - 1)):
        for lo in range(XLO):
            for part in (0, 1):
                nout[side, lo, part] = scaled(part, lo * NZ + (z + offset) % NZ).astype(BF16)
    for way in (0, 1):
        for i, offset in enumerate(offsets[way]):
            xout[0, way, i] = term(2, offset).astype(BF16)
    meet()
    tell(z_word, z_near)
    tell(x_word, x_near)
    for i in range(len(AHEAD)):
        for way in (0, 1):
            if i < len(offsets[way]):
                sent[0, way, i] = x_copy(0, way, i, xout.at[0, way, i])
    near = []
    for lo in range(XLO):
        for side, offset in ((0, 1), (1, NZ - 1)):
            sems = nsend.at[side, lo], nrecv.at[side, lo]
            near.append(go(remote(nout.at[side, lo], nbuf.at[side, lo], *sems, z_to[offset])))
    for i in range(len(AHEAD)):
        for way in (0, 1):
            if i < len(offsets[1 - way]):
                xout[1, way, i] = term(1 if way == 0 else 3, offsets[1 - way][i]).astype(BF16)
                sent[1, way, i] = x_copy(1, way, i, xout.at[1, way, i])
    y_far, y_next, y_prev = (y + 2) % NY, (y + 1) % NY, (y + NY - 1) % NY
    put_rows(y_far)
    y_a = go(remote(rows.at[y_far, 0], ybuf.at[0], ysend.at[0], yrecv.at[0], y_up))
    y_b = go(remote(rows.at[y_far, 1], ybuf.at[1], ysend.at[1], yrecv.at[1], y_dn))
    hear(z_word)
    tell(z_far_word, ((0, z_to[2]), (1, z_to[NZ - 2])))
    for i in range(len(AHEAD)):
        for way in (0, 1):
            if i < len(offsets[way]):
                sent[0, way, i].wait_recv()
                own = term(1 if way == 0 else 3, offsets[way][i])
                xsum[way, i] = (xbuf[0, way, i].astype(F32) + own).astype(BF16)
                sent[2, way, i] = x_copy(2, way, i, xsum.at[way, i])
    for copy in near:
        copy.wait_recv()
    hear(x_word)
    across = []
    for step in (2, 1, 3):
        oout[step - 1] = near_term(step).astype(BF16)
        sems = osend.at[step - 1], orecv.at[step - 1]
        across.append(go(remote(oout.at[step - 1], obuf.at[step - 1], *sems, x_to[step - 1])))
    put_rows(y_next)
    put_rows(y_prev)
    y_c = go(remote(rows.at[y_next, 1], ybuf.at[2], ysend.at[2], yrecv.at[2], y_up))
    y_d = go(remote(rows.at[y_prev, 0], ybuf.at[3], ysend.at[3], yrecv.at[3], y_dn))
    z_copies = []
    hear(z_far_word)
    for i in range(len(AHEAD)):
        for way in (0, 1):
            if i < len(offsets[way]):
                sent[2, way, i].wait_recv()
                sent[1, 1 - way, i].wait_recv()
                offset = offsets[way][i]
                slot = LATE.index(offset)
                block = term(0, offset) + xbuf[2, way, i].astype(F32) + xbuf[1, 1 - way, i].astype(F32)
                zsum[slot] = block.astype(BF16)
                sems = zsend.at[slot], zrecv.at[slot]
                z_copies.append(go(remote(zsum.at[slot], zbuf.at[slot], *sems, z_to[offset])))
    y_a.wait_recv()
    ysum[0] = (ybuf[0].astype(F32) + rows[y_next, 0].astype(F32)).astype(BF16)
    y_e = go(remote(ysum.at[0], ybuf.at[4], ysend.at[4], yrecv.at[4], y_up))
    y_b.wait_recv()
    ysum[1] = (ybuf[1].astype(F32) + rows[y_prev, 1].astype(F32)).astype(BF16)
    y_f = go(remote(ysum.at[1], ybuf.at[5], ysend.at[5], yrecv.at[5], y_dn))
    put_rows(y)
    total = near_term(0)
    for copy in across:
        copy.wait_recv()
    total = total + obuf[0].astype(F32) + obuf[1].astype(F32) + obuf[2].astype(F32)
    for copy in z_copies:
        copy.wait_recv()
    for slot in range(len(LATE)):
        total = total + zbuf[slot].astype(F32)
    last[0] = total.astype(BF16)
    final = go(remote(last.at[0], last.at[1], hsend, hrecv, x_to[1]))
    y_d.wait_recv()
    y_e.wait_recv()
    att[...] = (rows[y, 0].astype(F32) + ybuf[3].astype(F32) + ybuf[4].astype(F32)).astype(BF16)
    y_c.wait_recv()
    y_f.wait_recv()
    qgrad[...] = (rows[y, 1].astype(F32) + ybuf[2].astype(F32) + ybuf[5].astype(F32)).astype(BF16)
    final.wait_recv()
    mine, other = last[0], last[1]
    kgrad[...] = jnp.where(h == 0, mine, other)
    vgrad[...] = jnp.where(h == 0, other, mine)
    for copy in started:
        copy.wait_send()


def reduce(acc, share, grad, kv):
    vmem = pl.BlockSpec(memory_space=pltpu.VMEM)
    dma = pltpu.SemaphoreType.DMA
    block = (BLK, DH)
    late = len(LATE)
    word = pltpu.SemaphoreType.REGULAR((2,))
    return pl.pallas_call(
        reduce_kernel,
        out_shape=(
            jax.ShapeDtypeStruct((2 * ROWS, DH), BF16),
            jax.ShapeDtypeStruct((2 * ROWS, DH), BF16),
            jax.ShapeDtypeStruct(block, BF16),
            jax.ShapeDtypeStruct(block, BF16),
        ),
        in_specs=[vmem] * 4,
        out_specs=(vmem,) * 4,
        scratch_shapes=[
            pltpu.VMEM((NY, 2, 2 * ROWS, DH), BF16),
            pltpu.VMEM((6, 2 * ROWS, DH), BF16),
            pltpu.VMEM((2, 2 * ROWS, DH), BF16),
            pltpu.VMEM((2, XLO, 2) + block, BF16),
            pltpu.VMEM((2, XLO, 2) + block, BF16),
            pltpu.VMEM((3,) + block, BF16),
            pltpu.VMEM((3,) + block, BF16),
            pltpu.VMEM((2, 2, 3) + block, BF16),
            pltpu.VMEM((3, 2, 3) + block, BF16),
            pltpu.VMEM((2, 3) + block, BF16),
            pltpu.VMEM((late,) + block, BF16),
            pltpu.VMEM((late,) + block, BF16),
            pltpu.VMEM((2,) + block, BF16),
            dma((6,)), dma((6,)), dma((2, XLO)), dma((2, XLO)), dma((3,)), dma((3,)),
            dma((3, 2, 3)), dma((3, 2, 3)), dma((late,)), dma((late,)), dma, dma, word, word, word,
        ],
        compiler_params=pltpu.CompilerParams(collective_id=2, has_side_effects=True, vmem_limit_bytes=10 << 20),
        name="reduce_terms",
    )(acc, share, grad, kv)


def store_kernel(*refs):
    count = len(refs) // 2
    copies = [pltpu.make_async_copy(refs[i], refs[count + i], refs[-1].at[i]) for i in range(count)]
    for copy in copies:
        copy.start()
    for copy in copies:
        copy.wait()


def store(*arrays):
    return pl.pallas_call(
        store_kernel,
        out_shape=tuple(jax.ShapeDtypeStruct(a.shape, a.dtype) for a in arrays),
        in_specs=[pl.BlockSpec(memory_space=pltpu.VMEM)] * len(arrays),
        out_specs=(pl.BlockSpec(memory_space=pl.ANY),) * len(arrays),
        scratch_shapes=[pltpu.SemaphoreType.DMA((len(arrays),))],
        compiler_params=pltpu.CompilerParams(vmem_limit_bytes=1 << 20),
        name="store_outputs",
    )(*arrays)


def body(queries, key_rows, value_rows, out_grad, doc_lengths, balance):
    flat = (2 * ROWS, DH)
    bal = balance.reshape(SPANS // 2, BLK)
    qg, kg, tab, row_tab, zeros_acc, zeros_grad, zeros_kv = gather(
        queries.reshape(flat),
        out_grad.reshape(flat),
        key_rows.reshape(2, RUN, DH),
        value_rows.reshape(2, RUN, DH),
        bal,
        doc_lengths,
    )
    part, part_acc, more, more_gw = forward(tab, row_tab, qg, kg, zeros_acc)
    stats, acc, held, held_gw = exchange(tab, row_tab, qg, kg, part, part_acc)
    share, grad, kv = backward(
        tab, qg, kg, stats, held, held_gw, more, more_gw, zeros_grad, zeros_kv
    )
    kv = kv.reshape(2, XLO * NZ, BLK, DH)
    attended, query_grad, key_grad, value_grad = store(*reduce(acc, share, grad, kv))
    return attended.reshape(queries.shape), query_grad.reshape(queries.shape), key_grad, value_grad


def solution(mesh):
    return jax.shard_map(
        body,
        mesh=mesh,
        in_specs=(
            P(("seq", "ctx"), "head", None),
            P(("seq", "ctx"), None),
            P(("seq", "ctx"), None),
            P(("seq", "ctx"), "head", None),
            P("seq"),
            P("seq"),
        ),
        out_specs=(
            P(("seq", "ctx"), "head", None),
            P(("seq", "ctx"), "head", None),
            P(("seq", "ctx"), None),
            P(("seq", "ctx"), None),
        ),
        check_vma=False,
    )
```

```python
import functools
import math

import jax
import jax.numpy as jnp
from jax import lax
from jax.experimental import pallas as pl
from jax.experimental.pallas import tpu as pltpu
from jax.sharding import PartitionSpec as P

NX, NY, NZ = 4, 4, 8
XLO = 2
RUN = 64
DH = 128
HEADS_HERE = 4
ROWS = RUN * HEADS_HERE
BLK = 2 * RUN
KRUNS = XLO * NZ * 2
QRUNS = NY * 2
FIRST = 4
TILE = 3
SPANS = 128
MOST_TILES = 1 + (KRUNS - FIRST + TILE - 1) // TILE
ITEMS = QRUNS * (MOST_TILES - 1)
DOCS = 8
NEGATIVE = -1e30
FLOOR = -1e29
FAR = 1 << 20
SCALING = 1.0 / math.sqrt(DH)
LOG2E = 1.0 / math.log(2.0)
MESH = pl.DeviceIdType.MESH
F32 = jnp.float32
BF16 = jnp.bfloat16


def here():
    c = lax.axis_index("ctx")
    h = lax.axis_index("head")
    return h, c // (NY * NZ), (c // NZ) % NY, c % NZ


def device(x, y, z):
    return {"ctx": ((x % XLO) * NY + y) * NZ + z, "head": x // XLO}


def greet(targets):
    barrier = pltpu.get_barrier_semaphore()
    for target in targets:
        pl.semaphore_signal(barrier, inc=1, device_id=target, device_id_type=MESH)
    return lambda: pl.semaphore_wait(barrier, len(targets))


def remote(src, dst, send, recv, target):
    return pltpu.make_async_remote_copy(
        src_ref=src, dst_ref=dst, send_sem=send, recv_sem=recv, device_id=target, device_id_type=MESH
    )


def tables(bal, lengths, tab, row_tab, xl, y, z):
    lane = lax.broadcasted_iota(jnp.int32, (1, SPANS), 1)
    slabs = [bal[pl.ds(pl.multiple_of((i * NY + y) * NZ, NZ), NZ), :] for i in range(XLO)]
    held = [slab[:, half * RUN : half * RUN + 1] // RUN for half in (0, 1) for slab in slabs]
    held = jnp.concatenate(held, axis=0)
    index = lax.broadcasted_iota(jnp.int32, (KRUNS, 1), 0)
    match = held == lane
    has = jnp.sum(jnp.where(match, 1, 0), axis=0, keepdims=True)
    which = jnp.sum(jnp.where(match, index, 0), axis=0, keepdims=True)
    before = jnp.sum(jnp.where(held < lane, 1, 0), axis=0, keepdims=True)
    rank = jnp.where(has > 0, before, -1)
    hit = jnp.where(rank == lax.broadcasted_iota(jnp.int32, (SPANS, 1), 0), 1.0, 0.0).astype(BF16)
    row = lax.broadcasted_iota(jnp.int32, (8, 1), 0)
    block, half = which % (XLO * NZ), which // (XLO * NZ)
    found = jnp.where(row == 0, lane, jnp.where(row == 1, block, jnp.where(row == 6, half, 0)))
    found = found.astype(F32).astype(BF16)
    sorted_runs = lax.dot_general(found, hit, (((1,), (1,)), ((), ())), preferred_element_type=F32)
    sorted_runs = jnp.where((row == 0) & (lane >= KRUNS), F32(FAR // RUN), sorted_runs).astype(jnp.int32)
    q_rows = [bal[pl.ds((xl * NY + i) * NZ + z, 1), :] for i in range(NY)]
    low = jnp.concatenate([r[:, half * RUN : half * RUN + 1] for r in q_rows for half in (0, 1)], axis=0)
    pos = low + lax.broadcasted_iota(jnp.int32, (QRUNS, ROWS), 1) // HEADS_HERE
    start = jnp.zeros((QRUNS, ROWS), jnp.int32)
    first = jnp.zeros((QRUNS, 1), jnp.int32)
    end = 0
    for d in range(DOCS):
        end = end + lengths[d]
        first = jnp.where(low >= end, end, first)
        start = jnp.where(pos >= end, end, start)
    row_tab[0] = pos
    row_tab[1] = start
    low_run = jnp.sum(jnp.where((lane < first // RUN) & (has > 0), 1, 0), axis=1, keepdims=True)
    high_run = jnp.sum(jnp.where((lane <= low // RUN) & (has > 0), 1, 0), axis=1, keepdims=True)
    tiles = 1 + jnp.maximum(high_run - low_run - FIRST + TILE - 1, 0) // TILE
    own_lane = lax.broadcasted_iota(jnp.int32, (QRUNS, 1), 0) == lane
    low_row = jnp.sum(jnp.where(own_lane, low_run, 0), axis=0, keepdims=True)
    more = tiles - 1
    upper = lax.broadcasted_iota(jnp.int32, (QRUNS, 1), 0) >= lax.broadcasted_iota(jnp.int32, (1, SPANS), 1)
    more_row = jnp.sum(jnp.where(own_lane, more, 0), axis=0, keepdims=True)
    ends = jnp.sum(jnp.where(upper, more_row, 0), axis=1, keepdims=True)
    passed = lane >= ends
    run_row = jnp.minimum(jnp.sum(jnp.where(passed, 1, 0), axis=0, keepdims=True), QRUNS - 1)
    tile_row = lane + 1 - jnp.sum(jnp.where(passed, more, 0), axis=0, keepdims=True)
    count = jnp.sum(more, axis=0, keepdims=True)
    tile_row = jnp.where(lane >= count, MOST_TILES, tile_row)
    values = [None, None, low_row, run_row, tile_row, jnp.where(lane == 0, count, 0)]
    out = sorted_runs
    for i in range(2, 6):
        out = jnp.where(row == i, values[i], out)
    tab[...] = out


def gather_kernel(
    q_ref, g_ref, k_ref, v_ref, bal_ref, len_ref, qg, kg, tab, row_tab, zeros_acc, zeros_grad, zeros_kv, bal, lengths, lsem, ysend, yrecv, zsend, zrecv, xsend, xrecv
):
    h, xl, y, z = here()
    x = h * XLO + xl
    first = xl * NZ
    y_up, y_dn = device(x, (y + 1) % NY, z), device(x, (y + NY - 1) % NY, z)
    z_to = {d: device(x, y, (z + d + NZ) % NZ) for d in (1, 2, -1, -2)}
    x_up, x_dn = device((x + 1) % NX, y, z), device((x + NX - 1) % NX, y, z)
    meet = greet([z_to[2], z_to[-2], z_to[1], z_to[-1], y_up, y_dn, x_up, x_dn])
    started = []

    def go(copy):
        copy.start()
        started.append(copy)
        return copy

    sent_z = {}

    def part(j):
        return (h + j) % 2

    def behind(sign, dist):
        return (z - sign * dist + NZ) % NZ

    def z_send(sign, hops, dist, j):
        ref = kg.at[first + behind(sign, dist - hops), part(j)]
        way = 0 if sign > 0 else 1
        sems = zsend.at[way, dist - 1, j], zrecv.at[way, dist - 1, j]
        sent_z[sign, dist, j] = go(remote(ref, ref, *sems, z_to[sign * hops]))

    sent_x = []

    def x_send(slot, block):
        dst = kg.at[first + block, h]
        for side, target in ((0, x_up), (1, x_dn)):
            sent_x.append(go(remote(dst, dst, xsend.at[side, slot], xrecv.at[side, slot], target)))

    def local(src, dst, slot):
        copy = pltpu.make_async_copy(src, dst, lsem.at[slot])
        copy.start()
        return copy

    own_kv = [local(ref, kg.at[first + z, i], i) for i, ref in enumerate((k_ref, v_ref))]
    own_tab = [local(bal_ref, bal, 4), local(len_ref, lengths, 5)]
    for copy in own_kv:
        copy.wait()
    meet()
    for j in (0, 1):
        for sign in (1, -1):
            z_send(sign, 2, 2, j)
    y_q_up = go(remote(q_ref, qg.at[y, 0], ysend.at[0], yrecv.at[0], y_up))
    y_g_dn = go(remote(g_ref, qg.at[y, 1], ysend.at[2], yrecv.at[2], y_dn))
    x_send(0, z)
    for sign in (1, -1):
        z_send(sign, 1, 1, 0)
    y_g_up = go(remote(g_ref, qg.at[y, 1], ysend.at[1], yrecv.at[1], y_up))
    y_q_dn = go(remote(q_ref, qg.at[y, 0], ysend.at[3], yrecv.at[3], y_dn))
    own_q = [local(ref, qg.at[y, i], 2 + i) for i, ref in enumerate((q_ref, g_ref))]
    for copy in own_tab:
        copy.wait()
    tables(bal, lengths, tab, row_tab, xl, y, z)
    for j in (0, 1):
        for sign in (1, -1):
            sent_z[sign, 2, j].wait_recv()
            if j == (0 if sign > 0 else 1):
                z_send(sign, 2, 4, j)
            z_send(sign, 1, 3, j)
            if j == 0:
                x_send(1 if sign > 0 else 2, behind(sign, 2))
    for sign in (1, -1):
        z_send(sign, 1, 1, 1)
    y_q_up.wait_recv()
    q_on = qg.at[(y + NY - 1) % NY, 0]
    y_fwd_up = go(remote(q_on, q_on, ysend.at[4], yrecv.at[4], y_up))
    y_g_dn.wait_recv()
    g_on = qg.at[(y + 1) % NY, 1]
    y_fwd_dn = go(remote(g_on, g_on, ysend.at[5], yrecv.at[5], y_dn))
    for slot, (sign, dist) in enumerate(((1, 1), (-1, 1), (1, 4), (1, 3), (-1, 3))):
        sent_z[sign, dist, 0].wait_recv()
        x_send(3 + slot, behind(sign, dist))
    for ref in (zeros_acc, zeros_grad, zeros_kv):
        ref[...] = jnp.zeros_like(ref)
    for sign, dist in ((1, 1), (-1, 1), (1, 3), (-1, 3), (-1, 4)):
        sent_z[sign, dist, 1].wait_recv()
    for copy in (y_g_up, y_q_dn, y_fwd_up, y_fwd_dn):
        copy.wait_recv()
    for copy in sent_x:
        copy.wait_recv()
    for copy in started:
        copy.wait_send()
    for copy in own_q:
        copy.wait()


ZEROS = (
    jax.ShapeDtypeStruct((QRUNS, DH, ROWS), F32),
    jax.ShapeDtypeStruct((QRUNS, DH, ROWS), F32),
    jax.ShapeDtypeStruct((2, XLO * NZ, 2, RUN, DH), F32),
)


def gather(q, g, k, v, bal, lengths):
    hbm = pl.BlockSpec(memory_space=pltpu.HBM)
    vmem = pl.BlockSpec(memory_space=pltpu.VMEM)
    dma = pltpu.SemaphoreType.DMA
    return pl.pallas_call(
        gather_kernel,
        out_shape=(
            jax.ShapeDtypeStruct((NY, 2, 2 * ROWS, DH), BF16),
            jax.ShapeDtypeStruct((XLO * NZ, 2, 2, RUN, DH), BF16),
            jax.ShapeDtypeStruct((8, SPANS), jnp.int32),
            jax.ShapeDtypeStruct((2, QRUNS, ROWS), jnp.int32),
            *ZEROS,
        ),
        in_specs=[hbm] * 6,
        out_specs=(vmem,) * 7,
        scratch_shapes=[
            pltpu.VMEM((SPANS // 2, BLK), jnp.int32),
            pltpu.SMEM((DOCS,), jnp.int32),
            dma((6,)), dma((6,)), dma((6,)), dma((2, 4, 2)), dma((2, 4, 2)), dma((2, 8)), dma((2, 8)),
        ],
        compiler_params=pltpu.CompilerParams(collective_id=0, has_side_effects=True, vmem_limit_bytes=8 << 20),
        name="gather_rows",
    )(*(pltpu.with_memory_space_constraint(a, pltpu.HBM) for a in (q, g, k, v, bal, lengths)))


def tile_runs(tab, low_run, t):
    if t is None:
        runs = [low_run + u for u in range(FIRST)]
    else:
        runs = [low_run + FIRST + (t - 1) * TILE + u for u in range(TILE)]
    return [(tab[1, r], tab[6, r]) for r in runs], [tab[0, r] * RUN for r in runs]


def tile_rows(kg, indices, part):
    return jnp.concatenate([kg[block, part, half] for block, half in indices], axis=0)


def masked_scores(k, q, places, pos, start):
    scores = lax.dot_general(k, q, (((1,), (1,)), ((), ())), preferred_element_type=F32)
    offset = lax.broadcasted_iota(jnp.int32, (RUN, ROWS), 0)
    parts = []
    for u, base in enumerate(places):
        seen = (offset <= pos - base) & (offset >= start - base)
        parts.append(jnp.where(seen, scores[u * RUN : (u + 1) * RUN] * (SCALING * LOG2E), NEGATIVE))
    return jnp.concatenate(parts, axis=0)


def together(process, items):
    for end in [process(*item) for item in items]:
        end()


def first_tiles(process):
    together(process, [(q_run, None, q_run) for q_run in range(QRUNS)])


def further_tiles(tab, process):
    def steps(unroll, first, count):
        def step(i, _):
            slots = [first + unroll * i + u for u in range(unroll)]
            together(process, [(tab[3, slot], tab[4, slot], slot) for slot in slots])
            return 0

        lax.fori_loop(0, count, step, 0)

    fours = tab[5, 0] // 4
    steps(4, 0, fours)
    steps(2, 4 * fours, (tab[5, 0] - 4 * fours + 1) // 2)


def query_rows(qg, q_run, part):
    return qg[q_run // 2, part, pl.ds(pl.multiple_of((q_run % 2) * ROWS, ROWS), ROWS), :]


def forward_tile(tab, row_tab, qg, kg, held, held_gw, combine):
    def process(q_run, t, slot):
        at = pl.ds(q_run, 1)
        indices, places = tile_runs(tab, tab[2, q_run], t)
        s = masked_scores(
            tile_rows(kg, indices, 0), query_rows(qg, q_run, 0), places, row_tab[0, at, :], row_tab[1, at, :]
        )
        held[slot] = s
        v = tile_rows(kg, indices, 1)
        gw = lax.dot_general(
            v, query_rows(qg, q_run, 1), (((1,), (1,)), ((), ())), preferred_element_type=F32
        )
        held_gw[slot] = gw
        top = jnp.maximum(jnp.max(s, axis=0, keepdims=True), FLOOR)
        raw = jnp.exp2(s - top)
        total = jnp.sum(raw, axis=0, keepdims=True)
        inner = jnp.sum(raw * gw, axis=0, keepdims=True)
        acc = lax.dot_general(v, raw.astype(BF16), (((0,), (0,)), ((), ())), preferred_element_type=F32)
        return lambda: combine(q_run, top, total, inner, acc)

    return process


def combined(old, old_acc, top, total, inner, acc):
    new_top = jnp.maximum(old[0], top)
    old_share, share = jnp.exp2(old[0] - new_top), jnp.exp2(top - new_top)
    stats = new_top, old[1] * old_share + total * share, old[2] * old_share + inner * share
    return stats, old_acc * old_share + acc * share


def forward_kernel(tab, row_tab, qg, kg, zeros, stats, out, held, held_gw):
    stats[0] = jnp.full((QRUNS, ROWS), FLOOR, F32)
    stats[1] = jnp.zeros((QRUNS, ROWS), F32)
    stats[2] = jnp.zeros((QRUNS, ROWS), F32)

    def combine(q_run, *new):
        at = pl.ds(q_run, 1)
        rows, out[q_run] = combined([stats[i, at, :] for i in range(3)], out[q_run], *new)
        for i in range(3):
            stats[i, at, :] = rows[i]

    further_tiles(tab, forward_tile(tab, row_tab, qg, kg, held, held_gw, combine))


def forward(tab, row_tab, qg, kg, zeros):
    smem = pl.BlockSpec(memory_space=pltpu.SMEM)
    vmem = pl.BlockSpec(memory_space=pltpu.VMEM)
    return pl.pallas_call(
        forward_kernel,
        out_shape=(
            jax.ShapeDtypeStruct((3, QRUNS, ROWS), F32),
            jax.ShapeDtypeStruct((QRUNS, DH, ROWS), F32),
            jax.ShapeDtypeStruct((ITEMS, TILE * RUN, ROWS), F32),
            jax.ShapeDtypeStruct((ITEMS, TILE * RUN, ROWS), F32),
        ),
        in_specs=[smem] + [vmem] * 4,
        out_specs=(vmem,) * 4,
        input_output_aliases={4: 1},
        compiler_params=pltpu.CompilerParams(vmem_limit_bytes=8 << 20),
        name="forward_stats",
    )(tab, row_tab, qg, kg, zeros)


def exchange_kernel(
    tab_ref, row_tab, qg, kg, part, part_acc, out, acc_out, held, held_gw, tab, mine, lsem, send, recv
):
    h, xl, y, z = here()
    x = h * XLO + xl
    targets = [device(x, (y + d) % NY, z) for d in (2, 1, 3)]
    meet = greet(targets)
    table = pltpu.make_async_copy(tab_ref, tab, lsem)
    table.start()
    table.wait()

    def combine(q_run, *new):
        at = pl.ds(q_run, 1)
        rows, acc_out[q_run] = combined([part[i, at, :] for i in range(3)], part_acc[q_run], *new)
        for i in range(3):
            mine[i, at, :] = rows[i]

    first_tiles(forward_tile(tab, row_tab, qg, kg, held, held_gw, combine))
    meet()
    copies = []
    for d, target in enumerate(targets):
        copy = remote(mine, out.at[y], send.at[d], recv.at[d], target)
        copy.start()
        copies.append(copy)
    own = pltpu.make_async_copy(mine, out.at[y], lsem)
    own.start()
    own.wait()
    for copy in copies:
        copy.wait()


def exchange(tab, row_tab, qg, kg, part, part_acc):
    vmem = pl.BlockSpec(memory_space=pltpu.VMEM)
    dma = pltpu.SemaphoreType.DMA
    return pl.pallas_call(
        exchange_kernel,
        out_shape=(
            jax.ShapeDtypeStruct((NY,) + part.shape, F32),
            jax.ShapeDtypeStruct(part_acc.shape, F32),
            jax.ShapeDtypeStruct((QRUNS, FIRST * RUN, ROWS), F32),
            jax.ShapeDtypeStruct((QRUNS, FIRST * RUN, ROWS), F32),
        ),
        in_specs=[vmem] * 6,
        out_specs=(vmem,) * 4,
        scratch_shapes=[pltpu.SMEM(tab.shape, jnp.int32), pltpu.VMEM(part.shape, F32), dma, dma((NY - 1,)), dma((NY - 1,))],
        compiler_params=pltpu.CompilerParams(collective_id=1, has_side_effects=True, vmem_limit_bytes=8 << 20),
        name="exchange_stats",
    )(tab, row_tab, qg, kg, part, part_acc)


def backward_kernel(
    tab, qg, kg, stats, held, held_gw, more, more_gw, zeros_grad, zeros_kv, share_out, grad_acc, kv_acc, row_stats
):
    y = here()[2]
    top = jnp.maximum(jnp.maximum(stats[0, 0], stats[1, 0]), jnp.maximum(stats[2, 0], stats[3, 0]))
    shares = [jnp.exp2(stats[i, 0] - top) for i in range(NY)]
    total = sum(stats[i, 1] * shares[i] for i in range(NY))
    log_total = top + jnp.log(total) * LOG2E
    row_stats[0] = log_total
    row_stats[1] = sum(stats[i, 2] * shares[i] for i in range(NY)) / total
    share_out[...] = jnp.exp2(stats[y, 0] - log_total)

    def process(held, held_gw, q_run, t, slot):
        at = pl.ds(q_run, 1)
        indices, _ = tile_runs(tab, tab[2, q_run], t)
        weights = jnp.exp2(held[slot] - row_stats[0, at, :])
        gs = (weights * (held_gw[slot] - row_stats[1, at, :])).astype(BF16)
        value_part = jnp.dot(weights.astype(BF16), query_rows(qg, q_run, 1), preferred_element_type=F32)
        key_part = jnp.dot(gs, query_rows(qg, q_run, 0), preferred_element_type=F32)
        grad = lax.dot_general(
            tile_rows(kg, indices, 0), gs, (((0,), (0,)), ((), ())), preferred_element_type=F32
        )

        def end():
            for u, (block, half) in enumerate(indices):
                kv_acc[1, block, half] += value_part[u * RUN : (u + 1) * RUN]
                kv_acc[0, block, half] += key_part[u * RUN : (u + 1) * RUN]
            grad_acc[q_run] += grad

        return end

    first_tiles(functools.partial(process, held, held_gw))
    further_tiles(tab, functools.partial(process, more, more_gw))


def backward(tab, qg, kg, stats, held, held_gw, more, more_gw, zeros_grad, zeros_kv):
    smem = pl.BlockSpec(memory_space=pltpu.SMEM)
    vmem = pl.BlockSpec(memory_space=pltpu.VMEM)
    return pl.pallas_call(
        backward_kernel,
        out_shape=(
            jax.ShapeDtypeStruct((QRUNS, ROWS), F32),
            jax.ShapeDtypeStruct((QRUNS, DH, ROWS), F32),
            jax.ShapeDtypeStruct((2, XLO * NZ, 2, RUN, DH), F32),
        ),
        in_specs=[smem] + [vmem] * 9,
        out_specs=(vmem,) * 3,
        input_output_aliases={8: 1, 9: 2},
        scratch_shapes=[pltpu.VMEM((2, QRUNS, ROWS), F32)],
        compiler_params=pltpu.CompilerParams(vmem_limit_bytes=8 << 20),
        name="backward_terms",
    )(tab, qg, kg, stats, held, held_gw, more, more_gw, zeros_grad, zeros_kv)


AHEAD = (4, 3, 2)
BEHIND = (5, 6)
LATE = AHEAD + BEHIND


def reduce_kernel(
    acc, share, grad, kv, att, qgrad, kgrad, vgrad,
    rows, ybuf, ysum, nout, nbuf, oout, obuf, xout, xbuf, xsum, zsum, zbuf, last,
    ysend, yrecv, nsend, nrecv, osend, orecv, xsend, xrecv, zsend, zrecv, hsend, hrecv, z_word, x_word, z_far_word,
):
    h, xl, y, z = here()
    x = h * XLO + xl
    y_up, y_dn = device(x, (y + 1) % NY, z), device(x, (y + NY - 1) % NY, z)
    x_to = tuple(device((x + d) % NX, y, z) for d in (1, 2, 3))
    z_to = {d: device(x, y, (z + d) % NZ) for d in range(1, NZ)}
    z_near = ((0, z_to[1]), (1, z_to[NZ - 1]))
    x_near = ((0, x_to[0]), (1, x_to[2]))
    meet = greet([z_to[1], z_to[NZ - 1], x_to[0], x_to[2], y_up, y_dn])

    def tell(sem, targets):
        for side, target in targets:
            pl.semaphore_signal(sem.at[side], inc=1, device_id=target, device_id_type=MESH)

    def hear(sem):
        for side in (0, 1):
            pl.semaphore_wait(sem.at[side], 1)

    started = []

    def go(copy):
        copy.start()
        started.append(copy)
        return copy

    def scaled(part, block):
        return kv[part, block] * jnp.where(part == 0, F32(SCALING), F32(1.0))

    def term(step, offset):
        ring = (x + step) % NX
        return scaled(ring // XLO, (ring % XLO) * NZ + (z + offset) % NZ)

    def near_term(step):
        ring = (x + step) % NX
        sides = [nbuf[side, ring % XLO, ring // XLO].astype(F32) for side in (0, 1)]
        return term(step, 0) + sides[0] + sides[1]

    def put_rows(yy):
        for half in (0, 1):
            q_run = yy * 2 + half
            to = pl.ds(half * ROWS, ROWS)
            rows[yy, 0, to, :] = (acc[q_run] * share[pl.ds(q_run, 1), :]).T.astype(BF16)
            rows[yy, 1, to, :] = (grad[q_run] * SCALING).T.astype(BF16)

    def x_copy(kind, way, i, src):
        target = x_to[0] if way == 0 else x_to[2]
        return go(remote(src, xbuf.at[kind, way, i], xsend.at[kind, way, i], xrecv.at[kind, way, i], target))

    offsets = (AHEAD, BEHIND)
    sent = {}
    for side, offset in ((0, 1), (1, NZ - 1)):
        for lo in range(XLO):
            for part in (0, 1):
                nout[side, lo, part] = scaled(part, lo * NZ + (z + offset) % NZ).astype(BF16)
    for way in (0, 1):
        for i, offset in enumerate(offsets[way]):
            xout[0, way, i] = term(2, offset).astype(BF16)
    meet()
    tell(z_word, z_near)
    tell(x_word, x_near)
    for i in range(len(AHEAD)):
        for way in (0, 1):
            if i < len(offsets[way]):
                sent[0, way, i] = x_copy(0, way, i, xout.at[0, way, i])
    near = []
    for lo in range(XLO):
        for side, offset in ((0, 1), (1, NZ - 1)):
            sems = nsend.at[side, lo], nrecv.at[side, lo]
            near.append(go(remote(nout.at[side, lo], nbuf.at[side, lo], *sems, z_to[offset])))
    for i in range(len(AHEAD)):
        for way in (0, 1):
            if i < len(offsets[1 - way]):
                xout[1, way, i] = term(1 if way == 0 else 3, offsets[1 - way][i]).astype(BF16)
                sent[1, way, i] = x_copy(1, way, i, xout.at[1, way, i])
    y_far, y_next, y_prev = (y + 2) % NY, (y + 1) % NY, (y + NY - 1) % NY
    put_rows(y_far)
    y_a = go(remote(rows.at[y_far, 0], ybuf.at[0], ysend.at[0], yrecv.at[0], y_up))
    y_b = go(remote(rows.at[y_far, 1], ybuf.at[1], ysend.at[1], yrecv.at[1], y_dn))
    hear(z_word)
    tell(z_far_word, ((0, z_to[2]), (1, z_to[NZ - 2])))
    for i in range(len(AHEAD)):
        for way in (0, 1):
            if i < len(offsets[way]):
                sent[0, way, i].wait_recv()
                own = term(1 if way == 0 else 3, offsets[way][i])
                xsum[way, i] = (xbuf[0, way, i].astype(F32) + own).astype(BF16)
                sent[2, way, i] = x_copy(2, way, i, xsum.at[way, i])
    for copy in near:
        copy.wait_recv()
    hear(x_word)
    across = []
    for step in (2, 1, 3):
        oout[step - 1] = near_term(step).astype(BF16)
        sems = osend.at[step - 1], orecv.at[step - 1]
        across.append(go(remote(oout.at[step - 1], obuf.at[step - 1], *sems, x_to[step - 1])))
    put_rows(y_next)
    put_rows(y_prev)
    y_c = go(remote(rows.at[y_next, 1], ybuf.at[2], ysend.at[2], yrecv.at[2], y_up))
    y_d = go(remote(rows.at[y_prev, 0], ybuf.at[3], ysend.at[3], yrecv.at[3], y_dn))
    z_copies = []
    hear(z_far_word)
    for i in range(len(AHEAD)):
        for way in (0, 1):
            if i < len(offsets[way]):
                sent[2, way, i].wait_recv()
                sent[1, 1 - way, i].wait_recv()
                offset = offsets[way][i]
                slot = LATE.index(offset)
                block = term(0, offset) + xbuf[2, way, i].astype(F32) + xbuf[1, 1 - way, i].astype(F32)
                zsum[slot] = block.astype(BF16)
                sems = zsend.at[slot], zrecv.at[slot]
                z_copies.append(go(remote(zsum.at[slot], zbuf.at[slot], *sems, z_to[offset])))
    y_a.wait_recv()
    ysum[0] = (ybuf[0].astype(F32) + rows[y_next, 0].astype(F32)).astype(BF16)
    y_e = go(remote(ysum.at[0], ybuf.at[4], ysend.at[4], yrecv.at[4], y_up))
    y_b.wait_recv()
    ysum[1] = (ybuf[1].astype(F32) + rows[y_prev, 1].astype(F32)).astype(BF16)
    y_f = go(remote(ysum.at[1], ybuf.at[5], ysend.at[5], yrecv.at[5], y_dn))
    put_rows(y)
    total = near_term(0)
    for copy in across:
        copy.wait_recv()
    total = total + obuf[0].astype(F32) + obuf[1].astype(F32) + obuf[2].astype(F32)
    for copy in z_copies:
        copy.wait_recv()
    for slot in range(len(LATE)):
        total = total + zbuf[slot].astype(F32)
    last[0] = total.astype(BF16)
    final = go(remote(last.at[0], last.at[1], hsend, hrecv, x_to[1]))
    y_d.wait_recv()
    y_e.wait_recv()
    att[...] = (rows[y, 0].astype(F32) + ybuf[3].astype(F32) + ybuf[4].astype(F32)).astype(BF16)
    y_c.wait_recv()
    y_f.wait_recv()
    qgrad[...] = (rows[y, 1].astype(F32) + ybuf[2].astype(F32) + ybuf[5].astype(F32)).astype(BF16)
    final.wait_recv()
    mine, other = last[0], last[1]
    kgrad[...] = jnp.where(h == 0, mine, other)
    vgrad[...] = jnp.where(h == 0, other, mine)
    for copy in started:
        copy.wait_send()


def reduce(acc, share, grad, kv):
    vmem = pl.BlockSpec(memory_space=pltpu.VMEM)
    dma = pltpu.SemaphoreType.DMA
    block = (BLK, DH)
    late = len(LATE)
    word = pltpu.SemaphoreType.REGULAR((2,))
    return pl.pallas_call(
        reduce_kernel,
        out_shape=(
            jax.ShapeDtypeStruct((2 * ROWS, DH), BF16),
            jax.ShapeDtypeStruct((2 * ROWS, DH), BF16),
            jax.ShapeDtypeStruct(block, BF16),
            jax.ShapeDtypeStruct(block, BF16),
        ),
        in_specs=[vmem] * 4,
        out_specs=(vmem,) * 4,
        scratch_shapes=[
            pltpu.VMEM((NY, 2, 2 * ROWS, DH), BF16),
            pltpu.VMEM((6, 2 * ROWS, DH), BF16),
            pltpu.VMEM((2, 2 * ROWS, DH), BF16),
            pltpu.VMEM((2, XLO, 2) + block, BF16),
            pltpu.VMEM((2, XLO, 2) + block, BF16),
            pltpu.VMEM((3,) + block, BF16),
            pltpu.VMEM((3,) + block, BF16),
            pltpu.VMEM((2, 2, 3) + block, BF16),
            pltpu.VMEM((3, 2, 3) + block, BF16),
            pltpu.VMEM((2, 3) + block, BF16),
            pltpu.VMEM((late,) + block, BF16),
            pltpu.VMEM((late,) + block, BF16),
            pltpu.VMEM((2,) + block, BF16),
            dma((6,)), dma((6,)), dma((2, XLO)), dma((2, XLO)), dma((3,)), dma((3,)),
            dma((3, 2, 3)), dma((3, 2, 3)), dma((late,)), dma((late,)), dma, dma, word, word, word,
        ],
        compiler_params=pltpu.CompilerParams(collective_id=2, has_side_effects=True, vmem_limit_bytes=10 << 20),
        name="reduce_terms",
    )(acc, share, grad, kv)


def store_kernel(*refs):
    count = len(refs) // 2
    copies = [pltpu.make_async_copy(refs[i], refs[count + i], refs[-1].at[i]) for i in range(count)]
    for copy in copies:
        copy.start()
    for copy in copies:
        copy.wait()


def store(*arrays):
    return pl.pallas_call(
        store_kernel,
        out_shape=tuple(jax.ShapeDtypeStruct(a.shape, a.dtype) for a in arrays),
        in_specs=[pl.BlockSpec(memory_space=pltpu.VMEM)] * len(arrays),
        out_specs=(pl.BlockSpec(memory_space=pl.ANY),) * len(arrays),
        scratch_shapes=[pltpu.SemaphoreType.DMA((len(arrays),))],
        compiler_params=pltpu.CompilerParams(vmem_limit_bytes=1 << 20),
        name="store_outputs",
    )(*arrays)


def body(queries, key_rows, value_rows, out_grad, doc_lengths, balance):
    flat = (2 * ROWS, DH)
    bal = balance.reshape(SPANS // 2, BLK)
    qg, kg, tab, row_tab, zeros_acc, zeros_grad, zeros_kv = gather(
        queries.reshape(flat),
        out_grad.reshape(flat),
        key_rows.reshape(2, RUN, DH),
        value_rows.reshape(2, RUN, DH),
        bal,
        doc_lengths,
    )
    part, part_acc, more, more_gw = forward(tab, row_tab, qg, kg, zeros_acc)
    stats, acc, held, held_gw = exchange(tab, row_tab, qg, kg, part, part_acc)
    share, grad, kv = backward(
        tab, qg, kg, stats, held, held_gw, more, more_gw, zeros_grad, zeros_kv
    )
    kv = kv.reshape(2, XLO * NZ, BLK, DH)
    attended, query_grad, key_grad, value_grad = store(*reduce(acc, share, grad, kv))
    return attended.reshape(queries.shape), query_grad.reshape(queries.shape), key_grad, value_grad


def solution(mesh):
    return jax.shard_map(
        body,
        mesh=mesh,
        in_specs=(
            P(("seq", "ctx"), "head", None),
            P(("seq", "ctx"), None),
            P(("seq", "ctx"), None),
            P(("seq", "ctx"), "head", None),
            P("seq"),
            P("seq"),
        ),
        out_specs=(
            P(("seq", "ctx"), "head", None),
            P(("seq", "ctx"), "head", None),
            P(("seq", "ctx"), None),
            P(("seq", "ctx"), None),
        ),
        check_vma=False,
    )
```
